128 devices in a mesh: dp: 4 (over x), seq: 32 (over z, y, core).
Axes of the slice: x: 4, y: 4, z: 4, core: 2. Of those that a mesh axis runs over, the one named last changes fastest.
Arguments:
- conv_input: bfloat16 [16384, 5376], P(('dp', 'seq')), may hold values from -6 to 6
- doc_start: int32 [16384], P(('dp', 'seq')), may hold values 0 or 1
- conv_weight: float32 [4, 5376], replicated, may hold values from -3 to 3
- conv_bias: float32 [5376], replicated, may hold values from -0.5 to 0.5
- dt_raw: float32 [16384, 80], P(('dp', 'seq')), may hold values from -3 to 3
- dt_bias: float32 [80], replicated, may hold values from -5.5 to -4.2
- a_log: float32 [80], replicated, may hold values from -9 to 2, as said below
- skip_gain: float32 [80], replicated, may hold values from 0.5 to 1.5
- cotangent: bfloat16 [16384, 5120], P(('dp', 'seq')), may hold values from -6 to 6
Outputs:
- ssm_output: bfloat16 [16384, 5120], P(('dp', 'seq'))
- grad_input: bfloat16 [16384, 5376], P(('dp', 'seq'))
- grad_conv_weight: float32 [4, 5376], replicated
- grad_conv_bias: float32 [5376], replicated
- grad_dt_bias: float32 [80], replicated
- grad_a_log: float32 [80], replicated
- grad_skip_gain: float32 [80], replicated
The draws below stay inside these ranges and needn't reach their ends.
Inputs may be any that keep to these rules, and one draw needn't show every extreme that they name: `doc_start`: 1 marks the first token of a document; documents may cross shard boundaries. One value per head; exp(a_log) lies between 25 / 4096 and 4.2, so that the per-token decay rates exp(a_log) * steps_dt run from under 1 / 4096 to about 1.1.
All inputs are finite; a program needn't handle non-finite values.
Results may differ from the reference program's by a relative error of at most 0.00115.
Values may be sent and summed in bfloat16 or wider, within the bound.
A program may use at most 320 MiB of HBM per device.

```python
import math
import jax
import jax.numpy as jnp
from jax import lax

HEADS = 80
HEAD_DIM = 64
STATE = 128
CONV = 4
BLOCK = 64
LOCAL = 128
INNER = 5120
CH = 5376
CHAIN = 4096
TOKENS = 16384
N_DP = 4


def draw_a_log(key, part):
    key_pick, key_slow, key_fast = jax.random.split(key, 3)
    slow_share = 0.5
    picked = jax.random.uniform(key_pick, (HEADS,), jnp.float32) < slow_share
    slow_rate = jax.random.uniform(key_slow, (HEADS,), jnp.float32, math.log(0.2 / CHAIN), math.log(2.0 / CHAIN))
    fast_rate = jax.random.uniform(key_fast, (HEADS,), jnp.float32, math.log(2.0 / CHAIN), math.log(1.0 / 30.0))
    return jnp.where(picked, slow_rate, fast_rate) - math.log(0.008)


def with_ends(array, key, least, high):
    index_at = [jax.random.randint(jax.random.fold_in(key, axis), (), 0, length) for axis, length in enumerate(array.shape)]
    longest = array.shape.index(max(array.shape))
    neighbour = index_at[:longest] + [(index_at[longest] + 1) % array.shape[longest]] + index_at[longest + 1:]
    return array.at[tuple(index_at)].set(least).at[tuple(neighbour)].set(high)


def steps_of(own_key, shape, shards, smallest, high):
    gain, own = 1.0, jax.random.fold_in(own_key, 6)
    for dim, shards_of in shards:
        draws = jnp.exp(jax.random.uniform(jax.random.fold_in(own, dim), (shards_of,), jnp.float32, smallest / len(shards), high / len(shards)))
        gain = gain * jnp.repeat(draws, shape[dim] // shards_of).reshape([-1 if axis == dim else 1 for axis in range(len(shape))])
    return gain


def gaussian(own_key, dims, scale, bound, cuts=(), held_as=jnp.bfloat16):
    factor_of = steps_of(own_key, dims, cuts, -0.22, 0.18) if cuts else 1.0
    entries = jax.random.normal(own_key, dims, jnp.float32) * scale * factor_of
    return jnp.minimum(jnp.maximum(entries, -bound), bound).astype(held_as)


def setup_inputs(seed: int = 0) -> dict:
    keys = jax.random.split(jax.random.key(seed), 10)
    return {
        "conv_input": gaussian(keys[0], (TOKENS, CH), 1.0, 6.0, ((0, 128),)),
        "doc_start": with_ends((jax.random.randint(keys[1], (TOKENS,), 0, 4 * LOCAL) < 1).astype(jnp.int32), jax.random.fold_in(keys[1], 1), 0, 1),
        "conv_weight": gaussian(keys[2], (CONV, CH), CONV ** -0.5, 3.0, (), jnp.float32),
        "conv_bias": jnp.clip(jax.random.uniform(keys[3], (CH,), jnp.float32, -0.5, 0.5), -0.5, 0.5),
        "dt_raw": gaussian(keys[4], (TOKENS, HEADS), 0.5, 3.0, ((0, 128),), jnp.float32),
        "dt_bias": jnp.clip(jax.random.uniform(keys[5], (HEADS,), jnp.float32, -5.5, -4.2), -5.5, -4.2),
        "a_log": draw_a_log(jax.random.fold_in(keys[9], 71), 0),
        "skip_gain": jnp.clip(jax.random.uniform(keys[7], (HEADS,), jnp.float32, 0.5, 1.5), 0.5, 1.5),
        "cotangent": gaussian(keys[8], (TOKENS, INNER), 1.0, 6.0, ((0, 128),)),
    }


exact_mode = lax.Precision.HIGHEST

def prepare_inputs(tail_rows, conv_input, doc_start, conv_weight, conv_bias, dt_raw, dt_bias, a_log):
    row_count = conv_input.shape[0]
    extended = jnp.concatenate([tail_rows, conv_input], axis=0)
    resets = doc_start.astype(jnp.float32)
    segment = jnp.cumsum(resets)
    padded = jnp.concatenate([jnp.zeros((CONV - 1,), jnp.float32), segment])
    convolved = conv_bias[None, :] + conv_weight[CONV - 1][None, :] * extended[CONV - 1:]
    for offset in range(1, CONV):
        first_row = CONV - 1 - offset
        tap_valid = (padded[first_row:first_row + row_count] == segment).astype(jnp.float32)
        convolved = convolved + conv_weight[first_row][None, :] * extended[first_row:first_row + row_count] * tap_valid[:, None]
    activated = jax.nn.silu(convolved)
    values_x = activated[:, :INNER].reshape(row_count, HEADS, HEAD_DIM)
    keys_b = activated[:, INNER:INNER + STATE]
    reads_c = activated[:, INNER + STATE:]
    steps_dt = jax.nn.softplus(dt_raw + dt_bias[None, :])
    log_decay = -jnp.exp(a_log)[None, :] * steps_dt
    return (values_x, keys_b, reads_c, steps_dt, log_decay)

def scan_block(carry, block_data):
    carry_state, skip_gain = carry
    values_x, keys_b, reads_c, steps_dt, log_decay, resets = block_data
    length = values_x.shape[0]
    segment = jnp.cumsum(resets)
    running = jnp.cumsum(log_decay, axis=0)
    positions = jnp.arange(length)
    causal = (positions[:, None] >= positions[None, :]) & (segment[:, None] == segment[None, :])
    spread_log = running.T[:, :, None] - running.T[:, None, :]
    within = jnp.where(causal[None], jnp.exp(jnp.where(causal[None], spread_log, 0.0)), 0.0)
    scores = jnp.dot(reads_c, keys_b.T, precision=exact_mode)
    weights = within * scores[None] * steps_dt.T[:, None, :]
    output = jnp.einsum('hts,shp->thp', weights, values_x, precision=exact_mode)
    untouched = (segment == 0).astype(running.dtype)
    entry_weight = jnp.exp(running) * untouched[:, None]
    output = output + jnp.einsum('tn,hpn->thp', reads_c, carry_state, precision=exact_mode) * entry_weight[:, :, None]
    output = output + skip_gain[None, :, None] * values_x
    last_segment = (segment == segment[length - 1]).astype(running.dtype)
    leave_weight = jnp.exp(running[length - 1][None, :] - running) * last_segment[:, None] * steps_dt
    through = jnp.exp(running[length - 1]) * untouched[length - 1]
    added = jnp.einsum('shp,sn->hpn', leave_weight[:, :, None] * values_x, keys_b, precision=exact_mode)
    carry_state = carry_state * through[:, None, None] + added
    return ((carry_state, skip_gain), output)

def chain_blocks(values_x, keys_b, reads_c, steps_dt, log_decay, resets, skip_gain, start_state):
    row_count = values_x.shape[0]
    block_count = row_count // BLOCK
    pieces = tuple((member.reshape((block_count, BLOCK) + member.shape[1:]) for member in (values_x, keys_b, reads_c, steps_dt, log_decay, resets)))
    stepper = jax.checkpoint(scan_block)
    (final_state, _), outputs = lax.scan(stepper, (start_state, skip_gain), pieces)
    return (outputs.reshape(row_count, INNER), final_state)

def reference(conv_input, doc_start, conv_weight, conv_bias, dt_raw, dt_bias, a_log, skip_gain, cotangent):
    zero_tail = jnp.zeros((CONV - 1, CH), jnp.float32)
    zero_state = jnp.zeros((HEADS, HEAD_DIM, STATE), jnp.float32)
    outputs = []
    grads_in = []
    totals = (jnp.zeros((CONV, CH), jnp.float32), jnp.zeros((CH,), jnp.float32), jnp.zeros((HEADS,), jnp.float32), jnp.zeros((HEADS,), jnp.float32), jnp.zeros((HEADS,), jnp.float32))
    for group in range(N_DP):
        first_row = group * CHAIN
        rows_in = conv_input[first_row:first_row + CHAIN].astype(jnp.float32)
        starts = doc_start[first_row:first_row + CHAIN]
        raw_steps = dt_raw[first_row:first_row + CHAIN]
        upstream = cotangent[first_row:first_row + CHAIN].astype(jnp.float32)

        def forward(rows_value, weight_value, bias_value, dtb_value, alog_value, gain_value):
            values_x, keys_b, reads_c, steps_dt, log_decay = prepare_inputs(zero_tail, rows_value, starts, weight_value, bias_value, raw_steps, dtb_value, alog_value)
            result, _ = chain_blocks(values_x, keys_b, reads_c, steps_dt, log_decay, starts.astype(jnp.float32), gain_value, zero_state)
            return result
        result, pull_back = jax.vjp(forward, rows_in, conv_weight, conv_bias, dt_bias, a_log, skip_gain)
        grads = pull_back(upstream)
        outputs.append(result.astype(jnp.bfloat16))
        grads_in.append(grads[0].astype(jnp.bfloat16))
        totals = tuple((before + extra for before, extra in zip(totals, grads[1:])))
    scale = float(TOKENS) ** (-0.5)
    return (jnp.concatenate(outputs, axis=0), jnp.concatenate(grads_in, axis=0), totals[0] * scale, totals[1] * scale, totals[2] * scale, totals[3] * scale, totals[4] * scale)
```

```python
import functools

import jax
import jax.numpy as jnp
from jax import lax
from jax.experimental import pallas as pl
from jax.experimental.pallas import tpu as pltpu
from jax.sharding import PartitionSpec as P

HEADS = 80
HEAD_DIM = 64
STATE = 128
CONV = 4
INNER = 5120
CH = 5376
ROWS = 128
TILE = 512
TILES = INNER // TILE
TILE_HEADS = TILE // HEAD_DIM
LANES = 128

F32 = jnp.float32
BF16 = jnp.bfloat16
EXACT = lax.Precision.HIGHEST
VMEM_BYTES = 48 << 20


def iota(shape, axis):
    return lax.broadcasted_iota(jnp.int32, shape, axis)


def halves(value):
    high = value.astype(BF16)
    return high, (value - high.astype(F32)).astype(BF16)


def mm(a, b):
    return lax.dot_general(a, b, (((1,), (0,)), ((), ())), preferred_element_type=F32)


def mm_nt(a, b):
    return lax.dot_general(a, b, (((1,), (1,)), ((), ())), preferred_element_type=F32)


def exact(a, b):
    return lax.dot_general(
        a, b, (((1,), (0,)), ((), ())), precision=EXACT, preferred_element_type=F32
    )


def interleave(group, late):
    row, col = iota((2 * STATE, STATE), 0), iota((2 * STATE, STATE), 1)
    place = row % (2 * group)
    first = group if late else 0
    here = (place >= first) & (place < first + group)
    return jnp.where(here & (col == group * (row // (2 * group)) + place - first), 1.0, 0.0)


def head_columns(tile):
    head, col = iota((LANES, TILE), 0), iota((LANES, TILE), 1)
    return jnp.where(head == TILE_HEADS * tile + col // HEAD_DIM, 1.0, 0.0).astype(BF16)


def spread_heads(both_ref, tile):
    one_hot = head_columns(tile)
    return mm(both_ref[...], jnp.concatenate([one_hot, one_hot], axis=0))


def convolve(tail, rows, taps, valid):
    extended = jnp.concatenate([tail, rows], axis=0)
    total = taps[4:5] + taps[3:4] * rows
    shifted = [rows]
    for back in range(1, CONV):
        moved = extended[8 - back : 8 - back + ROWS] * valid[:, back - 1 : back]
        shifted.append(moved)
        total = total + taps[3 - back : 4 - back] * moved
    return total, shifted


def sigmoid(v):
    return 1.0 / (1.0 + jnp.exp(-v))


def head_kernel(raw_ref, small_ref, col_ref, row_ref, run_ref, runT_ref, dt_ref, dtT_ref, both_ref,
                sig_ref, sigsum_ref, through_ref, mask_ref):
    reset_col, reset_row = col_ref[:, 0:1], row_ref[0:1, :]
    low = iota((ROWS, ROWS), 0) >= iota((ROWS, ROWS), 1)
    segment_col = jnp.sum(jnp.where(low, reset_row, 0.0), axis=1, keepdims=True)
    high = iota((ROWS, ROWS), 0) <= iota((ROWS, ROWS), 1)
    segment_row = jnp.sum(jnp.where(high, reset_col, 0.0), axis=0, keepdims=True)
    mask_ref[0] = jnp.where(low & (segment_col == segment_row), 1.0, 0.0)
    mask_ref[1] = jnp.where(high & (segment_col == segment_row), 1.0, 0.0)
    biased = raw_ref[...] + small_ref[0:1, :]
    dt = jnp.maximum(biased, 0.0) + jnp.log1p(jnp.exp(-jnp.abs(biased)))
    decay = -jnp.exp(small_ref[1:2, :]) * dt
    lower = jnp.where(low, 1.0, 0.0)
    running = exact(lower, decay)
    sig = sigmoid(biased)
    sig_ref[...] = sig
    sigsum_ref[...] = exact(lower, sig)
    run_ref[...] = running
    runT_ref[...] = running.T
    dt_ref[...] = dt
    dtT_ref[...] = dt.T
    last = running[ROWS - 1 : ROWS]
    count = segment_col[ROWS - 1 : ROWS]
    untouched = jnp.where(segment_col == 0.0, 1.0, 0.0)
    entry = jnp.exp(running) * untouched
    leave = jnp.exp(last - running) * jnp.where(segment_col == count, 1.0, 0.0) * dt
    for at, part in ((0, leave), (ROWS, entry)):
        first, second = halves(part)
        both_ref[at : at + ROWS, :LANES] = first
        both_ref[at : at + ROWS, LANES:] = second
    through_ref[...] = jnp.broadcast_to(entry[ROWS - 1 : ROWS], (8, LANES))


def head_stage(raw, small, col, row):
    square = jax.ShapeDtypeStruct((ROWS, LANES), F32)
    return pl.pallas_call(
        head_kernel,
        out_shape=(
            square, square, square, square,
            jax.ShapeDtypeStruct((2 * ROWS, 2 * LANES), BF16),
            square, square,
            jax.ShapeDtypeStruct((8, LANES), F32),
            jax.ShapeDtypeStruct((2, ROWS, ROWS), F32),
        ),
        name="heads",
    )(raw, small, col, row)


def local_kernel(group, x_ref, tail_ref, taps_ref, xs_ref, tails_ref, tapss_ref, valid_ref, cot_ref, both_ref,
                 act_ref, pair_ref, bc_ref, lhs_hi, lhs_lo):
    tile = pl.program_id(0)
    valid = valid_ref[...]

    @pl.when(tile == 0)
    def _():
        total, _ = convolve(tails_ref[...].astype(F32), xs_ref[...].astype(F32), tapss_ref[...], valid)
        small = total * sigmoid(total)
        bc_ref[...] = small
        for at, late in ((0, False), (STATE, True)):
            pick = interleave(group, late).astype(BF16)
            first, second = halves(small[:, at : at + STATE])
            lhs_hi[:, at : at + ROWS] = mm_nt(pick, first).astype(BF16)
            lhs_lo[:, at : at + ROWS] = mm_nt(pick, second).astype(BF16)

    total, _ = convolve(tail_ref[...].astype(F32), x_ref[...].astype(F32), taps_ref[...], valid)
    act = total * sigmoid(total)
    act_ref[...] = act
    weight = spread_heads(both_ref, tile)
    first, second = halves(weight * jnp.concatenate([act, cot_ref[...].astype(F32)], axis=0))
    result = mm(lhs_hi[...], first) + mm(lhs_hi[...], second) + mm(lhs_lo[...], first)
    pair_ref[...] = result.reshape(pair_ref.shape)


def tile_spec(rows):
    return pl.BlockSpec((rows, TILE), lambda i: (0, i))


def small_spec(rows):
    return pl.BlockSpec((rows, 2 * STATE), lambda i: (0, INNER // (2 * STATE)))


def whole(shape):
    return pl.BlockSpec(shape, lambda i: (0,) * len(shape))


def local_stage(group, conv_input, tail, taps, valid, cotangent, both):
    groups = STATE // group
    return pl.pallas_call(
        functools.partial(local_kernel, group),
        grid=(TILES,),
        in_specs=[
            tile_spec(ROWS), tile_spec(8), tile_spec(8),
            small_spec(ROWS), small_spec(8), small_spec(8),
            whole((ROWS, 8)), tile_spec(ROWS), whole((2 * ROWS, 2 * LANES)),
        ],
        out_specs=[
            tile_spec(ROWS),
            pl.BlockSpec((groups, 2 * group, TILE), lambda i: (0, 0, i)),
            whole((ROWS, 2 * STATE)),
        ],
        out_shape=(
            jax.ShapeDtypeStruct((ROWS, INNER), F32),
            jax.ShapeDtypeStruct((groups, 2 * group, INNER), F32),
            jax.ShapeDtypeStruct((ROWS, 2 * STATE), F32),
        ),
        scratch_shapes=[pltpu.VMEM((2 * STATE, 2 * ROWS), BF16)] * 2,
        compiler_params=pltpu.CompilerParams(vmem_limit_bytes=VMEM_BYTES),
        name="local",
    )(conv_input, tail, taps, conv_input, tail, taps, valid, cotangent, both)


def within_kernel(act_ref, cot_ref, bc_ref, run_ref, runT_ref, dt_ref, dtT_ref, mask_ref,
                  out_ref, grad_ref, score_grad_ref, score, scoreT):
    tile = pl.program_id(0)

    @pl.when(tile == 0)
    def _():
        keys, reads = bc_ref[:, :STATE], bc_ref[:, STATE:]
        keys_hi, keys_lo = halves(keys)
        reads_hi, reads_lo = halves(reads)
        score[...] = mask_ref[0] * (mm_nt(reads_hi, keys_hi) + mm_nt(reads_hi, keys_lo) + mm_nt(reads_lo, keys_hi))
        scoreT[...] = mask_ref[1] * (mm_nt(keys_hi, reads_hi) + mm_nt(keys_hi, reads_lo) + mm_nt(keys_lo, reads_hi))
        score_grad_ref[...] = jnp.zeros_like(score_grad_ref)

    turn = lax.rem(LANES - TILE_HEADS * tile, LANES)
    run = pltpu.roll(run_ref[...], turn, 1)
    dt = pltpu.roll(dt_ref[...], turn, 1)
    left = iota((ROWS, LANES), 1) < HEAD_DIM
    left = jnp.where(left, 1.0, 0.0).astype(BF16)
    right = 1.0 - left
    score_grad = score_grad_ref[...]
    for pair in range(TILE_HEADS // 2):
        lanes = slice(LANES * pair, LANES * (pair + 1))
        spread, weights, weightsT = [], [], []
        for head in (2 * pair, 2 * pair + 1):
            run_col, run_row = run[:, head : head + 1], runT_ref[head : head + 1, :]
            difference = run_col - run_row
            step = jnp.exp(jnp.minimum(difference, 0.0)) * dtT_ref[head : head + 1, :]
            spread.append(step)
            weights.append(step * score[...])
            weightsT.append(jnp.exp(jnp.minimum(-difference, 0.0)) * dt[:, head : head + 1] * scoreT[...])
        x_hi, x_lo = halves(act_ref[:, lanes])
        upstream = cot_ref[:, lanes]
        x_hi2 = jnp.concatenate([x_hi * left, x_hi * right], axis=0)
        x_lo2 = jnp.concatenate([x_lo * left, x_lo * right], axis=0)
        upstream2 = jnp.concatenate([upstream * left, upstream * right], axis=0)
        w_hi, w_lo = halves(jnp.concatenate(weights, axis=1))
        wide = mm(w_hi, jnp.concatenate([x_hi2, x_lo2], axis=1))
        out_ref[:, lanes] = wide[:, :LANES] + wide[:, LANES:] + mm(w_lo, x_hi2)
        wt_hi, wt_lo = halves(jnp.concatenate(weightsT, axis=1))
        grad_ref[:, lanes] = mm(wt_hi, upstream2) + mm(wt_lo, upstream2)
        inner = mm_nt(upstream2, jnp.concatenate([x_hi, x_lo], axis=0))
        inner = inner[:, :ROWS] + inner[:, ROWS:]
        score_grad = score_grad + inner[:ROWS] * spread[0] + inner[ROWS:] * spread[1]
    score_grad_ref[...] = score_grad

    @pl.when(tile == TILES - 1)
    def _():
        score_grad_ref[...] = score_grad_ref[...] * mask_ref[0]


def within_stage(act, cotangent, bc, run, runT, dt, dtT, mask):
    square = whole((ROWS, LANES))
    rows = pl.BlockSpec((TILE_HEADS, LANES), lambda i: (i, 0))
    wide = jax.ShapeDtypeStruct((ROWS, INNER), F32)
    return pl.pallas_call(
        within_kernel,
        grid=(TILES,),
        in_specs=[
            tile_spec(ROWS), tile_spec(ROWS), whole((ROWS, 2 * STATE)), square, rows, square, rows,
            whole((2, ROWS, ROWS)),
        ],
        out_specs=[tile_spec(ROWS), tile_spec(ROWS), whole((ROWS, ROWS))],
        out_shape=(wide, wide, jax.ShapeDtypeStruct((ROWS, ROWS), F32)),
        scratch_shapes=[pltpu.VMEM((ROWS, ROWS), F32)] * 2,
        compiler_params=pltpu.CompilerParams(vmem_limit_bytes=VMEM_BYTES),
        name="within",
    )(act, cotangent, bc, run, runT, dt, dtT, mask)


def carry_kernel(shards, pair_ref, through_ref, out_ref, decay):
    tile = pl.program_id(0)
    decay[...] = exact(through_ref[...], head_columns(tile).astype(F32))
    group = pair_ref.shape[1] // 2
    early = iota(pair_ref.shape[1:], 0) < group
    state = jnp.zeros(pair_ref.shape[1:], F32)
    for shard in range(shards):
        out_ref[shard] = state
        state = decay[shard : shard + 1, :] * state + pair_ref[shard]
    state = jnp.zeros(pair_ref.shape[1:], F32)
    for shard in reversed(range(shards)):
        out_ref[shard] = jnp.where(early, out_ref[shard], state)
        state = decay[shard : shard + 1, :] * state + pair_ref[shard]


def carry_stage(pairs, through):
    shards, rows, _ = pairs.shape
    block = pl.BlockSpec((shards, rows, TILE), lambda i: (0, 0, i))
    return pl.pallas_call(
        functools.partial(carry_kernel, shards),
        grid=(TILES,),
        in_specs=[block, whole((shards, LANES))],
        out_specs=block,
        out_shape=jax.ShapeDtypeStruct(pairs.shape, F32),
        scratch_shapes=[pltpu.VMEM((shards, TILE), F32)],
        compiler_params=pltpu.CompilerParams(vmem_limit_bytes=VMEM_BYTES),
        name="carry",
    )(pairs, through)


def conv_backward(grad, shifted, taps, valid):
    width = grad.shape[1]
    zeros = jnp.zeros((8, width), F32)
    total = jnp.concatenate([zeros, grad * taps[3:4]], axis=0)
    parts = [jnp.sum(grad * shifted[0], axis=0, keepdims=True)]
    for back in range(1, CONV):
        parts.insert(0, jnp.sum(grad * shifted[back], axis=0, keepdims=True))
        moved = jnp.concatenate([zeros, grad * valid[:, back - 1 : back] * taps[3 - back : 4 - back], zeros], axis=0)
        total = total + moved[back : back + ROWS + 8]
    parts.append(jnp.sum(grad, axis=0, keepdims=True))
    parts.append(jnp.zeros((3, width), F32))
    return total, jnp.concatenate(parts, axis=0)


def finish_kernel(group, x_ref, tail_ref, taps_ref, xs_ref, tails_ref, tapss_ref, valid_ref, cot_ref, both_ref,
                  out_in_ref, grad_in_ref, pair_ref, bc_ref, score_grad_ref, gain_ref, run_ref, dt_ref, sig_ref,
                  sigsum_ref, small_ref, through_ref,
                  out_ref, grad_ref, end_ref, borrowed_ref, taps_grad_ref, grads_ref, ends_ref, borroweds_ref,
                  tapss_grad_ref, heads_ref,
                  lhs_hi, lhs_lo, bc_grad, by_head, by_token):
    tile = pl.program_id(0)
    valid = valid_ref[...]

    @pl.when(tile == 0)
    def _():
        for at, source, late in ((0, STATE, False), (ROWS, 0, True)):
            pick = interleave(group, late).astype(BF16)
            first, second = halves(bc_ref[:, source : source + STATE])
            lhs_hi[at : at + ROWS, :] = mm_nt(first, pick).astype(BF16)
            lhs_lo[at : at + ROWS, :] = mm_nt(second, pick).astype(BF16)
        bc_grad[...] = jnp.zeros_like(bc_grad)
        by_head[...] = jnp.zeros_like(by_head)
        by_token[...] = jnp.zeros_like(by_token)

    total, shifted = convolve(tail_ref[...].astype(F32), x_ref[...].astype(F32), taps_ref[...], valid)
    gate = sigmoid(total)
    act = total * gate
    upstream = cot_ref[...].astype(F32)
    weight = spread_heads(both_ref, tile)
    leave, entry = weight[:ROWS], weight[ROWS:]
    states = pair_ref[...].reshape(2 * STATE, TILE)
    states_hi, states_lo = halves(states)
    read = mm(lhs_hi[...], states_hi) + mm(lhs_hi[...], states_lo) + mm(lhs_lo[...], states_hi)
    gain = gain_ref[...]
    through_state = out_in_ref[...] + entry * read[:ROWS]
    out_ref[...] = (through_state + gain * act).astype(BF16)
    act_grad_late = leave * read[ROWS:]
    act_grad = grad_in_ref[...] + act_grad_late

    first, second = halves(jnp.concatenate([entry * upstream, leave * act], axis=0))
    bc_grad[...] += mm_nt(first, states_hi) + mm_nt(first, states_lo) + mm_nt(second, states_hi)

    one_hot = head_columns(tile)
    first, second = halves(jnp.concatenate([upstream * through_state, act * act_grad], axis=0))
    by_token[...] += mm_nt(first, one_hot) + mm_nt(second, one_hot)
    crossed = states * pltpu.roll(states, group, 0)
    crossed = jnp.where(iota((2 * STATE, TILE), 0) % (2 * group) >= group, crossed, 0.0)
    sums = jnp.concatenate(
        [
            jnp.sum(act * act_grad_late, axis=0, keepdims=True),
            jnp.sum(crossed, axis=0, keepdims=True),
            jnp.sum(upstream * act, axis=0, keepdims=True),
            jnp.zeros((5, TILE), F32),
        ],
        axis=0,
    )
    by_head[...] += lax.dot_general(
        sums, one_hot.astype(F32), (((1,), (1,)), ((), ())), precision=EXACT, preferred_element_type=F32
    )

    act_grad = act_grad + gain * upstream
    conv_grad = act_grad * (gate + act * (1.0 - gate))
    full, taps_grad_ref[...] = conv_backward(conv_grad, shifted, taps_ref[...], valid)
    borrowed_ref[...] = full[:8]
    grad_ref[...] = full[8:].astype(BF16)
    end_ref[...] = full[ROWS - 8 :]

    @pl.when(tile == TILES - 1)
    def _():
        score_grad = score_grad_ref[...]
        keys, reads = bc_ref[:, :STATE], bc_ref[:, STATE:]
        reads_grad = exact(bc_grad[:ROWS], interleave(group, False)) + exact(score_grad, keys)
        keys_grad = exact(bc_grad[ROWS:], interleave(group, True)) + exact(score_grad.T, reads)
        total, shifted = convolve(tails_ref[...].astype(F32), xs_ref[...].astype(F32), tapss_ref[...], valid)
        gate = sigmoid(total)
        small_grad = jnp.concatenate([keys_grad, reads_grad], axis=1) * (gate + total * gate * (1.0 - gate))
        full, tapss_grad_ref[...] = conv_backward(small_grad, shifted, tapss_ref[...], valid)
        borroweds_ref[...] = full[:8]
        grads_ref[...] = full[8:].astype(BF16)
        ends_ref[...] = full[ROWS - 8 :]

        read_sum, added_sum = by_token[:ROWS], by_token[ROWS:]
        at_end = by_head[0:1, :] + through_ref[0:1, :] * by_head[1:2, :]
        run_grad = read_sum - added_sum + jnp.where(iota((ROWS, LANES), 0) == ROWS - 1, at_end, 0.0)
        alog_grad = jnp.sum(run_grad * run_ref[...], axis=0, keepdims=True)
        bias_grad = jnp.sum(added_sum / dt_ref[...] * sig_ref[...], axis=0, keepdims=True)
        rate = jnp.exp(small_ref[1:2, :])
        bias_grad = bias_grad - rate * jnp.sum(run_grad * sigsum_ref[...], axis=0, keepdims=True)
        heads_ref[...] = jnp.concatenate([bias_grad, alog_grad, by_head[2:3, :], jnp.zeros((5, LANES), F32)], axis=0)


def finish_stage(group, conv_input, tail, taps, valid, cotangent, both, out_in, grad_in, pairs, bc, score_grad,
                 gain, run, dt, sig, sigsum, small, through):
    groups = STATE // group
    square = whole((ROWS, LANES))
    eight = pl.BlockSpec((8, 2 * STATE), lambda i: (0, 0))
    return pl.pallas_call(
        functools.partial(finish_kernel, group),
        grid=(TILES,),
        in_specs=[
            tile_spec(ROWS), tile_spec(8), tile_spec(8),
            small_spec(ROWS), small_spec(8), small_spec(8),
            whole((ROWS, 8)), tile_spec(ROWS), whole((2 * ROWS, 2 * LANES)),
            tile_spec(ROWS), tile_spec(ROWS),
            pl.BlockSpec((groups, 2 * group, TILE), lambda i: (0, 0, i)),
            whole((ROWS, 2 * STATE)), whole((ROWS, ROWS)), tile_spec(1),
            square, square, square, square, whole((8, LANES)), whole((8, LANES)),
        ],
        out_specs=[
            tile_spec(ROWS), tile_spec(ROWS), tile_spec(16), tile_spec(8), tile_spec(8),
            whole((ROWS, 2 * STATE)), whole((16, 2 * STATE)), eight, eight, whole((8, LANES)),
        ],
        out_shape=(
            jax.ShapeDtypeStruct((ROWS, INNER), BF16),
            jax.ShapeDtypeStruct((ROWS, INNER), BF16),
            jax.ShapeDtypeStruct((16, INNER), F32),
            jax.ShapeDtypeStruct((8, INNER), F32),
            jax.ShapeDtypeStruct((8, INNER), F32),
            jax.ShapeDtypeStruct((ROWS, 2 * STATE), BF16),
            jax.ShapeDtypeStruct((16, 2 * STATE), F32),
            jax.ShapeDtypeStruct((8, 2 * STATE), F32),
            jax.ShapeDtypeStruct((8, 2 * STATE), F32),
            jax.ShapeDtypeStruct((8, LANES), F32),
        ),
        scratch_shapes=[
            pltpu.VMEM((2 * ROWS, 2 * STATE), BF16), pltpu.VMEM((2 * ROWS, 2 * STATE), BF16),
            pltpu.VMEM((2 * ROWS, 2 * STATE), F32), pltpu.VMEM((8, LANES), F32), pltpu.VMEM((2 * ROWS, LANES), F32),
        ],
        compiler_params=pltpu.CompilerParams(vmem_limit_bytes=VMEM_BYTES),
        name="finish",
    )(conv_input, tail, taps, conv_input, tail, taps, valid, cotangent, both, out_in, grad_in, pairs, bc, score_grad,
      gain, run, dt, sig, sigsum, small, through)


def exchange(array, axis):
    return lax.all_to_all(array, axis, 0, 0, tiled=True)


def pad_heads(array):
    return jnp.pad(array, ((0, 0), (0, LANES - HEADS)))


def neighbour(array, by):
    size = lax.axis_size("seq")
    return lax.ppermute(array, "seq", [(i, i + by) for i in range(size) if 0 <= i + by < size])


def total_over_all(flat):
    size = lax.axis_size("dp") * lax.axis_size("seq")
    piece = exchange(flat.reshape(size, flat.shape[0] // size), ("dp", "seq")).sum(0)
    return exchange(jnp.broadcast_to(piece[None], (size,) + piece.shape), ("dp", "seq")).reshape(-1)


def on_device(conv_input, doc_start, conv_weight, conv_bias, dt_raw, dt_bias, a_log, skip_gain, cotangent):
    shards = lax.axis_size("seq")
    group = STATE // shards
    resets = doc_start.astype(F32)
    kept = 1.0 - resets
    keep = jnp.stack([kept[ROWS - 2] * kept[ROWS - 1], kept[ROWS - 1], jnp.ones((), F32)])
    tail_out = conv_input[ROWS - CONV + 1 :] * keep[:, None].astype(BF16)
    tail = neighbour(jnp.pad(tail_out, ((8 - CONV + 1, 0), (0, 0))), 1)
    one_back = jnp.concatenate([jnp.ones((1,), F32), kept[:-1]])
    two_back = jnp.concatenate([jnp.ones((2,), F32), kept[:-2]])
    valid = jnp.stack([kept, kept * one_back, kept * one_back * two_back] + [kept] * 5, axis=1)
    taps = jnp.concatenate([conv_weight, conv_bias[None], jnp.zeros((3, CH), F32)], axis=0)
    small = jnp.pad(jnp.stack([dt_bias, a_log]), ((0, 6), (0, LANES - HEADS)))
    gain = jnp.repeat(skip_gain, HEAD_DIM)[None]

    run, runT, dt, dtT, both, sig, sigsum, through, mask = head_stage(
        pad_heads(dt_raw), small, jnp.broadcast_to(resets[:, None], (ROWS, 8)), resets[None]
    )
    all_through = exchange(jnp.broadcast_to(through[None, 0], (shards, LANES)), "seq")
    act, pairs, bc = local_stage(group, conv_input, tail, taps, valid, cotangent, both)
    gathered = exchange(pairs, "seq")
    out_in, grad_in, score_grad = within_stage(act, cotangent, bc, run, runT, dt, dtT, mask)
    carried = exchange(carry_stage(gathered, all_through), "seq")
    out, grad, end, borrowed, taps_grad, grads, ends, borroweds, tapss_grad, heads = finish_stage(
        group, conv_input, tail, taps, valid, cotangent, both, out_in, grad_in, carried, bc, score_grad, gain,
        run, dt, sig, sigsum, small, through,
    )
    returned = neighbour(jnp.concatenate([borrowed, borroweds], axis=1), -1)[8 - CONV + 1 :]
    tail_rows = jnp.concatenate([end, ends], axis=1)
    tail_rows = jnp.concatenate([tail_rows[: 16 - CONV + 1], tail_rows[16 - CONV + 1 :] + returned * keep[:, None]])
    whole_grad = jnp.concatenate(
        [jnp.concatenate([grad[: ROWS - 16], grads[: ROWS - 16]], axis=1), tail_rows.astype(BF16)], axis=0
    )
    params = jnp.concatenate([taps_grad[:5], tapss_grad[:5]], axis=1).reshape(-1)
    params = jnp.concatenate([params, heads[:3].reshape(-1)])
    size = lax.axis_size("dp") * shards
    used = params.shape[0]
    params = jnp.pad(params, (0, -used % (size * LANES)))
    params = total_over_all(params) * float(size * ROWS) ** (-0.5)
    heads = params[5 * CH : 5 * CH + 3 * LANES].reshape(3, LANES)[:, :HEADS]
    params = params[: 5 * CH].reshape(5, CH)
    return (out, whole_grad, params[:CONV], params[CONV], heads[0], heads[1], heads[2])


def solution(mesh):
    sharded = P(("dp", "seq"), None)
    return jax.shard_map(
        on_device,
        mesh=mesh,
        in_specs=(sharded, P(("dp", "seq")), P(), P(), sharded, P(), P(), P(), sharded),
        out_specs=(sharded, sharded, P(), P(), P(), P(), P()),
        check_vma=False,
    )
```

```python
import functools

import jax
import jax.numpy as jnp
from jax import lax
from jax.experimental import pallas as pl
from jax.experimental.pallas import tpu as pltpu
from jax.sharding import PartitionSpec as P

HEADS = 80
HEAD_DIM = 64
STATE = 128
CONV = 4
INNER = 5120
CH = 5376
ROWS = 128
TILE = 512
TILES = INNER // TILE
TILE_HEADS = TILE // HEAD_DIM
LANES = 128

F32 = jnp.float32
BF16 = jnp.bfloat16
EXACT = lax.Precision.HIGHEST
HALF_TILES = TILES // 2
VMEM_BYTES = 60 << 20


def iota(shape, axis):
    return lax.broadcasted_iota(jnp.int32, shape, axis)


def halves(value):
    high = value.astype(BF16)
    return high, (value - high.astype(F32)).astype(BF16)


def mm(a, b):
    return lax.dot_general(a, b, (((1,), (0,)), ((), ())), preferred_element_type=F32)


def mm_nt(a, b):
    return lax.dot_general(a, b, (((1,), (1,)), ((), ())), preferred_element_type=F32)


def exact(a, b):
    return lax.dot_general(
        a, b, (((1,), (0,)), ((), ())), precision=EXACT, preferred_element_type=F32
    )


def interleave(group, late):
    row, col = iota((2 * STATE, STATE), 0), iota((2 * STATE, STATE), 1)
    place = row % (2 * group)
    first = group if late else 0
    here = (place >= first) & (place < first + group)
    return jnp.where(here & (col == group * (row // (2 * group)) + place - first), 1.0, 0.0)


def head_columns(tile):
    head, col = iota((LANES, TILE), 0), iota((LANES, TILE), 1)
    return jnp.where(head == TILE_HEADS * tile + col // HEAD_DIM, 1.0, 0.0).astype(BF16)


def spread_heads(both_ref, tile):
    one_hot = head_columns(tile)
    return mm(both_ref[...], jnp.concatenate([one_hot, one_hot], axis=0))


def convolve(tail, rows, taps, valid):
    extended = jnp.concatenate([tail, rows], axis=0)
    total = taps[4:5] + taps[3:4] * rows
    shifted = [rows]
    for back in range(1, CONV):
        moved = extended[8 - back : 8 - back + ROWS] * valid[:, back - 1 : back]
        shifted.append(moved)
        total = total + taps[3 - back : 4 - back] * moved
    return total, shifted


def sigmoid(v):
    return 1.0 / (1.0 + jnp.exp(-v))


def head_kernel(raw_in_ref, small_ref, row_ref, end_ref, run_ref, runT_ref, dt_ref, dtT_ref, both_ref, sig_ref,
                sigsum_ref, through_ref, mask_ref, valid_ref, keep_ref, tail_ref, raw):
    reset_row = row_ref[...].astype(F32)
    token, other = iota((ROWS, ROWS), 0), iota((ROWS, ROWS), 1)
    reset_col = jnp.sum(jnp.where(token == other, reset_row, 0.0), axis=1, keepdims=True)
    low, high = token >= other, token <= other
    segment_col = jnp.sum(jnp.where(low, reset_row, 0.0), axis=1, keepdims=True)
    segment_row = jnp.sum(jnp.where(high, reset_col, 0.0), axis=0, keepdims=True)
    mask_ref[0] = jnp.where(low & (segment_col == segment_row), 1.0, 0.0)
    mask_ref[1] = jnp.where(high & (segment_col == segment_row), 1.0, 0.0)

    kept = jnp.broadcast_to(1.0 - reset_col, (ROWS, LANES))
    one_back = jnp.where(token < 1, 1.0, pltpu.roll(kept, 1, 0))
    two_back = jnp.where(token < 2, 1.0, pltpu.roll(kept, 2, 0))
    valid = jnp.where(other == 0, kept, jnp.where(other == 1, kept * one_back, kept * one_back * two_back))
    valid_ref[...] = valid[:, :8]
    one_on, two_on = pltpu.roll(kept, ROWS - 1, 0), pltpu.roll(kept, ROWS - 2, 0)
    keep = jnp.where(
        token == ROWS - 1, 1.0, jnp.where(token == ROWS - 2, one_on, jnp.where(token == ROWS - 3, one_on * two_on, 0.0))
    )[ROWS - 8 :]
    keep_ref[...] = keep
    tail_ref[...] = (end_ref[8:, :].astype(F32) * keep[:, 0:1]).astype(BF16)

    raw[...] = jnp.zeros_like(raw)
    raw[:, :HEADS] = raw_in_ref[...]
    biased = raw[...] + small_ref[0:1, :]
    dt = jnp.maximum(biased, 0.0) + jnp.log1p(jnp.exp(-jnp.abs(biased)))
    decay = -jnp.exp(small_ref[1:2, :]) * dt
    lower = jnp.where(low, 1.0, 0.0)
    running = exact(lower, decay)
    sig = sigmoid(biased)
    sig_ref[...] = sig
    sigsum_ref[...] = exact(lower, sig)
    run_ref[...] = running
    runT_ref[...] = running.T
    dt_ref[...] = dt
    dtT_ref[...] = dt.T
    last = running[ROWS - 1 : ROWS]
    count = segment_col[ROWS - 1 : ROWS]
    untouched = jnp.where(segment_col == 0.0, 1.0, 0.0)
    entry = jnp.exp(running) * untouched
    leave = jnp.exp(last - running) * jnp.where(segment_col == count, 1.0, 0.0) * dt
    for at, part in ((0, leave), (ROWS, entry)):
        first, second = halves(part)
        both_ref[at : at + ROWS, :LANES] = first
        both_ref[at : at + ROWS, LANES:] = second
    through_ref[...] = jnp.broadcast_to(entry[ROWS - 1 : ROWS], through_ref.shape)


def head_stage(shards, raw, small, row, conv_input):
    square = jax.ShapeDtypeStruct((ROWS, LANES), F32)
    shapes = (
        square, square, square, square,
        jax.ShapeDtypeStruct((2 * ROWS, 2 * LANES), BF16),
        square, square,
        jax.ShapeDtypeStruct((shards, LANES), F32),
        jax.ShapeDtypeStruct((2, ROWS, ROWS), F32),
        jax.ShapeDtypeStruct((ROWS, 8), F32),
        jax.ShapeDtypeStruct((8, LANES), F32),
        jax.ShapeDtypeStruct((8, CH), BF16),
    )
    return pl.pallas_call(
        head_kernel,
        grid=(1,),
        in_specs=[
            whole(raw.shape), whole((8, LANES)), whole((1, ROWS)),
            pl.BlockSpec((16, CH), lambda *at: (ROWS // 16 - 1, 0)),
        ],
        out_specs=[whole(shape.shape) for shape in shapes],
        out_shape=shapes,
        scratch_shapes=[pltpu.VMEM((ROWS, LANES), F32)],
        compiler_params=pltpu.CompilerParams(vmem_limit_bytes=VMEM_BYTES),
        name="heads",
    )(raw, small, row, conv_input)


def whole(shape):
    return pl.BlockSpec(shape, lambda *at: (0,) * len(shape))


def call(kernel, name, half, grid, in_specs, out_specs, out_shape, scratch_shapes, operands):
    return pl.pallas_call(
        kernel,
        grid_spec=pltpu.PrefetchScalarGridSpec(
            num_scalar_prefetch=1, grid=(grid,), in_specs=in_specs, out_specs=out_specs, scratch_shapes=scratch_shapes
        ),
        out_shape=out_shape,
        compiler_params=pltpu.CompilerParams(vmem_limit_bytes=VMEM_BYTES),
        name=name,
    )(half, *operands)


def tile_at(i, half):
    return lax.rem(i + HALF_TILES * half[0], TILES)


def tile_spec(rows):
    return pl.BlockSpec((rows, TILE), lambda i, half: (0, tile_at(i, half)))


def small_spec(rows):
    return pl.BlockSpec((rows, 2 * STATE), lambda *at: (0, INNER // (2 * STATE)))


def pair_spec(shape, first):
    if first:
        return pl.BlockSpec(shape[:2] + (TILE,), lambda i, half: (0, 0, jnp.minimum(i, HALF_TILES - 1)))
    return pl.BlockSpec(shape[:2] + (TILE,), lambda i, half: (0, 0, jnp.maximum(i - HALF_TILES, 0)))


def local_kernel(group, half_ref, x_ref, tail_ref, taps_ref, xs_ref, tails_ref, tapss_ref, valid_ref, cot_ref,
                 both_ref, pair_ref, bc_ref, lhs_hi, lhs_lo):
    valid = valid_ref[...]

    @pl.when(pl.program_id(0) == 0)
    def _():
        total, _ = convolve(tails_ref[...].astype(F32), xs_ref[...].astype(F32), tapss_ref[...], valid)
        small = total * sigmoid(total)
        bc_ref[...] = small
        for at, late in ((0, False), (STATE, True)):
            pick = interleave(group, late).astype(BF16)
            first, second = halves(small[:, at : at + STATE])
            lhs_hi[:, at : at + ROWS] = mm_nt(pick, first).astype(BF16)
            lhs_lo[:, at : at + ROWS] = mm_nt(pick, second).astype(BF16)

    total, _ = convolve(tail_ref[...].astype(F32), x_ref[...].astype(F32), taps_ref[...], valid)
    act = total * sigmoid(total)
    weight = spread_heads(both_ref, tile_at(pl.program_id(0), half_ref))
    first, second = halves(weight * jnp.concatenate([act, cot_ref[...].astype(F32)], axis=0))
    result = mm(lhs_hi[...], first) + mm(lhs_hi[...], second) + mm(lhs_lo[...], first)
    pair_ref[...] = result.reshape(pair_ref.shape)


def local_stage(group, half, conv_input, tail, taps, valid, cotangent, both):
    shape = (STATE // group, 2 * group, INNER // 2)
    return call(
        functools.partial(local_kernel, group), "local", half, HALF_TILES,
        [
            tile_spec(ROWS), tile_spec(8), tile_spec(8),
            small_spec(ROWS), small_spec(8), small_spec(8),
            whole((ROWS, 8)), tile_spec(ROWS), whole((2 * ROWS, 2 * LANES)),
        ],
        [pair_spec(shape, True), whole((ROWS, 2 * STATE))],
        (jax.ShapeDtypeStruct(shape, F32), jax.ShapeDtypeStruct((ROWS, 2 * STATE), F32)),
        [pltpu.VMEM((2 * STATE, 2 * ROWS), BF16)] * 2,
        (conv_input, tail, taps, conv_input, tail, taps, valid, cotangent, both),
    )


def within_kernel(half_ref, x_ref, tail_ref, taps_ref, valid_ref, cot_ref, bc_ref, run_ref, runT_ref, dt_ref, dtT_ref,
                  mask_ref, out_ref, grad_ref, score_grad_ref, score, scoreT):
    tile = pl.program_id(0)

    @pl.when(tile == 0)
    def _():
        keys, reads = bc_ref[:, :STATE], bc_ref[:, STATE:]
        keys_hi, keys_lo = halves(keys)
        reads_hi, reads_lo = halves(reads)
        score[...] = mask_ref[0] * (mm_nt(reads_hi, keys_hi) + mm_nt(reads_hi, keys_lo) + mm_nt(reads_lo, keys_hi))
        scoreT[...] = mask_ref[1] * (mm_nt(keys_hi, reads_hi) + mm_nt(keys_hi, reads_lo) + mm_nt(keys_lo, reads_hi))
        score_grad_ref[...] = jnp.zeros_like(score_grad_ref)

    total, _ = convolve(tail_ref[...].astype(F32), x_ref[...].astype(F32), taps_ref[...], valid_ref[...])
    act = total * sigmoid(total)
    turn = lax.rem(LANES - TILE_HEADS * tile_at(tile, half_ref), LANES)
    run = pltpu.roll(run_ref[...], turn, 1)
    dt = pltpu.roll(dt_ref[...], turn, 1)
    left = iota((ROWS, LANES), 1) < HEAD_DIM
    left = jnp.where(left, 1.0, 0.0).astype(BF16)
    right = 1.0 - left
    score_grad = score_grad_ref[...]
    for pair in range(TILE_HEADS // 2):
        lanes = slice(LANES * pair, LANES * (pair + 1))
        spread, weights, weightsT = [], [], []
        for head in (2 * pair, 2 * pair + 1):
            run_col, run_row = run[:, head : head + 1], runT_ref[head : head + 1, :]
            difference = run_col - run_row
            step = jnp.exp(jnp.minimum(difference, 0.0)) * dtT_ref[head : head + 1, :]
            spread.append(step)
            weights.append(step * score[...])
            weightsT.append(jnp.exp(jnp.minimum(-difference, 0.0)) * dt[:, head : head + 1] * scoreT[...])
        x_hi, x_lo = halves(act[:, lanes])
        upstream = cot_ref[:, lanes]
        x_hi2 = jnp.concatenate([x_hi * left, x_hi * right], axis=0)
        x_lo2 = jnp.concatenate([x_lo * left, x_lo * right], axis=0)
        upstream2 = jnp.concatenate([upstream * left, upstream * right], axis=0)
        w_hi, w_lo = halves(jnp.concatenate(weights, axis=1))
        wide = mm(w_hi, jnp.concatenate([x_hi2, x_lo2], axis=1))
        out_ref[:, lanes] = wide[:, :LANES] + wide[:, LANES:] + mm(w_lo, x_hi2)
        wt_hi, wt_lo = halves(jnp.concatenate(weightsT, axis=1))
        grad_ref[:, lanes] = mm(wt_hi, upstream2) + mm(wt_lo, upstream2)
        inner = mm_nt(upstream2, jnp.concatenate([x_hi, x_lo], axis=0))
        inner = inner[:, :ROWS] + inner[:, ROWS:]
        score_grad = score_grad + inner[:ROWS] * spread[0] + inner[ROWS:] * spread[1]
    score_grad_ref[...] = score_grad

    @pl.when(tile == TILES - 1)
    def _():
        score_grad_ref[...] = score_grad_ref[...] * mask_ref[0]


def within_stage(half, conv_input, tail, taps, valid, cotangent, bc, run, runT, dt, dtT, mask):
    square = whole((ROWS, LANES))
    rows = pl.BlockSpec((TILE_HEADS, LANES), lambda i, half: (tile_at(i, half), 0))
    wide = jax.ShapeDtypeStruct((ROWS, INNER), F32)
    return call(
        within_kernel, "within", half, TILES,
        [
            tile_spec(ROWS), tile_spec(8), tile_spec(8), whole((ROWS, 8)), tile_spec(ROWS),
            whole((ROWS, 2 * STATE)), square, rows, square, rows, whole((2, ROWS, ROWS)),
        ],
        [tile_spec(ROWS), tile_spec(ROWS), whole((ROWS, ROWS))],
        (wide, wide, jax.ShapeDtypeStruct((ROWS, ROWS), F32)),
        [pltpu.VMEM((ROWS, ROWS), F32)] * 2,
        (conv_input, tail, taps, valid, cotangent, bc, run, runT, dt, dtT, mask),
    )


def chip_decay(half_ref, through_ref, rows):
    one_hot = head_columns(tile_at(pl.program_id(0), half_ref)).astype(F32)
    return exact(through_ref[rows, :], one_hot)


def own_pair(half_ref):
    return pl.ds(pl.multiple_of(8 * (half_ref[1] // 4), 8), 8)


def even_odd(half_ref, through_ref):
    chips = chip_decay(half_ref, through_ref, own_pair(half_ref))
    place = lax.rem(half_ref[1], 4)
    row = iota(chips.shape, 0)
    earlier = jnp.sum(jnp.where(row == 2 * place, chips, 0.0), axis=0, keepdims=True)
    later = jnp.sum(jnp.where(row == 2 * place + 1, chips, 0.0), axis=0, keepdims=True)
    return earlier[None], later[None]


def join_kernel(group, half_ref, mine_ref, other_ref, through_ref, out_ref):
    earlier, later = even_odd(half_ref, through_ref)
    even = half_ref[0] == 0
    mine, other = mine_ref[...], other_ref[...]
    first, second = jnp.where(even, mine, other), jnp.where(even, other, mine)
    out_ref[:, :group, :] = later * first[:, :group] + second[:, :group]
    out_ref[:, group:, :] = first[:, group:] + earlier * second[:, group:]


def join_stage(group, half, mine, other, through):
    spec = pair_spec(mine.shape, True)
    return call(
        functools.partial(join_kernel, group), "join", half, HALF_TILES,
        [spec, spec, whole(through.shape)], spec, jax.ShapeDtypeStruct(mine.shape, F32), [], (mine, other, through),
    )


def part_kernel(group, half_ref, chip_ref, mine_ref, other_ref, through_ref, keep_ref, send_ref):
    earlier, later = even_odd(half_ref, through_ref)
    even = half_ref[0] == 0
    chip, mine, other = chip_ref[...], mine_ref[...], other_ref[...]
    state, adjoint = chip[:, :group], chip[:, group:]
    state_later = earlier * state + jnp.where(even, mine[:, :group], other[:, :group])
    adjoint_earlier = later * adjoint + jnp.where(even, other[:, group:], mine[:, group:])
    keep_ref[:, :group, :] = jnp.where(even, state, state_later)
    keep_ref[:, group:, :] = jnp.where(even, adjoint_earlier, adjoint)
    send_ref[:, :group, :] = jnp.where(even, state_later, state)
    send_ref[:, group:, :] = jnp.where(even, adjoint, adjoint_earlier)


def part_stage(group, half, chip, mine, other, through):
    spec = pair_spec(mine.shape, True)
    shape = jax.ShapeDtypeStruct(mine.shape, F32)
    return call(
        functools.partial(part_kernel, group), "part", half, HALF_TILES,
        [spec, spec, spec, whole(through.shape)], [spec, spec], (shape, shape), [], (chip, mine, other, through),
    )


def carry_kernel(group, half_ref, pair_ref, through_ref, out_ref, decay):
    chips = pair_ref.shape[0]
    decay[...] = chip_decay(half_ref, through_ref, slice(None))
    state = jnp.zeros((group, TILE), F32)
    for chip in range(chips):
        out_ref[chip, :group, :] = state
        state = decay[2 * chip : 2 * chip + 1, :] * decay[2 * chip + 1 : 2 * chip + 2, :] * state
        state = state + pair_ref[chip, :group, :]
    state = jnp.zeros((group, TILE), F32)
    for chip in reversed(range(chips)):
        out_ref[chip, group:, :] = state
        state = decay[2 * chip : 2 * chip + 1, :] * decay[2 * chip + 1 : 2 * chip + 2, :] * state
        state = state + pair_ref[chip, group:, :]


def carry_stage(group, half, pairs, through):
    spec = pair_spec(pairs.shape, True)
    return call(
        functools.partial(carry_kernel, group), "carry", half, HALF_TILES,
        [spec, whole(through.shape)], spec, jax.ShapeDtypeStruct(pairs.shape, F32),
        [pltpu.VMEM((through.shape[0], TILE), F32)], (pairs, through),
    )


def conv_backward(grad, shifted, taps, valid):
    width = grad.shape[1]
    zeros = jnp.zeros((8, width), F32)
    total = jnp.concatenate([zeros, grad * taps[3:4]], axis=0)
    parts = [jnp.sum(grad * shifted[0], axis=0, keepdims=True)]
    for back in range(1, CONV):
        parts.insert(0, jnp.sum(grad * shifted[back], axis=0, keepdims=True))
        moved = jnp.concatenate([zeros, grad * valid[:, back - 1 : back] * taps[3 - back : 4 - back], zeros], axis=0)
        total = total + moved[back : back + ROWS + 8]
    parts.append(jnp.sum(grad, axis=0, keepdims=True))
    parts.append(jnp.zeros((3, width), F32))
    return total, jnp.concatenate(parts, axis=0)


def finish_kernel(group, half_ref, x_ref, tail_ref, taps_ref, xs_ref, tails_ref, tapss_ref, valid_ref, cot_ref, both_ref,
                  out_in_ref, grad_in_ref, pair_a_ref, pair_b_ref, bc_ref, score_grad_ref, run_ref, dt_ref, sig_ref,
                  sigsum_ref, small_ref, through_ref,
                  out_ref, grad_ref, end_ref, borrowed_ref, taps_grad_ref, grads_ref, ends_ref, borroweds_ref,
                  tapss_grad_ref, heads_ref,
                  lhs_hi, lhs_lo, bc_grad, by_head, by_token):
    tile = pl.program_id(0)
    valid = valid_ref[...]

    @pl.when(tile == 0)
    def _():
        for at, source, late in ((0, STATE, False), (ROWS, 0, True)):
            pick = interleave(group, late).astype(BF16)
            first, second = halves(bc_ref[:, source : source + STATE])
            lhs_hi[at : at + ROWS, :] = mm_nt(first, pick).astype(BF16)
            lhs_lo[at : at + ROWS, :] = mm_nt(second, pick).astype(BF16)
        bc_grad[...] = jnp.zeros_like(bc_grad)
        by_head[...] = jnp.zeros_like(by_head)
        by_token[...] = jnp.zeros_like(by_token)

    total, shifted = convolve(tail_ref[...].astype(F32), x_ref[...].astype(F32), taps_ref[...], valid)
    gate = sigmoid(total)
    act = total * gate
    upstream = cot_ref[...].astype(F32)
    here = tile_at(tile, half_ref)
    weight = spread_heads(both_ref, here)
    leave, entry = weight[:ROWS], weight[ROWS:]
    states = jnp.where(tile < HALF_TILES, pair_a_ref[...], pair_b_ref[...]).reshape(2 * STATE, TILE)
    states_hi, states_lo = halves(states)
    read = mm(lhs_hi[...], states_hi) + mm(lhs_hi[...], states_lo) + mm(lhs_lo[...], states_hi)
    one_hot = head_columns(here)
    gain = exact(small_ref[...], one_hot.astype(F32))[2:3]
    through_state = out_in_ref[...] + entry * read[:ROWS]
    out_ref[...] = (through_state + gain * act).astype(BF16)
    act_grad_late = leave * read[ROWS:]
    act_grad = grad_in_ref[...] + act_grad_late

    first, second = halves(jnp.concatenate([entry * upstream, leave * act], axis=0))
    bc_grad[...] += mm_nt(first, states_hi) + mm_nt(first, states_lo) + mm_nt(second, states_hi)

    first, second = halves(jnp.concatenate([upstream * through_state, act * act_grad], axis=0))
    by_token[...] += mm_nt(first, one_hot) + mm_nt(second, one_hot)
    crossed = states * pltpu.roll(states, group, 0)
    crossed = jnp.where(iota((2 * STATE, TILE), 0) % (2 * group) >= group, crossed, 0.0)
    sums = jnp.concatenate(
        [
            jnp.sum(act * act_grad_late, axis=0, keepdims=True),
            jnp.sum(crossed, axis=0, keepdims=True),
            jnp.sum(upstream * act, axis=0, keepdims=True),
            jnp.zeros((5, TILE), F32),
        ],
        axis=0,
    )
    by_head[...] += lax.dot_general(
        sums, one_hot.astype(F32), (((1,), (1,)), ((), ())), precision=EXACT, preferred_element_type=F32
    )

    act_grad = act_grad + gain * upstream
    conv_grad = act_grad * (gate + act * (1.0 - gate))
    full, taps_grad_ref[...] = conv_backward(conv_grad, shifted, taps_ref[...], valid)
    borrowed_ref[...] = full[:8]
    grad_ref[...] = full[8:].astype(BF16)
    end_ref[...] = full[ROWS - 8 :]

    @pl.when(tile == TILES - 1)
    def _():
        score_grad = score_grad_ref[...]
        keys, reads = bc_ref[:, :STATE], bc_ref[:, STATE:]
        reads_grad = exact(bc_grad[:ROWS], interleave(group, False)) + exact(score_grad, keys)
        keys_grad = exact(bc_grad[ROWS:], interleave(group, True)) + exact(score_grad.T, reads)
        total, shifted = convolve(tails_ref[...].astype(F32), xs_ref[...].astype(F32), tapss_ref[...], valid)
        gate = sigmoid(total)
        small_grad = jnp.concatenate([keys_grad, reads_grad], axis=1) * (gate + total * gate * (1.0 - gate))
        full, tapss_grad_ref[...] = conv_backward(small_grad, shifted, tapss_ref[...], valid)
        borroweds_ref[...] = full[:8]
        grads_ref[...] = full[8:].astype(BF16)
        ends_ref[...] = full[ROWS - 8 :]

        read_sum, added_sum = by_token[:ROWS], by_token[ROWS:]
        at_end = by_head[0:1, :] + through_ref[0:1, :] * by_head[1:2, :]
        run_grad = read_sum - added_sum + jnp.where(iota((ROWS, LANES), 0) == ROWS - 1, at_end, 0.0)
        alog_grad = jnp.sum(run_grad * run_ref[...], axis=0, keepdims=True)
        bias_grad = jnp.sum(added_sum / dt_ref[...] * sig_ref[...], axis=0, keepdims=True)
        rate = jnp.exp(small_ref[1:2, :])
        bias_grad = bias_grad - rate * jnp.sum(run_grad * sigsum_ref[...], axis=0, keepdims=True)
        heads_ref[...] = jnp.concatenate([bias_grad, alog_grad, by_head[2:3, :], jnp.zeros((5, LANES), F32)], axis=0)


def finish_stage(group, half, conv_input, tail, taps, valid, cotangent, both, out_in, grad_in, pairs_a, pairs_b, bc,
                 score_grad, run, dt, sig, sigsum, small, through):
    square = whole((ROWS, LANES))
    shapes = (
        jax.ShapeDtypeStruct((ROWS, INNER), BF16),
        jax.ShapeDtypeStruct((ROWS, INNER), BF16),
        jax.ShapeDtypeStruct((16, INNER), F32),
        jax.ShapeDtypeStruct((8, INNER), F32),
        jax.ShapeDtypeStruct((8, INNER), F32),
        jax.ShapeDtypeStruct((ROWS, 2 * STATE), BF16),
        jax.ShapeDtypeStruct((16, 2 * STATE), F32),
        jax.ShapeDtypeStruct((8, 2 * STATE), F32),
        jax.ShapeDtypeStruct((8, 2 * STATE), F32),
        jax.ShapeDtypeStruct((8, LANES), F32),
    )
    return call(
        functools.partial(finish_kernel, group), "finish", half, TILES,
        [
            tile_spec(ROWS), tile_spec(8), tile_spec(8),
            small_spec(ROWS), small_spec(8), small_spec(8),
            whole((ROWS, 8)), tile_spec(ROWS), whole((2 * ROWS, 2 * LANES)),
            tile_spec(ROWS), tile_spec(ROWS), pair_spec(pairs_a.shape, True), pair_spec(pairs_b.shape, False),
            whole((ROWS, 2 * STATE)), whole((ROWS, ROWS)),
            square, square, square, square, whole((8, LANES)), whole((8, LANES)),
        ],
        [tile_spec(shape.shape[0]) for shape in shapes[:5]] + [whole(shape.shape) for shape in shapes[5:]],
        shapes,
        [
            pltpu.VMEM((2 * ROWS, 2 * STATE), BF16), pltpu.VMEM((2 * ROWS, 2 * STATE), BF16),
            pltpu.VMEM((2 * ROWS, 2 * STATE), F32), pltpu.VMEM((8, LANES), F32), pltpu.VMEM((2 * ROWS, LANES), F32),
        ],
        (conv_input, tail, taps, conv_input, tail, taps, valid, cotangent, both, out_in, grad_in, pairs_a, pairs_b, bc,
         score_grad, run, dt, sig, sigsum, small, through),
    )


def exchange(array, axis):
    return lax.all_to_all(array, axis, 0, 0, tiled=True)


def neighbour(array, by):
    size = lax.axis_size("seq")
    return lax.ppermute(array, "seq", [(i, i + by) for i in range(size) if 0 <= i + by < size])


def total_over_all(flat):
    size = lax.axis_size("dp") * lax.axis_size("seq")
    piece = exchange(flat.reshape(size, flat.shape[0] // size), ("dp", "seq")).sum(0)
    return exchange(jnp.broadcast_to(piece[None], (size,) + piece.shape), ("dp", "seq")).reshape(-1)


def swap(array):
    return lax.ppermute(array, "seq", [(i, i ^ 1) for i in range(lax.axis_size("seq"))])


def between_chips(array):
    size = lax.axis_size("seq")
    groups = [list(range(0, size, 2)), list(range(1, size, 2))]
    return lax.all_to_all(array, "seq", 0, 0, axis_index_groups=groups, tiled=True)


def on_device(conv_input, doc_start, conv_weight, conv_bias, dt_raw, dt_bias, a_log, skip_gain, cotangent):
    shards, place = lax.axis_size("seq"), lax.axis_index("seq")
    group = 2 * STATE // shards
    core = lax.rem(place, 2)
    half = jnp.stack([core, place // 2])
    other_half = jnp.stack([1 - core, place // 2])
    taps = jnp.concatenate([conv_weight, conv_bias[None], jnp.zeros((3, CH), F32)], axis=0)
    small = jnp.pad(jnp.stack([dt_bias, a_log, skip_gain]), ((0, 5), (0, LANES - HEADS)))

    run, runT, dt, dtT, both, sig, sigsum, through, mask, valid, keep, tail = head_stage(
        shards, dt_raw, small, doc_start[None], conv_input
    )
    tail = neighbour(tail, 1)
    all_through = exchange(through, "seq")
    theirs, bc = local_stage(group, other_half, conv_input, tail, taps, valid, cotangent, both)
    other = swap(theirs)
    mine, _ = local_stage(group, half, conv_input, tail, taps, valid, cotangent, both)
    gathered = between_chips(join_stage(group, half, mine, other, all_through))
    out_in, grad_in, score_grad = within_stage(
        half, conv_input, tail, taps, valid, cotangent, bc, run, runT, dt, dtT, mask
    )
    chip = between_chips(carry_stage(group, half, gathered, all_through))
    pairs_a, pairs_b = part_stage(group, half, chip, mine, other, all_through)
    pairs_b = swap(pairs_b)
    out, grad, end, borrowed, taps_grad, grads, ends, borroweds, tapss_grad, heads = finish_stage(
        group, half, conv_input, tail, taps, valid, cotangent, both, out_in, grad_in, pairs_a, pairs_b, bc, score_grad,
        run, dt, sig, sigsum, small, through[:8],
    )
    keep = keep[8 - CONV + 1 :, 0:1]
    returned = neighbour(jnp.concatenate([borrowed, borroweds], axis=1), -1)[8 - CONV + 1 :]
    tail_rows = jnp.concatenate([end, ends], axis=1)
    tail_rows = jnp.concatenate([tail_rows[: 16 - CONV + 1], tail_rows[16 - CONV + 1 :] + returned * keep])
    whole_grad = jnp.concatenate(
        [jnp.concatenate([grad[: ROWS - 16], grads[: ROWS - 16]], axis=1), tail_rows.astype(BF16)], axis=0
    )
    params = jnp.concatenate([taps_grad[:5], tapss_grad[:5]], axis=1).reshape(-1)
    params = jnp.concatenate([params, heads[:3].reshape(-1)])
    size = lax.axis_size("dp") * shards
    used = params.shape[0]
    params = jnp.pad(params, (0, -used % (size * LANES)))
    params = total_over_all(params) * float(size * ROWS) ** (-0.5)
    heads = params[5 * CH : 5 * CH + 3 * LANES].reshape(3, LANES)[:, :HEADS]
    params = params[: 5 * CH].reshape(5, CH)
    return (out, whole_grad, params[:CONV], params[CONV], heads[0], heads[1], heads[2])


def solution(mesh):
    sharded = P(("dp", "seq"), None)
    return jax.shard_map(
        on_device,
        mesh=mesh,
        in_specs=(sharded, P(("dp", "seq")), P(), P(), sharded, P(), P(), P(), sharded),
        out_specs=(sharded, sharded, P(), P(), P(), P(), P()),
        check_vma=False,
    )
```

```python
import functools

import jax
import jax.numpy as jnp
from jax import lax
from jax.experimental import pallas as pl
from jax.experimental.pallas import tpu as pltpu
from jax.sharding import PartitionSpec as P

HEADS = 80
HEAD_DIM = 64
STATE = 128
CONV = 4
INNER = 5120
CH = 5376
ROWS = 128
TILE = 512
TILES = INNER // TILE
TILE_HEADS = TILE // HEAD_DIM
LANES = 128

F32 = jnp.float32
BF16 = jnp.bfloat16
EXACT = lax.Precision.HIGHEST
HALF_TILES = TILES // 2
VMEM_BYTES = 60 << 20
MESH = pl.DeviceIdType.MESH


def iota(shape, axis):
    return lax.broadcasted_iota(jnp.int32, shape, axis)


def halves(value):
    high = value.astype(BF16)
    return high, (value - high.astype(F32)).astype(BF16)


def mm(a, b):
    return lax.dot_general(a, b, (((1,), (0,)), ((), ())), preferred_element_type=F32)


def mm_nt(a, b):
    return lax.dot_general(a, b, (((1,), (1,)), ((), ())), preferred_element_type=F32)


def exact(a, b):
    return lax.dot_general(
        a, b, (((1,), (0,)), ((), ())), precision=EXACT, preferred_element_type=F32
    )


def spread_exact(rows, one_hot):
    first, rest = rows.astype(BF16), rows
    rest = rest - first.astype(F32)
    second, third = halves(rest)
    return mm(first, one_hot) + mm(second, one_hot) + mm(third, one_hot)


def interleave(group, late):
    row, col = iota((2 * STATE, STATE), 0), iota((2 * STATE, STATE), 1)
    place = row % (2 * group)
    first = group if late else 0
    here = (place >= first) & (place < first + group)
    return jnp.where(here & (col == group * (row // (2 * group)) + place - first), 1.0, 0.0)


def head_columns(tile):
    head, col = iota((LANES, TILE), 0), iota((LANES, TILE), 1)
    return jnp.where(head == TILE_HEADS * tile + col // HEAD_DIM, 1.0, 0.0).astype(BF16)


def spread_heads(both_ref, tile):
    one_hot = head_columns(tile)
    return mm(both_ref[...], jnp.concatenate([one_hot, one_hot], axis=0))


def convolve(tail, rows, taps, valid):
    extended = jnp.concatenate([tail, rows], axis=0)
    total = taps[4:5] + taps[3:4] * rows
    shifted = [rows]
    for back in range(1, CONV):
        moved = extended[8 - back : 8 - back + ROWS] * valid[:, back - 1 : back]
        shifted.append(moved)
        total = total + taps[3 - back : 4 - back] * moved
    return total, shifted


def sigmoid(v):
    return 1.0 / (1.0 + jnp.exp(-v))


def greet(axes):
    barrier = pltpu.get_barrier_semaphore()
    for axis, size in axes:
        place = lax.axis_index(axis)

        def signal(k, carry):
            pl.semaphore_signal(
                barrier, inc=1, device_id={axis: lax.rem(place + k, size)}, device_id_type=MESH
            )
            return carry

        lax.fori_loop(1, size, signal, 0)
    pl.semaphore_wait(barrier, sum(size - 1 for _, size in axes))


def remote(source, target, send, receive, axis, peer):
    return pltpu.make_async_remote_copy(
        src_ref=source, dst_ref=target, send_sem=send, recv_sem=receive, device_id={axis: peer}, device_id_type=MESH
    )


def send_all(axis, size, source, target, send, receive):
    place = lax.axis_index(axis)

    def start(k, carry):
        peer = lax.rem(place + k, size)
        remote(source(peer), target.at[place], send.at[peer], receive.at[place], axis, peer).start()
        return carry

    lax.fori_loop(1, size, start, 0)


def wait_all(axis, size, source, target, send, receive):
    place = lax.axis_index(axis)

    def wait(k, carry):
        peer = lax.rem(place + k, size)
        copy = remote(source(peer), target.at[peer], send.at[peer], receive.at[peer], axis, peer)
        copy.wait_send()
        copy.wait_recv()
        return carry

    lax.fori_loop(1, size, wait, 0)


def head_kernel(shards, raw_in_ref, small_ref, row_ref, end_ref, run_ref, runT_ref, dt_ref, dtT_ref, both_ref, sig_ref,
                sigsum_ref, through_ref, mask_ref, valid_ref, keep_ref, tail_ref, own_ref, raw, own, slots, tail_out, send,
                receive, tail_send, tail_receive):
    greet((("seq", shards),))
    place = lax.axis_index("seq")
    reset_row = row_ref[...].astype(F32)
    token, other = iota((ROWS, ROWS), 0), iota((ROWS, ROWS), 1)
    reset_col = jnp.sum(jnp.where(token == other, reset_row, 0.0), axis=1, keepdims=True)
    low, high = token >= other, token <= other
    segment_col = jnp.sum(jnp.where(low, reset_row, 0.0), axis=1, keepdims=True)
    segment_row = jnp.sum(jnp.where(high, reset_col, 0.0), axis=0, keepdims=True)
    mask_ref[0] = jnp.where(low & (segment_col == segment_row), 1.0, 0.0)
    mask_ref[1] = jnp.where(high & (segment_col == segment_row), 1.0, 0.0)

    kept = jnp.broadcast_to(1.0 - reset_col, (ROWS, LANES))
    one_back = jnp.where(token < 1, 1.0, pltpu.roll(kept, 1, 0))
    two_back = jnp.where(token < 2, 1.0, pltpu.roll(kept, 2, 0))
    valid = jnp.where(other == 0, kept, jnp.where(other == 1, kept * one_back, kept * one_back * two_back))
    valid_ref[...] = valid[:, :8]
    one_on, two_on = pltpu.roll(kept, ROWS - 1, 0), pltpu.roll(kept, ROWS - 2, 0)
    keep = jnp.where(
        token == ROWS - 1, 1.0, jnp.where(token == ROWS - 2, one_on, jnp.where(token == ROWS - 3, one_on * two_on, 0.0))
    )[ROWS - 8 :]
    keep_ref[...] = keep
    tail_out[...] = (end_ref[8:, :].astype(F32) * keep[:, 0:1]).astype(BF16)
    onward = remote(tail_out, tail_ref, tail_send, tail_receive, "seq", lax.rem(place + 1, shards))

    @pl.when(place < shards - 1)
    def _():
        onward.start()

    raw[...] = jnp.zeros_like(raw)
    raw[:HEADS, :] = raw_in_ref[...]
    biased = raw[...].T + small_ref[0:1, :]
    dt = jnp.maximum(biased, 0.0) + jnp.log1p(jnp.exp(-jnp.abs(biased)))
    decay = -jnp.exp(small_ref[1:2, :]) * dt
    lower = jnp.where(low, 1.0, 0.0)
    running = exact(lower, decay)
    last = running[ROWS - 1 : ROWS]
    count = segment_col[ROWS - 1 : ROWS]
    untouched = jnp.where(segment_col == 0.0, 1.0, 0.0)
    entry = jnp.exp(running) * untouched
    own[...] = jnp.broadcast_to(entry[ROWS - 1 : ROWS], own.shape)
    own_ref[...] = own[...]
    send_all("seq", shards, lambda peer: own, slots, send, receive)
    sig = sigmoid(biased)
    sig_ref[...] = sig
    sigsum_ref[...] = exact(lower, sig)
    run_ref[...] = running
    runT_ref[...] = running.T
    dt_ref[...] = dt
    dtT_ref[...] = dt.T
    leave = jnp.exp(last - running) * jnp.where(segment_col == count, 1.0, 0.0) * dt
    for at, part in ((0, leave), (ROWS, entry)):
        first, second = halves(part)
        both_ref[at : at + ROWS, :LANES] = first
        both_ref[at : at + ROWS, LANES:] = second
    slots[place] = own[...]
    wait_all("seq", shards, lambda peer: own, slots, send, receive)
    for shard in range(shards):
        through_ref[shard : shard + 1, :] = slots[shard, 0:1, :]

    @pl.when(place < shards - 1)
    def _():
        onward.wait_send()

    @pl.when(place > 0)
    def _():
        onward.wait_recv()

    @pl.when(place == 0)
    def _():
        tail_ref[...] = jnp.zeros_like(tail_ref)


def head_stage(shards, raw, small, row, end):
    square = jax.ShapeDtypeStruct((ROWS, LANES), F32)
    shapes = (
        square, square, square, square,
        jax.ShapeDtypeStruct((2 * ROWS, 2 * LANES), BF16),
        square, square,
        jax.ShapeDtypeStruct((shards, LANES), F32),
        jax.ShapeDtypeStruct((2, ROWS, ROWS), F32),
        jax.ShapeDtypeStruct((ROWS, 8), F32),
        jax.ShapeDtypeStruct((8, LANES), F32),
        jax.ShapeDtypeStruct((8, CH), BF16),
        jax.ShapeDtypeStruct((8, LANES), F32),
    )
    in_vmem = pl.BlockSpec(memory_space=pltpu.VMEM)
    return pl.pallas_call(
        functools.partial(head_kernel, shards),
        in_specs=[in_vmem] * 4,
        out_specs=[in_vmem] * len(shapes),
        out_shape=shapes,
        scratch_shapes=[
            pltpu.VMEM((ROWS, LANES), F32), pltpu.VMEM((8, LANES), F32), pltpu.VMEM((shards, 8, LANES), F32),
            pltpu.VMEM((8, CH), BF16), pltpu.SemaphoreType.DMA((shards,)), pltpu.SemaphoreType.DMA((shards,)),
            pltpu.SemaphoreType.DMA, pltpu.SemaphoreType.DMA,
        ],
        compiler_params=pltpu.CompilerParams(
            vmem_limit_bytes=VMEM_BYTES, collective_id=0, has_side_effects=True
        ),
        name="heads",
    )(raw, small, row, end)


def whole(shape):
    return pl.BlockSpec(shape, lambda *at: (0,) * len(shape))


def call(kernel, name, half, grid, in_specs, out_specs, out_shape, scratch_shapes, operands):
    return pl.pallas_call(
        kernel,
        grid_spec=pltpu.PrefetchScalarGridSpec(
            num_scalar_prefetch=1, grid=(grid,), in_specs=in_specs, out_specs=out_specs, scratch_shapes=scratch_shapes
        ),
        out_shape=out_shape,
        compiler_params=pltpu.CompilerParams(vmem_limit_bytes=VMEM_BYTES),
        name=name,
    )(half, *operands)


def tile_at(i, half):
    return lax.rem(i + HALF_TILES * half[0], TILES)


def tile_spec(rows):
    return pl.BlockSpec((rows, TILE), lambda i, half: (0, tile_at(i, half)))


def small_spec(rows):
    return pl.BlockSpec((rows, 2 * STATE), lambda *at: (0, INNER // (2 * STATE)))


def pair_spec(shape, first):
    if first:
        return pl.BlockSpec(shape[:2] + (TILE,), lambda i, half: (0, 0, jnp.minimum(i, HALF_TILES - 1)))
    return pl.BlockSpec(shape[:2] + (TILE,), lambda i, half: (0, 0, jnp.maximum(i - HALF_TILES, 0)))


def local_kernel(group, half_ref, x_ref, tail_ref, taps_ref, xs_ref, tails_ref, tapss_ref, valid_ref, cot_ref,
                 both_ref, pair_ref, bc_ref, lhs_hi, lhs_lo):
    valid = valid_ref[...]

    @pl.when(pl.program_id(0) == 0)
    def _():
        total, _ = convolve(tails_ref[...].astype(F32), xs_ref[...].astype(F32), tapss_ref[...], valid)
        small = total * sigmoid(total)
        bc_ref[...] = small
        for at, late in ((0, False), (STATE, True)):
            pick = interleave(group, late).astype(BF16)
            first, second = halves(small[:, at : at + STATE])
            lhs_hi[:, at : at + ROWS] = mm_nt(pick, first).astype(BF16)
            lhs_lo[:, at : at + ROWS] = mm_nt(pick, second).astype(BF16)

    total, _ = convolve(tail_ref[...].astype(F32), x_ref[...].astype(F32), taps_ref[...], valid)
    act = total * sigmoid(total)
    weight = spread_heads(both_ref, tile_at(pl.program_id(0), half_ref))
    first, second = halves(weight * jnp.concatenate([act, cot_ref[...].astype(F32)], axis=0))
    result = mm(lhs_hi[...], first) + mm(lhs_hi[...], second) + mm(lhs_lo[...], first)
    pair_ref[...] = result.reshape(pair_ref.shape)


def local_stage(group, half, conv_input, tail, taps, valid, cotangent, both):
    shape = (STATE // group, 2 * group, INNER // 2)
    return call(
        functools.partial(local_kernel, group), "local", half, HALF_TILES,
        [
            tile_spec(ROWS), tile_spec(8), tile_spec(8),
            small_spec(ROWS), small_spec(8), small_spec(8),
            whole((ROWS, 8)), tile_spec(ROWS), whole((2 * ROWS, 2 * LANES)),
        ],
        [pair_spec(shape, True), whole((ROWS, 2 * STATE))],
        (jax.ShapeDtypeStruct(shape, F32), jax.ShapeDtypeStruct((ROWS, 2 * STATE), F32)),
        [pltpu.VMEM((2 * STATE, 2 * ROWS), BF16)] * 2,
        (conv_input, tail, taps, conv_input, tail, taps, valid, cotangent, both),
    )


def within_kernel(half_ref, x_ref, tail_ref, taps_ref, valid_ref, cot_ref, bc_ref, run_ref, runT_ref, dt_ref, dtT_ref,
                  mask_ref, out_ref, grad_ref, score_grad_ref, score, scoreT):
    tile = pl.program_id(0)

    @pl.when(tile == 0)
    def _():
        keys, reads = bc_ref[:, :STATE], bc_ref[:, STATE:]
        keys_hi, keys_lo = halves(keys)
        reads_hi, reads_lo = halves(reads)
        score[...] = mask_ref[0] * (mm_nt(reads_hi, keys_hi) + mm_nt(reads_hi, keys_lo) + mm_nt(reads_lo, keys_hi))
        scoreT[...] = mask_ref[1] * (mm_nt(keys_hi, reads_hi) + mm_nt(keys_hi, reads_lo) + mm_nt(keys_lo, reads_hi))
        score_grad_ref[...] = jnp.zeros_like(score_grad_ref)

    total, _ = convolve(tail_ref[...].astype(F32), x_ref[...].astype(F32), taps_ref[...], valid_ref[...])
    act = total * sigmoid(total)
    turn = lax.rem(LANES - TILE_HEADS * tile_at(tile, half_ref), LANES)
    run = pltpu.roll(run_ref[...], turn, 1)
    dt = pltpu.roll(dt_ref[...], turn, 1)
    left = iota((ROWS, LANES), 1) < HEAD_DIM
    left = jnp.where(left, 1.0, 0.0).astype(BF16)
    right = 1.0 - left
    score_grad = score_grad_ref[...]
    for pair in range(TILE_HEADS // 2):
        lanes = slice(LANES * pair, LANES * (pair + 1))
        spread, weights, weightsT = [], [], []
        for head in (2 * pair, 2 * pair + 1):
            run_col, run_row = run[:, head : head + 1], runT_ref[head : head + 1, :]
            difference = run_col - run_row
            step = jnp.exp(jnp.minimum(difference, 0.0)) * dtT_ref[head : head + 1, :]
            spread.append(step)
            weights.append(step * score[...])
            weightsT.append(jnp.exp(jnp.minimum(-difference, 0.0)) * dt[:, head : head + 1] * scoreT[...])
        x_hi, x_lo = halves(act[:, lanes])
        upstream = cot_ref[:, lanes]
        x_hi2 = jnp.concatenate([x_hi * left, x_hi * right], axis=0)
        x_lo2 = jnp.concatenate([x_lo * left, x_lo * right], axis=0)
        upstream2 = jnp.concatenate([upstream * left, upstream * right], axis=0)
        w_hi, w_lo = halves(jnp.concatenate(weights, axis=1))
        wide = mm(w_hi, jnp.concatenate([x_hi2, x_lo2], axis=1))
        out_ref[:, lanes] = wide[:, :LANES] + wide[:, LANES:] + mm(w_lo, x_hi2)
        wt_hi, wt_lo = halves(jnp.concatenate(weightsT, axis=1))
        grad_ref[:, lanes] = mm(wt_hi, upstream2) + mm(wt_lo, upstream2)
        inner = mm_nt(upstream2, jnp.concatenate([x_hi, x_lo], axis=0))
        inner = inner[:, :ROWS] + inner[:, ROWS:]
        score_grad = score_grad + inner[:ROWS] * spread[0] + inner[ROWS:] * spread[1]
    score_grad_ref[...] = score_grad

    @pl.when(tile == TILES - 1)
    def _():
        score_grad_ref[...] = score_grad_ref[...] * mask_ref[0]


def within_stage(half, conv_input, tail, taps, valid, cotangent, bc, run, runT, dt, dtT, mask):
    square = whole((ROWS, LANES))
    rows = pl.BlockSpec((TILE_HEADS, LANES), lambda i, half: (tile_at(i, half), 0))
    wide = jax.ShapeDtypeStruct((ROWS, INNER), F32)
    return call(
        within_kernel, "within", half, TILES,
        [
            tile_spec(ROWS), tile_spec(8), tile_spec(8), whole((ROWS, 8)), tile_spec(ROWS),
            whole((ROWS, 2 * STATE)), square, rows, square, rows, whole((2, ROWS, ROWS)),
        ],
        [tile_spec(ROWS), tile_spec(ROWS), whole((ROWS, ROWS))],
        (wide, wide, jax.ShapeDtypeStruct((ROWS, ROWS), F32)),
        [pltpu.VMEM((ROWS, ROWS), F32)] * 2,
        (conv_input, tail, taps, valid, cotangent, bc, run, runT, dt, dtT, mask),
    )


def chip_decay(half_ref, through_ref, rows):
    return spread_exact(through_ref[rows, :], head_columns(tile_at(pl.program_id(0), half_ref)))


def own_pair(half_ref):
    return pl.ds(pl.multiple_of(8 * (half_ref[1] // 4), 8), 8)


def even_odd(half_ref, through_ref):
    chips = chip_decay(half_ref, through_ref, own_pair(half_ref))
    place = lax.rem(half_ref[1], 4)
    row = iota(chips.shape, 0)
    earlier = jnp.sum(jnp.where(row == 2 * place, chips, 0.0), axis=0, keepdims=True)
    later = jnp.sum(jnp.where(row == 2 * place + 1, chips, 0.0), axis=0, keepdims=True)
    return earlier[None], later[None]


def join_kernel(group, half_ref, mine_ref, other_ref, through_ref, out_ref):
    earlier, later = even_odd(half_ref, through_ref)
    even = half_ref[0] == 0
    mine, other = mine_ref[...], other_ref[...]
    first, second = jnp.where(even, mine, other), jnp.where(even, other, mine)
    out_ref[:, :group, :] = later * first[:, :group] + second[:, :group]
    out_ref[:, group:, :] = first[:, group:] + earlier * second[:, group:]


def join_stage(group, half, mine, other, through):
    spec = pair_spec(mine.shape, True)
    return call(
        functools.partial(join_kernel, group), "join", half, HALF_TILES,
        [spec, spec, whole(through.shape)], spec, jax.ShapeDtypeStruct(mine.shape, F32), [], (mine, other, through),
    )


def part_kernel(group, half_ref, chip_ref, mine_ref, other_ref, through_ref, keep_ref, send_ref):
    earlier, later = even_odd(half_ref, through_ref)
    even = half_ref[0] == 0
    chip, mine, other = chip_ref[...], mine_ref[...], other_ref[...]
    state, adjoint = chip[:, :group], chip[:, group:]
    state_later = earlier * state + jnp.where(even, mine[:, :group], other[:, :group])
    adjoint_earlier = later * adjoint + jnp.where(even, other[:, group:], mine[:, group:])
    keep_ref[:, :group, :] = jnp.where(even, state, state_later)
    keep_ref[:, group:, :] = jnp.where(even, adjoint_earlier, adjoint)
    send_ref[:, :group, :] = jnp.where(even, state_later, state)
    send_ref[:, group:, :] = jnp.where(even, adjoint, adjoint_earlier)


def part_stage(group, half, chip, mine, other, through):
    spec = pair_spec(mine.shape, True)
    shape = jax.ShapeDtypeStruct(mine.shape, F32)
    return call(
        functools.partial(part_kernel, group), "part", half, HALF_TILES,
        [spec, spec, spec, whole(through.shape)], [spec, spec], (shape, shape), [], (chip, mine, other, through),
    )


def carry_kernel(group, half_ref, pair_ref, through_ref, out_ref, decay):
    chips = pair_ref.shape[0]
    decay[...] = chip_decay(half_ref, through_ref, slice(None))
    state = jnp.zeros((group, TILE), F32)
    for chip in range(chips):
        out_ref[chip, :group, :] = state
        state = decay[2 * chip : 2 * chip + 1, :] * decay[2 * chip + 1 : 2 * chip + 2, :] * state
        state = state + pair_ref[chip, :group, :]
    state = jnp.zeros((group, TILE), F32)
    for chip in reversed(range(chips)):
        out_ref[chip, group:, :] = state
        state = decay[2 * chip : 2 * chip + 1, :] * decay[2 * chip + 1 : 2 * chip + 2, :] * state
        state = state + pair_ref[chip, group:, :]


def carry_stage(group, half, pairs, through):
    spec = pair_spec(pairs.shape, True)
    return call(
        functools.partial(carry_kernel, group), "carry", half, HALF_TILES,
        [spec, whole(through.shape)], spec, jax.ShapeDtypeStruct(pairs.shape, F32),
        [pltpu.VMEM((through.shape[0], TILE), F32)], (pairs, through),
    )


def conv_backward(grad, shifted, taps, valid):
    width = grad.shape[1]
    zeros = jnp.zeros((8, width), F32)
    total = jnp.concatenate([zeros, grad * taps[3:4]], axis=0)
    parts = [jnp.sum(grad * shifted[0], axis=0, keepdims=True)]
    for back in range(1, CONV):
        parts.insert(0, jnp.sum(grad * shifted[back], axis=0, keepdims=True))
        moved = jnp.concatenate([zeros, grad * valid[:, back - 1 : back] * taps[3 - back : 4 - back], zeros], axis=0)
        total = total + moved[back : back + ROWS + 8]
    parts.append(jnp.sum(grad, axis=0, keepdims=True))
    parts.append(jnp.zeros((3, width), F32))
    return total, jnp.concatenate(parts, axis=0)


def finish_kernel(group, half_ref, x_ref, tail_ref, taps_ref, xs_ref, tails_ref, tapss_ref, valid_ref, cot_ref, both_ref,
                  out_in_ref, grad_in_ref, pair_a_ref, pair_b_ref, bc_ref, score_grad_ref, run_ref, dt_ref, sig_ref,
                  sigsum_ref, small_ref, through_ref,
                  out_ref, grad_ref, end_ref, borrowed_ref, taps_grad_ref, grads_ref, ends_ref, borroweds_ref,
                  tapss_grad_ref, heads_ref,
                  lhs_hi, lhs_lo, bc_grad, by_head, by_token):
    tile = pl.program_id(0)
    valid = valid_ref[...]

    @pl.when(tile == 0)
    def _():
        for at, source, late in ((0, STATE, False), (ROWS, 0, True)):
            pick = interleave(group, late).astype(BF16)
            first, second = halves(bc_ref[:, source : source + STATE])
            lhs_hi[at : at + ROWS, :] = mm_nt(first, pick).astype(BF16)
            lhs_lo[at : at + ROWS, :] = mm_nt(second, pick).astype(BF16)
        bc_grad[...] = jnp.zeros_like(bc_grad)
        by_head[...] = jnp.zeros_like(by_head)
        by_token[...] = jnp.zeros_like(by_token)

    total, shifted = convolve(tail_ref[...].astype(F32), x_ref[...].astype(F32), taps_ref[...], valid)
    gate = sigmoid(total)
    act = total * gate
    upstream = cot_ref[...].astype(F32)
    here = tile_at(tile, half_ref)
    weight = spread_heads(both_ref, here)
    leave, entry = weight[:ROWS], weight[ROWS:]
    states = jnp.where(tile < HALF_TILES, pair_a_ref[...], pair_b_ref[...]).reshape(2 * STATE, TILE)
    states_hi, states_lo = halves(states)
    read = mm(lhs_hi[...], states_hi) + mm(lhs_hi[...], states_lo) + mm(lhs_lo[...], states_hi)
    one_hot = head_columns(here)
    gain = spread_exact(small_ref[...], one_hot)[2:3]
    through_state = out_in_ref[...] + entry * read[:ROWS]
    out_ref[...] = (through_state + gain * act).astype(BF16)
    act_grad_late = leave * read[ROWS:]
    act_grad = grad_in_ref[...] + act_grad_late

    first, second = halves(jnp.concatenate([entry * upstream, leave * act], axis=0))
    bc_grad[...] += mm_nt(first, states_hi) + mm_nt(first, states_lo) + mm_nt(second, states_hi)

    first, second = halves(jnp.concatenate([upstream * through_state, act * act_grad], axis=0))
    by_token[...] += mm_nt(first, one_hot) + mm_nt(second, one_hot)
    crossed = states * pltpu.roll(states, group, 0)
    crossed = jnp.where(iota((2 * STATE, TILE), 0) % (2 * group) >= group, crossed, 0.0)
    sums = jnp.concatenate(
        [
            jnp.sum(act * act_grad_late, axis=0, keepdims=True),
            jnp.sum(crossed, axis=0, keepdims=True),
            jnp.sum(upstream * act, axis=0, keepdims=True),
            jnp.zeros((5, TILE), F32),
        ],
        axis=0,
    )
    by_head[...] += lax.dot_general(
        sums, one_hot.astype(F32), (((1,), (1,)), ((), ())), precision=EXACT, preferred_element_type=F32
    )

    act_grad = act_grad + gain * upstream
    conv_grad = act_grad * (gate + act * (1.0 - gate))
    full, taps_grad_ref[...] = conv_backward(conv_grad, shifted, taps_ref[...], valid)
    borrowed_ref[...] = full[:8]
    grad_ref[...] = full[8:].astype(BF16)
    end_ref[...] = full[ROWS - 8 :]

    @pl.when(tile == TILES - 1)
    def _():
        score_grad = score_grad_ref[...]
        keys, reads = bc_ref[:, :STATE], bc_ref[:, STATE:]
        reads_grad = exact(bc_grad[:ROWS], interleave(group, False)) + exact(score_grad, keys)
        keys_grad = exact(bc_grad[ROWS:], interleave(group, True)) + exact(score_grad.T, reads)
        total, shifted = convolve(tails_ref[...].astype(F32), xs_ref[...].astype(F32), tapss_ref[...], valid)
        gate = sigmoid(total)
        small_grad = jnp.concatenate([keys_grad, reads_grad], axis=1) * (gate + total * gate * (1.0 - gate))
        full, tapss_grad_ref[...] = conv_backward(small_grad, shifted, tapss_ref[...], valid)
        borroweds_ref[...] = full[:8]
        grads_ref[...] = full[8:].astype(BF16)
        ends_ref[...] = full[ROWS - 8 :]

        read_sum, added_sum = by_token[:ROWS], by_token[ROWS:]
        at_end = by_head[0:1, :] + through_ref[0:1, :] * by_head[1:2, :]
        run_grad = read_sum - added_sum + jnp.where(iota((ROWS, LANES), 0) == ROWS - 1, at_end, 0.0)
        alog_grad = jnp.sum(run_grad * run_ref[...], axis=0, keepdims=True)
        bias_grad = jnp.sum(added_sum / dt_ref[...] * sig_ref[...], axis=0, keepdims=True)
        rate = jnp.exp(small_ref[1:2, :])
        bias_grad = bias_grad - rate * jnp.sum(run_grad * sigsum_ref[...], axis=0, keepdims=True)
        heads_ref[...] = jnp.concatenate([bias_grad, alog_grad, by_head[2:3, :], jnp.zeros((5, LANES), F32)], axis=0)


def finish_stage(group, half, conv_input, tail, taps, valid, cotangent, both, out_in, grad_in, pairs_a, pairs_b, bc,
                 score_grad, run, dt, sig, sigsum, small, through):
    square = whole((ROWS, LANES))
    shapes = (
        jax.ShapeDtypeStruct((ROWS, INNER), BF16),
        jax.ShapeDtypeStruct((ROWS, INNER), BF16),
        jax.ShapeDtypeStruct((16, INNER), F32),
        jax.ShapeDtypeStruct((8, INNER), F32),
        jax.ShapeDtypeStruct((8, INNER), F32),
        jax.ShapeDtypeStruct((ROWS, 2 * STATE), BF16),
        jax.ShapeDtypeStruct((16, 2 * STATE), F32),
        jax.ShapeDtypeStruct((8, 2 * STATE), F32),
        jax.ShapeDtypeStruct((8, 2 * STATE), F32),
        jax.ShapeDtypeStruct((8, LANES), F32),
    )
    return call(
        functools.partial(finish_kernel, group), "finish", half, TILES,
        [
            tile_spec(ROWS), tile_spec(8), tile_spec(8),
            small_spec(ROWS), small_spec(8), small_spec(8),
            whole((ROWS, 8)), tile_spec(ROWS), whole((2 * ROWS, 2 * LANES)),
            tile_spec(ROWS), tile_spec(ROWS), pair_spec(pairs_a.shape, True), pair_spec(pairs_b.shape, False),
            whole((ROWS, 2 * STATE)), whole((ROWS, ROWS)),
            square, square, square, square, whole((8, LANES)), whole((8, LANES)),
        ],
        [tile_spec(shape.shape[0]) for shape in shapes[:5]] + [whole(shape.shape) for shape in shapes[5:]],
        shapes,
        [
            pltpu.VMEM((2 * ROWS, 2 * STATE), BF16), pltpu.VMEM((2 * ROWS, 2 * STATE), BF16),
            pltpu.VMEM((2 * ROWS, 2 * STATE), F32), pltpu.VMEM((8, LANES), F32), pltpu.VMEM((2 * ROWS, LANES), F32),
        ],
        (conv_input, tail, taps, conv_input, tail, taps, valid, cotangent, both, out_in, grad_in, pairs_a, pairs_b, bc,
         score_grad, run, dt, sig, sigsum, small, through),
    )


def total_kernel(shards, groups, scale, taps_ref, small_ref, heads_ref, borrowed_ref, borroweds_ref, end_ref, ends_ref,
                 keep_ref, weight_ref, bias_ref, heads_out_ref, last_ref,
                 parts, slots, piece, dp_slots, result, got, got_small, send, receive, dp_send, dp_receive, back_send,
                 back_receive, rows_send, rows_receive):
    greet((("seq", shards), ("dp", groups)))
    place, group = lax.axis_index("seq"), lax.axis_index("dp")
    before = lax.rem(place + shards - 1, shards)
    returns = [
        remote(borrowed_ref, got, rows_send.at[0], rows_receive.at[0], "seq", before),
        remote(borroweds_ref, got_small, rows_send.at[1], rows_receive.at[1], "seq", before),
    ]
    wide = CH // LANES
    parts[...] = jnp.zeros_like(parts)
    for at in range(wide + 1):
        if at < INNER // LANES:
            block = taps_ref[:, LANES * at : LANES * (at + 1)]
        elif at < wide:
            block = small_ref[:, LANES * at - INNER : LANES * (at + 1) - INNER]
        else:
            block = heads_ref[...]
        parts[at % shards, 8 * (at // shards) : 8 * (at // shards) + 8, :] = block
    send_all("seq", shards, lambda peer: parts.at[peer], slots, send, receive)

    @pl.when(place > 0)
    def _():
        for copy in returns:
            copy.start()

    slots[place] = parts[place]
    wait_all("seq", shards, lambda peer: parts.at[peer], slots, send, receive)
    piece[...] = jnp.sum(slots[...], axis=0)
    send_all("dp", groups, lambda peer: piece, dp_slots, dp_send, dp_receive)
    dp_slots[group] = piece[...]
    wait_all("dp", groups, lambda peer: piece, dp_slots, dp_send, dp_receive)
    piece[...] = jnp.sum(dp_slots[...], axis=0) * scale
    send_all("seq", shards, lambda peer: piece, result, back_send, back_receive)
    result[place] = piece[...]

    @pl.when(place > 0)
    def _():
        for copy in returns:
            copy.wait_send()

    rows = 8 - CONV + 1

    @pl.when(place < shards - 1)
    def _():
        for copy in returns:
            copy.wait_recv()
        keep = keep_ref[:, 0:1]
        for lanes, source, end in ((slice(0, INNER), got, end_ref), (slice(INNER, CH), got_small, ends_ref)):
            last_ref[:8, lanes] = end[:8, :].astype(BF16)
            late = iota(source.shape, 0) >= rows
            last_ref[8:, lanes] = (end[8:, :] + jnp.where(late, source[...] * keep, 0.0)).astype(BF16)

    @pl.when(place == shards - 1)
    def _():
        last_ref[:, :INNER] = end_ref[...].astype(BF16)
        last_ref[:, INNER:] = ends_ref[...].astype(BF16)

    wait_all("seq", shards, lambda peer: piece, result, back_send, back_receive)
    for at in range(wide + 1):
        block = result[at % shards, 8 * (at // shards) : 8 * (at // shards) + 8, :]
        if at < wide:
            weight_ref[:, LANES * at : LANES * (at + 1)] = block[:CONV]
            bias_ref[:, LANES * at : LANES * (at + 1)] = block[CONV : CONV + 1]
        else:
            heads_out_ref[...] = block


def total_stage(shards, groups, scale, *operands):
    depth = 8 * pl.cdiv(CH // LANES + 1, shards)
    in_vmem = pl.BlockSpec(memory_space=pltpu.VMEM)
    shapes = (
        jax.ShapeDtypeStruct((CONV, CH), F32),
        jax.ShapeDtypeStruct((1, CH), F32),
        jax.ShapeDtypeStruct((8, LANES), F32),
        jax.ShapeDtypeStruct((16, CH), BF16),
    )
    dma = pltpu.SemaphoreType.DMA
    return pl.pallas_call(
        functools.partial(total_kernel, shards, groups, scale),
        in_specs=[in_vmem] * len(operands),
        out_specs=[in_vmem] * len(shapes),
        out_shape=shapes,
        scratch_shapes=[
            pltpu.VMEM((shards, depth, LANES), F32), pltpu.VMEM((shards, depth, LANES), F32),
            pltpu.VMEM((depth, LANES), F32), pltpu.VMEM((groups, depth, LANES), F32),
            pltpu.VMEM((shards, depth, LANES), F32),
            pltpu.VMEM((8, INNER), F32), pltpu.VMEM((8, 2 * STATE), F32),
            dma((shards,)), dma((shards,)), dma((groups,)), dma((groups,)), dma((shards,)), dma((shards,)),
            dma((2,)), dma((2,)),
        ],
        compiler_params=pltpu.CompilerParams(
            vmem_limit_bytes=VMEM_BYTES, collective_id=1, has_side_effects=True
        ),
        name="totals",
    )(*operands)


def swap(array):
    return lax.ppermute(array, "seq", [(i, i ^ 1) for i in range(lax.axis_size("seq"))])


def between_chips(array):
    size = lax.axis_size("seq")
    groups = [list(range(0, size, 2)), list(range(1, size, 2))]
    return lax.all_to_all(array, "seq", 0, 0, axis_index_groups=groups, tiled=True)


def on_device(conv_input, doc_start, conv_weight, conv_bias, dt_raw, dt_bias, a_log, skip_gain, cotangent):
    shards, place = lax.axis_size("seq"), lax.axis_index("seq")
    group = 2 * STATE // shards
    core = lax.rem(place, 2)
    half = jnp.stack([core, place // 2])
    other_half = jnp.stack([1 - core, place // 2])
    taps = jnp.concatenate([conv_weight, conv_bias[None], jnp.zeros((3, CH), F32)], axis=0)
    small = jnp.pad(jnp.stack([dt_bias, a_log, skip_gain]), ((0, 5), (0, LANES - HEADS)))

    run, runT, dt, dtT, both, sig, sigsum, all_through, mask, valid, keep, tail, through = head_stage(
        shards, dt_raw.T, small, doc_start[None], conv_input[ROWS - 16 :]
    )
    theirs, bc = local_stage(group, other_half, conv_input, tail, taps, valid, cotangent, both)
    other = swap(theirs)
    mine, _ = local_stage(group, half, conv_input, tail, taps, valid, cotangent, both)
    gathered = between_chips(join_stage(group, half, mine, other, all_through))
    out_in, grad_in, score_grad = within_stage(
        half, conv_input, tail, taps, valid, cotangent, bc, run, runT, dt, dtT, mask
    )
    chip = between_chips(carry_stage(group, half, gathered, all_through))
    pairs_a, pairs_b = part_stage(group, half, chip, mine, other, all_through)
    pairs_b = swap(pairs_b)
    out, grad, end, borrowed, taps_grad, grads, ends, borroweds, tapss_grad, heads = finish_stage(
        group, half, conv_input, tail, taps, valid, cotangent, both, out_in, grad_in, pairs_a, pairs_b, bc, score_grad,
        run, dt, sig, sigsum, small, through,
    )
    groups = lax.axis_size("dp")
    weight_grad, bias_grad, heads, last = total_stage(
        shards, groups, float(groups * shards * ROWS) ** (-0.5), taps_grad, tapss_grad, heads, borrowed, borroweds,
        end, ends, keep,
    )
    whole_grad = jnp.concatenate(
        [jnp.concatenate([grad[: ROWS - 16], grads[: ROWS - 16]], axis=1), last], axis=0
    )
    return (out, whole_grad, weight_grad, bias_grad[0], heads[0, :HEADS], heads[1, :HEADS], heads[2, :HEADS])


def solution(mesh):
    sharded = P(("dp", "seq"), None)
    return jax.shard_map(
        on_device,
        mesh=mesh,
        in_specs=(sharded, P(("dp", "seq")), P(), P(), sharded, P(), P(), P(), sharded),
        out_specs=(sharded, sharded, P(), P(), P(), P(), P()),
        check_vma=False,
    )
```

```python
import functools

import jax
import jax.numpy as jnp
from jax import lax
from jax.experimental import pallas as pl
from jax.experimental.pallas import tpu as pltpu
from jax.sharding import PartitionSpec as P

HEADS = 80
HEAD_DIM = 64
STATE = 128
CONV = 4
INNER = 5120
CH = 5376
ROWS = 128
TILE = 512
TILES = INNER // TILE
TILE_HEADS = TILE // HEAD_DIM
LANES = 128

F32 = jnp.float32
BF16 = jnp.bfloat16
EXACT = lax.Precision.HIGHEST
HALF_TILES = TILES // 2
VMEM_BYTES = 60 << 20
MESH = pl.DeviceIdType.MESH


def iota(shape, axis):
    return lax.broadcasted_iota(jnp.int32, shape, axis)


def halves(value):
    high = value.astype(BF16)
    return high, (value - high.astype(F32)).astype(BF16)


def mm(a, b):
    return lax.dot_general(a, b, (((1,), (0,)), ((), ())), preferred_element_type=F32)


def mm_nt(a, b):
    return lax.dot_general(a, b, (((1,), (1,)), ((), ())), preferred_element_type=F32)


def exact(a, b):
    return lax.dot_general(
        a, b, (((1,), (0,)), ((), ())), precision=EXACT, preferred_element_type=F32
    )


def spread_exact(rows, one_hot):
    first, rest = rows.astype(BF16), rows
    rest = rest - first.astype(F32)
    second, third = halves(rest)
    return mm(first, one_hot) + mm(second, one_hot) + mm(third, one_hot)


def interleave(group, late):
    row, col = iota((2 * STATE, STATE), 0), iota((2 * STATE, STATE), 1)
    place = row % (2 * group)
    first = group if late else 0
    here = (place >= first) & (place < first + group)
    return jnp.where(here & (col == group * (row // (2 * group)) + place - first), 1.0, 0.0)


def head_columns(tile):
    head, col = iota((LANES, TILE), 0), iota((LANES, TILE), 1)
    return jnp.where(head == TILE_HEADS * tile + col // HEAD_DIM, 1.0, 0.0).astype(BF16)


def spread_heads(both_ref, tile):
    one_hot = head_columns(tile)
    return mm(both_ref[...], jnp.concatenate([one_hot, one_hot], axis=0))


def convolve(tail, rows, taps, valid):
    extended = jnp.concatenate([tail, rows], axis=0)
    total = taps[4:5] + taps[3:4] * rows
    shifted = [rows]
    for back in range(1, CONV):
        moved = extended[8 - back : 8 - back + ROWS] * valid[:, back - 1 : back]
        shifted.append(moved)
        total = total + taps[3 - back : 4 - back] * moved
    return total, shifted


def sigmoid(v):
    return 1.0 / (1.0 + jnp.exp(-v))


def greet(axes):
    barrier = pltpu.get_barrier_semaphore()
    for axis, size in axes:
        place = lax.axis_index(axis)

        def signal(k, carry):
            pl.semaphore_signal(
                barrier, inc=1, device_id={axis: lax.rem(place + k, size)}, device_id_type=MESH
            )
            return carry

        lax.fori_loop(1, size, signal, 0)
    pl.semaphore_wait(barrier, sum(size - 1 for _, size in axes))


def remote(source, target, send, receive, axis, peer):
    return pltpu.make_async_remote_copy(
        src_ref=source, dst_ref=target, send_sem=send, recv_sem=receive, device_id={axis: peer}, device_id_type=MESH
    )


def send_all(axis, size, source, target, send, receive):
    place = lax.axis_index(axis)

    def start(k, carry):
        peer = lax.rem(place + k, size)
        remote(source(peer), target.at[place], send.at[peer], receive.at[place], axis, peer).start()
        return carry

    lax.fori_loop(1, size, start, 0)


def wait_all(axis, size, source, target, send, receive):
    place = lax.axis_index(axis)

    def wait(k, carry):
        peer = lax.rem(place + k, size)
        copy = remote(source(peer), target.at[peer], send.at[peer], receive.at[peer], axis, peer)
        copy.wait_send()
        copy.wait_recv()
        return carry

    lax.fori_loop(1, size, wait, 0)


def head_kernel(shards, raw_in_ref, small_ref, row_ref, end_ref, run_ref, runT_ref, dt_ref, dtT_ref, both_ref, sig_ref,
                sigsum_ref, through_ref, mask_ref, valid_ref, keep_ref, tail_ref, own_ref, raw, own, slots, tail_out, send,
                receive, tail_send, tail_receive):
    greet((("seq", shards),))
    place = lax.axis_index("seq")
    reset_row = row_ref[...].astype(F32)
    token, other = iota((ROWS, ROWS), 0), iota((ROWS, ROWS), 1)
    reset_col = jnp.sum(jnp.where(token == other, reset_row, 0.0), axis=1, keepdims=True)
    low, high = token >= other, token <= other
    segment_col = jnp.sum(jnp.where(low, reset_row, 0.0), axis=1, keepdims=True)
    segment_row = jnp.sum(jnp.where(high, reset_col, 0.0), axis=0, keepdims=True)
    mask_ref[0] = jnp.where(low & (segment_col == segment_row), 1.0, 0.0)
    mask_ref[1] = jnp.where(high & (segment_col == segment_row), 1.0, 0.0)

    kept = jnp.broadcast_to(1.0 - reset_col, (ROWS, LANES))
    one_back = jnp.where(token < 1, 1.0, pltpu.roll(kept, 1, 0))
    two_back = jnp.where(token < 2, 1.0, pltpu.roll(kept, 2, 0))
    valid = jnp.where(other == 0, kept, jnp.where(other == 1, kept * one_back, kept * one_back * two_back))
    valid_ref[...] = valid[:, :8]
    one_on, two_on = pltpu.roll(kept, ROWS - 1, 0), pltpu.roll(kept, ROWS - 2, 0)
    keep = jnp.where(
        token == ROWS - 1, 1.0, jnp.where(token == ROWS - 2, one_on, jnp.where(token == ROWS - 3, one_on * two_on, 0.0))
    )[ROWS - 8 :]
    keep_ref[...] = keep
    tail_out[...] = (end_ref[8:, :].astype(F32) * keep[:, 0:1]).astype(BF16)
    onward = remote(tail_out, tail_ref, tail_send, tail_receive, "seq", lax.rem(place + 1, shards))

    @pl.when(place < shards - 1)
    def _():
        onward.start()

    raw[...] = jnp.zeros_like(raw)
    raw[:HEADS, :] = raw_in_ref[...]
    biased = raw[...].T + small_ref[0:1, :]
    dt = jnp.maximum(biased, 0.0) + jnp.log1p(jnp.exp(-jnp.abs(biased)))
    decay = -jnp.exp(small_ref[1:2, :]) * dt
    lower = jnp.where(low, 1.0, 0.0)
    running = exact(lower, decay)
    last = running[ROWS - 1 : ROWS]
    count = segment_col[ROWS - 1 : ROWS]
    untouched = jnp.where(segment_col == 0.0, 1.0, 0.0)
    entry = jnp.exp(running) * untouched
    own[...] = jnp.broadcast_to(entry[ROWS - 1 : ROWS], own.shape)
    own_ref[...] = own[...]
    send_all("seq", shards, lambda peer: own, slots, send, receive)
    sig = sigmoid(biased)
    sig_ref[...] = sig
    sigsum_ref[...] = exact(lower, sig)
    run_ref[...] = running
    runT_ref[...] = running.T
    dt_ref[...] = dt
    dtT_ref[...] = dt.T
    leave = jnp.exp(last - running) * jnp.where(segment_col == count, 1.0, 0.0) * dt
    for at, part in ((0, leave), (ROWS, entry)):
        first, second = halves(part)
        both_ref[at : at + ROWS, :LANES] = first
        both_ref[at : at + ROWS, LANES:] = second
    slots[place] = own[...]
    wait_all("seq", shards, lambda peer: own, slots, send, receive)
    for shard in range(shards):
        through_ref[shard : shard + 1, :] = slots[shard, 0:1, :]

    @pl.when(place < shards - 1)
    def _():
        onward.wait_send()

    @pl.when(place > 0)
    def _():
        onward.wait_recv()

    @pl.when(place == 0)
    def _():
        tail_ref[...] = jnp.zeros_like(tail_ref)


def head_stage(shards, raw, small, row, end):
    square = jax.ShapeDtypeStruct((ROWS, LANES), F32)
    shapes = (
        square, square, square, square,
        jax.ShapeDtypeStruct((2 * ROWS, 2 * LANES), BF16),
        square, square,
        jax.ShapeDtypeStruct((shards, LANES), F32),
        jax.ShapeDtypeStruct((2, ROWS, ROWS), F32),
        jax.ShapeDtypeStruct((ROWS, 8), F32),
        jax.ShapeDtypeStruct((8, LANES), F32),
        jax.ShapeDtypeStruct((8, CH), BF16),
        jax.ShapeDtypeStruct((8, LANES), F32),
    )
    in_vmem = pl.BlockSpec(memory_space=pltpu.VMEM)
    return pl.pallas_call(
        functools.partial(head_kernel, shards),
        in_specs=[in_vmem] * 4,
        out_specs=[in_vmem] * len(shapes),
        out_shape=shapes,
        scratch_shapes=[
            pltpu.VMEM((ROWS, LANES), F32), pltpu.VMEM((8, LANES), F32), pltpu.VMEM((shards, 8, LANES), F32),
            pltpu.VMEM((8, CH), BF16), pltpu.SemaphoreType.DMA((shards,)), pltpu.SemaphoreType.DMA((shards,)),
            pltpu.SemaphoreType.DMA, pltpu.SemaphoreType.DMA,
        ],
        compiler_params=pltpu.CompilerParams(
            vmem_limit_bytes=VMEM_BYTES, collective_id=0, has_side_effects=True
        ),
        name="heads",
    )(raw, small, row, end)


def whole(shape):
    return pl.BlockSpec(shape, lambda *at: (0,) * len(shape))


def call(kernel, name, half, grid, in_specs, out_specs, out_shape, scratch_shapes, operands, aliases={}):
    return pl.pallas_call(
        kernel,
        grid_spec=pltpu.PrefetchScalarGridSpec(
            num_scalar_prefetch=1, grid=(grid,), in_specs=in_specs, out_specs=out_specs, scratch_shapes=scratch_shapes
        ),
        out_shape=out_shape,
        input_output_aliases=aliases,
        compiler_params=pltpu.CompilerParams(vmem_limit_bytes=VMEM_BYTES),
        name=name,
    )(half, *operands)


def tile_at(i, half):
    return lax.rem(i + HALF_TILES * half[0], TILES)


def tile_spec(rows):
    return pl.BlockSpec((rows, TILE), lambda i, half: (0, tile_at(i, half)))


def small_spec(rows):
    return pl.BlockSpec((rows, 2 * STATE), lambda *at: (0, INNER // (2 * STATE)))


def pair_spec(shape, first):
    if first:
        return pl.BlockSpec(shape[:2] + (TILE,), lambda i, half: (0, 0, jnp.minimum(i, HALF_TILES - 1)))
    return pl.BlockSpec(shape[:2] + (TILE,), lambda i, half: (0, 0, jnp.maximum(i - HALF_TILES, 0)))


def local_kernel(group, half_ref, x_ref, tail_ref, taps_ref, xs_ref, tails_ref, tapss_ref, valid_ref, cot_ref,
                 both_ref, pair_ref, bc_ref, lhs_hi, lhs_lo):
    valid = valid_ref[...]

    @pl.when(pl.program_id(0) == 0)
    def _():
        total, _ = convolve(tails_ref[...].astype(F32), xs_ref[...].astype(F32), tapss_ref[...], valid)
        small = total * sigmoid(total)
        bc_ref[...] = small
        for at, late in ((0, False), (STATE, True)):
            pick = interleave(group, late).astype(BF16)
            first, second = halves(small[:, at : at + STATE])
            lhs_hi[:, at : at + ROWS] = mm_nt(pick, first).astype(BF16)
            lhs_lo[:, at : at + ROWS] = mm_nt(pick, second).astype(BF16)

    total, _ = convolve(tail_ref[...].astype(F32), x_ref[...].astype(F32), taps_ref[...], valid)
    act = total * sigmoid(total)
    weight = spread_heads(both_ref, tile_at(pl.program_id(0), half_ref))
    first, second = halves(weight * jnp.concatenate([act, cot_ref[...].astype(F32)], axis=0))
    result = mm(lhs_hi[...], first) + mm(lhs_hi[...], second) + mm(lhs_lo[...], first)
    pair_ref[...] = result.reshape(pair_ref.shape)


def local_stage(group, half, conv_input, tail, taps, valid, cotangent, both):
    shape = (STATE // group, 2 * group, INNER // 2)
    return call(
        functools.partial(local_kernel, group), "local", half, HALF_TILES,
        [
            tile_spec(ROWS), tile_spec(8), tile_spec(8),
            small_spec(ROWS), small_spec(8), small_spec(8),
            whole((ROWS, 8)), tile_spec(ROWS), whole((2 * ROWS, 2 * LANES)),
        ],
        [pair_spec(shape, True), whole((ROWS, 2 * STATE))],
        (jax.ShapeDtypeStruct(shape, F32), jax.ShapeDtypeStruct((ROWS, 2 * STATE), F32)),
        [pltpu.VMEM((2 * STATE, 2 * ROWS), BF16)] * 2,
        (conv_input, tail, taps, conv_input, tail, taps, valid, cotangent, both),
    )


def within_kernel(half_ref, x_ref, tail_ref, taps_ref, valid_ref, cot_ref, bc_ref, run_ref, runT_ref, dt_ref, dtT_ref,
                  mask_ref, out_ref, grad_ref, score_grad_ref, score, scoreT):
    tile = pl.program_id(0)

    @pl.when(tile == 0)
    def _():
        keys, reads = bc_ref[:, :STATE], bc_ref[:, STATE:]
        keys_hi, keys_lo = halves(keys)
        reads_hi, reads_lo = halves(reads)
        score[...] = mask_ref[0] * (mm_nt(reads_hi, keys_hi) + mm_nt(reads_hi, keys_lo) + mm_nt(reads_lo, keys_hi))
        scoreT[...] = mask_ref[1] * (mm_nt(keys_hi, reads_hi) + mm_nt(keys_hi, reads_lo) + mm_nt(keys_lo, reads_hi))
        score_grad_ref[...] = jnp.zeros_like(score_grad_ref)

    total, _ = convolve(tail_ref[...].astype(F32), x_ref[...].astype(F32), taps_ref[...], valid_ref[...])
    act = total * sigmoid(total)
    turn = lax.rem(LANES - TILE_HEADS * tile_at(tile, half_ref), LANES)
    run = pltpu.roll(run_ref[...], turn, 1)
    dt = pltpu.roll(dt_ref[...], turn, 1)
    left = iota((ROWS, LANES), 1) < HEAD_DIM
    left = jnp.where(left, 1.0, 0.0).astype(BF16)
    right = 1.0 - left
    score_grad = score_grad_ref[...]
    for pair in range(TILE_HEADS // 2):
        lanes = slice(LANES * pair, LANES * (pair + 1))
        spread, weights, weightsT = [], [], []
        for head in (2 * pair, 2 * pair + 1):
            run_col, run_row = run[:, head : head + 1], runT_ref[head : head + 1, :]
            difference = run_col - run_row
            step = jnp.exp(jnp.minimum(difference, 0.0)) * dtT_ref[head : head + 1, :]
            spread.append(step)
            weights.append(step * score[...])
            weightsT.append(jnp.exp(jnp.minimum(-difference, 0.0)) * dt[:, head : head + 1] * scoreT[...])
        x_hi, x_lo = halves(act[:, lanes])
        upstream = cot_ref[:, lanes]
        x_hi2 = jnp.concatenate([x_hi * left, x_hi * right], axis=0)
        x_lo2 = jnp.concatenate([x_lo * left, x_lo * right], axis=0)
        upstream2 = jnp.concatenate([upstream * left, upstream * right], axis=0)
        w_hi, w_lo = halves(jnp.concatenate(weights, axis=1))
        wide = mm(w_hi, jnp.concatenate([x_hi2, x_lo2], axis=1))
        out_ref[:, lanes] = wide[:, :LANES] + wide[:, LANES:] + mm(w_lo, x_hi2)
        wt_hi, wt_lo = halves(jnp.concatenate(weightsT, axis=1))
        grad_ref[:, lanes] = mm(wt_hi, upstream2) + mm(wt_lo, upstream2)
        inner = mm_nt(upstream2, jnp.concatenate([x_hi, x_lo], axis=0))
        inner = inner[:, :ROWS] + inner[:, ROWS:]
        score_grad = score_grad + inner[:ROWS] * spread[0] + inner[ROWS:] * spread[1]
    score_grad_ref[...] = score_grad

    @pl.when(tile == TILES - 1)
    def _():
        score_grad_ref[...] = score_grad_ref[...] * mask_ref[0]


def within_stage(half, conv_input, tail, taps, valid, cotangent, bc, run, runT, dt, dtT, mask):
    square = whole((ROWS, LANES))
    rows = pl.BlockSpec((TILE_HEADS, LANES), lambda i, half: (tile_at(i, half), 0))
    wide = jax.ShapeDtypeStruct((ROWS, INNER), F32)
    return call(
        within_kernel, "within", half, TILES,
        [
            tile_spec(ROWS), tile_spec(8), tile_spec(8), whole((ROWS, 8)), tile_spec(ROWS),
            whole((ROWS, 2 * STATE)), square, rows, square, rows, whole((2, ROWS, ROWS)),
        ],
        [tile_spec(ROWS), tile_spec(ROWS), whole((ROWS, ROWS))],
        (wide, wide, jax.ShapeDtypeStruct((ROWS, ROWS), F32)),
        [pltpu.VMEM((ROWS, ROWS), F32)] * 2,
        (conv_input, tail, taps, valid, cotangent, bc, run, runT, dt, dtT, mask),
    )


def chip_decay(half_ref, through_ref, rows):
    return spread_exact(through_ref[rows, :], head_columns(tile_at(pl.program_id(0), half_ref)))


def own_pair(half_ref):
    return pl.ds(pl.multiple_of(8 * (half_ref[1] // 4), 8), 8)


def even_odd(half_ref, through_ref):
    chips = chip_decay(half_ref, through_ref, own_pair(half_ref))
    place = lax.rem(half_ref[1], 4)
    row = iota(chips.shape, 0)
    earlier = jnp.sum(jnp.where(row == 2 * place, chips, 0.0), axis=0, keepdims=True)
    later = jnp.sum(jnp.where(row == 2 * place + 1, chips, 0.0), axis=0, keepdims=True)
    return earlier[None], later[None]


def join_kernel(group, half_ref, mine_ref, other_ref, through_ref, out_ref):
    earlier, later = even_odd(half_ref, through_ref)
    even = half_ref[2] == 0
    mine, other = mine_ref[...], other_ref[...]
    first, second = jnp.where(even, mine, other), jnp.where(even, other, mine)
    out_ref[:, :group, :] = later * first[:, :group] + second[:, :group]
    out_ref[:, group:, :] = first[:, group:] + earlier * second[:, group:]


def join_stage(group, half, mine, other, through):
    spec = pair_spec(mine.shape, True)
    return call(
        functools.partial(join_kernel, group), "join", half, HALF_TILES,
        [spec, spec, whole(through.shape)], spec, jax.ShapeDtypeStruct(mine.shape, F32), [], (mine, other, through),
    )


def carry_kernel(group, half_ref, pair_ref, through_ref, out_ref, decay):
    chips = pair_ref.shape[0]
    decay[...] = chip_decay(half_ref, through_ref, slice(None))
    state = jnp.zeros((group, TILE), F32)
    for chip in range(chips):
        out_ref[chip, :group, :] = state
        state = decay[2 * chip : 2 * chip + 1, :] * decay[2 * chip + 1 : 2 * chip + 2, :] * state
        state = state + pair_ref[chip, :group, :]
    state = jnp.zeros((group, TILE), F32)
    for chip in reversed(range(chips)):
        out_ref[chip, group:, :] = state
        state = decay[2 * chip : 2 * chip + 1, :] * decay[2 * chip + 1 : 2 * chip + 2, :] * state
        state = state + pair_ref[chip, group:, :]


def carry_stage(group, half, pairs, through):
    spec = pair_spec(pairs.shape, True)
    return call(
        functools.partial(carry_kernel, group), "carry", half, HALF_TILES,
        [spec, whole(through.shape)], spec, jax.ShapeDtypeStruct(pairs.shape, F32),
        [pltpu.VMEM((through.shape[0], TILE), F32)], (pairs, through),
    )


def conv_backward(grad, shifted, taps, valid):
    width = grad.shape[1]
    zeros = jnp.zeros((8, width), F32)
    total = jnp.concatenate([zeros, grad * taps[3:4]], axis=0)
    parts = [jnp.sum(grad * shifted[0], axis=0, keepdims=True)]
    for back in range(1, CONV):
        parts.insert(0, jnp.sum(grad * shifted[back], axis=0, keepdims=True))
        moved = jnp.concatenate([zeros, grad * valid[:, back - 1 : back] * taps[3 - back : 4 - back], zeros], axis=0)
        total = total + moved[back : back + ROWS + 8]
    parts.append(jnp.sum(grad, axis=0, keepdims=True))
    parts.append(jnp.zeros((3, width), F32))
    return total, jnp.concatenate(parts, axis=0)


def finish_kernel(group, final, half_ref, x_ref, tail_ref, taps_ref, xs_ref, tails_ref, tapss_ref, valid_ref, cot_ref, both_ref,
                  out_in_ref, grad_in_ref, chip_ref, partner_ref, bc_ref, small_ref, through_ref, *refs):
    if final:
        score_grad_ref, run_ref, dt_ref, sig_ref, sigsum_ref, own_ref = refs[:6]
        bc_before, head_before, token_before = refs[6:9]
        out_ref, grad_ref, end_ref, borrowed_ref, taps_grad_ref = refs[14:19]
        grads_ref, ends_ref, borroweds_ref, tapss_grad_ref, heads_ref = refs[19:24]
        lhs_hi, lhs_lo, bc_grad, by_head, by_token = refs[24:]
    else:
        out_ref, grad_ref, end_ref, borrowed_ref, taps_grad_ref, bc_grad, by_head, by_token, lhs_hi, lhs_lo = refs
    tile = pl.program_id(0)
    valid = valid_ref[...]

    @pl.when(tile == 0)
    def _():
        for at, source, late in ((0, STATE, False), (ROWS, 0, True)):
            pick = interleave(group, late).astype(BF16)
            first, second = halves(bc_ref[:, source : source + STATE])
            lhs_hi[at : at + ROWS, :] = mm_nt(first, pick).astype(BF16)
            lhs_lo[at : at + ROWS, :] = mm_nt(second, pick).astype(BF16)
        if final:
            bc_grad[...] = bc_before[...]
            by_head[...] = head_before[...]
            by_token[...] = token_before[...]
        else:
            bc_grad[...] = jnp.zeros_like(bc_grad)
            by_head[...] = jnp.zeros_like(by_head)
            by_token[...] = jnp.zeros_like(by_token)

    total, shifted = convolve(tail_ref[...].astype(F32), x_ref[...].astype(F32), taps_ref[...], valid)
    gate = sigmoid(total)
    act = total * gate
    upstream = cot_ref[...].astype(F32)
    here = tile_at(tile, half_ref)
    weight = spread_heads(both_ref, here)
    leave, entry = weight[:ROWS], weight[ROWS:]
    earlier, later = even_odd(half_ref, through_ref)
    even = half_ref[2] == 0
    weight_state, weight_adjoint = jnp.where(even, 1.0, earlier), jnp.where(even, later, 1.0)
    with_state, with_adjoint = jnp.where(even, 0.0, 1.0), jnp.where(even, 1.0, 0.0)
    states = jnp.concatenate(
        [
            weight_state * chip_ref[:, :group, :] + with_state * partner_ref[:, :group, :],
            weight_adjoint * chip_ref[:, group:, :] + with_adjoint * partner_ref[:, group:, :],
        ],
        axis=1,
    ).reshape(2 * STATE, TILE)
    states_hi, states_lo = halves(states)
    read = mm(lhs_hi[...], states_hi) + mm(lhs_hi[...], states_lo) + mm(lhs_lo[...], states_hi)
    one_hot = head_columns(here)
    gain = spread_exact(small_ref[...], one_hot)[2:3]
    through_state = out_in_ref[...] + entry * read[:ROWS]
    out_ref[...] = (through_state + gain * act).astype(BF16)
    act_grad_late = leave * read[ROWS:]
    act_grad = grad_in_ref[...] + act_grad_late

    first, second = halves(jnp.concatenate([entry * upstream, leave * act], axis=0))
    bc_grad[...] += mm_nt(first, states_hi) + mm_nt(first, states_lo) + mm_nt(second, states_hi)

    first, second = halves(jnp.concatenate([upstream * through_state, act * act_grad], axis=0))
    by_token[...] += mm_nt(first, one_hot) + mm_nt(second, one_hot)
    crossed = states * pltpu.roll(states, group, 0)
    crossed = jnp.where(iota((2 * STATE, TILE), 0) % (2 * group) >= group, crossed, 0.0)
    sums = jnp.concatenate(
        [
            jnp.sum(act * act_grad_late, axis=0, keepdims=True),
            jnp.sum(crossed, axis=0, keepdims=True),
            jnp.sum(upstream * act, axis=0, keepdims=True),
            jnp.zeros((5, TILE), F32),
        ],
        axis=0,
    )
    by_head[...] += lax.dot_general(
        sums, one_hot.astype(F32), (((1,), (1,)), ((), ())), precision=EXACT, preferred_element_type=F32
    )

    act_grad = act_grad + gain * upstream
    conv_grad = act_grad * (gate + act * (1.0 - gate))
    full, taps_grad_ref[...] = conv_backward(conv_grad, shifted, taps_ref[...], valid)
    borrowed_ref[...] = full[:8]
    grad_ref[...] = full[8:].astype(BF16)
    end_ref[...] = full[ROWS - 8 :]

    if not final:
        return

    @pl.when(tile == HALF_TILES - 1)
    def _():
        score_grad = score_grad_ref[...]
        keys, reads = bc_ref[:, :STATE], bc_ref[:, STATE:]
        reads_grad = exact(bc_grad[:ROWS], interleave(group, False)) + exact(score_grad, keys)
        keys_grad = exact(bc_grad[ROWS:], interleave(group, True)) + exact(score_grad.T, reads)
        total, shifted = convolve(tails_ref[...].astype(F32), xs_ref[...].astype(F32), tapss_ref[...], valid)
        gate = sigmoid(total)
        small_grad = jnp.concatenate([keys_grad, reads_grad], axis=1) * (gate + total * gate * (1.0 - gate))
        full, tapss_grad_ref[...] = conv_backward(small_grad, shifted, tapss_ref[...], valid)
        borroweds_ref[...] = full[:8]
        grads_ref[...] = full[8:].astype(BF16)
        ends_ref[...] = full[ROWS - 8 :]

        read_sum, added_sum = by_token[:ROWS], by_token[ROWS:]
        at_end = by_head[0:1, :] + own_ref[0:1, :] * by_head[1:2, :]
        run_grad = read_sum - added_sum + jnp.where(iota((ROWS, LANES), 0) == ROWS - 1, at_end, 0.0)
        alog_grad = jnp.sum(run_grad * run_ref[...], axis=0, keepdims=True)
        bias_grad = jnp.sum(added_sum / dt_ref[...] * sig_ref[...], axis=0, keepdims=True)
        rate = jnp.exp(small_ref[1:2, :])
        bias_grad = bias_grad - rate * jnp.sum(run_grad * sigsum_ref[...], axis=0, keepdims=True)
        heads_ref[...] = jnp.concatenate([bias_grad, alog_grad, by_head[2:3, :], jnp.zeros((5, LANES), F32)], axis=0)


def finish_stage(group, half, operands, chip, partner, bc, small, through, last=None, before=None):
    final = last is not None
    square = whole((ROWS, LANES))
    wide = (
        jax.ShapeDtypeStruct((ROWS, INNER), BF16),
        jax.ShapeDtypeStruct((ROWS, INNER), BF16),
        jax.ShapeDtypeStruct((16, INNER), F32),
        jax.ShapeDtypeStruct((8, INNER), F32),
        jax.ShapeDtypeStruct((8, INNER), F32),
    )
    sums = (
        jax.ShapeDtypeStruct((2 * ROWS, 2 * STATE), F32),
        jax.ShapeDtypeStruct((8, LANES), F32),
        jax.ShapeDtypeStruct((2 * ROWS, LANES), F32),
    )
    ends = (
        jax.ShapeDtypeStruct((ROWS, 2 * STATE), BF16),
        jax.ShapeDtypeStruct((16, 2 * STATE), F32),
        jax.ShapeDtypeStruct((8, 2 * STATE), F32),
        jax.ShapeDtypeStruct((8, 2 * STATE), F32),
        jax.ShapeDtypeStruct((8, LANES), F32),
    )
    in_specs = [
        tile_spec(ROWS), tile_spec(8), tile_spec(8),
        small_spec(ROWS), small_spec(8), small_spec(8),
        whole((ROWS, 8)), tile_spec(ROWS), whole((2 * ROWS, 2 * LANES)),
        tile_spec(ROWS), tile_spec(ROWS), pair_spec(chip.shape, True), pair_spec(partner.shape, True),
        whole((ROWS, 2 * STATE)), whole((8, LANES)), whole(through.shape),
    ]
    given = tuple(operands) + (chip, partner, bc, small, through)
    lhs = [pltpu.VMEM((2 * ROWS, 2 * STATE), BF16)] * 2
    aliases = {}
    if final:
        in_specs += [whole((ROWS, ROWS)), square, square, square, square, whole((8, LANES))]
        in_specs += [whole(part.shape) for part in sums] + [pl.BlockSpec(memory_space=pl.ANY)] * len(wide)
        aliases = {1 + len(given) + len(last) + len(sums) + at: at for at in range(len(wide))}
        given += tuple(last) + tuple(before[len(wide):]) + tuple(before[: len(wide)])
        rest, scratch = ends, lhs + [pltpu.VMEM(part.shape, F32) for part in sums]
    else:
        rest, scratch = sums, lhs
    return call(
        functools.partial(finish_kernel, group, final), "finish_second" if final else "finish_first", half, HALF_TILES,
        in_specs, [tile_spec(part.shape[0]) for part in wide] + [whole(part.shape) for part in rest], wide + rest,
        scratch, given, aliases,
    )


def total_kernel(shards, groups, scale, taps_ref, small_ref, heads_ref, borrowed_ref, borroweds_ref, end_ref, ends_ref,
                 keep_ref, weight_ref, bias_ref, heads_out_ref, last_ref,
                 parts, slots, piece, dp_slots, result, got, got_small, send, receive, dp_send, dp_receive, back_send,
                 back_receive, rows_send, rows_receive):
    greet((("seq", shards), ("dp", groups)))
    place, group = lax.axis_index("seq"), lax.axis_index("dp")
    before = lax.rem(place + shards - 1, shards)
    returns = [
        remote(borrowed_ref, got, rows_send.at[0], rows_receive.at[0], "seq", before),
        remote(borroweds_ref, got_small, rows_send.at[1], rows_receive.at[1], "seq", before),
    ]
    wide = CH // LANES
    parts[...] = jnp.zeros_like(parts)
    for at in range(wide + 1):
        if at < INNER // LANES:
            block = taps_ref[:, LANES * at : LANES * (at + 1)]
        elif at < wide:
            block = small_ref[:, LANES * at - INNER : LANES * (at + 1) - INNER]
        else:
            block = heads_ref[...]
        parts[at % shards, 8 * (at // shards) : 8 * (at // shards) + 8, :] = block
    send_all("seq", shards, lambda peer: parts.at[peer], slots, send, receive)

    @pl.when(place > 0)
    def _():
        for copy in returns:
            copy.start()

    slots[place] = parts[place]
    wait_all("seq", shards, lambda peer: parts.at[peer], slots, send, receive)
    piece[...] = jnp.sum(slots[...], axis=0)
    send_all("dp", groups, lambda peer: piece, dp_slots, dp_send, dp_receive)
    dp_slots[group] = piece[...]
    wait_all("dp", groups, lambda peer: piece, dp_slots, dp_send, dp_receive)
    piece[...] = jnp.sum(dp_slots[...], axis=0) * scale
    send_all("seq", shards, lambda peer: piece, result, back_send, back_receive)
    result[place] = piece[...]

    @pl.when(place > 0)
    def _():
        for copy in returns:
            copy.wait_send()

    rows = 8 - CONV + 1

    @pl.when(place < shards - 1)
    def _():
        for copy in returns:
            copy.wait_recv()
        keep = keep_ref[:, 0:1]
        for lanes, source, end in ((slice(0, INNER), got, end_ref), (slice(INNER, CH), got_small, ends_ref)):
            last_ref[:8, lanes] = end[:8, :].astype(BF16)
            late = iota(source.shape, 0) >= rows
            last_ref[8:, lanes] = (end[8:, :] + jnp.where(late, source[...] * keep, 0.0)).astype(BF16)

    @pl.when(place == shards - 1)
    def _():
        last_ref[:, :INNER] = end_ref[...].astype(BF16)
        last_ref[:, INNER:] = ends_ref[...].astype(BF16)

    wait_all("seq", shards, lambda peer: piece, result, back_send, back_receive)
    for at in range(wide + 1):
        block = result[at % shards, 8 * (at // shards) : 8 * (at // shards) + 8, :]
        if at < wide:
            weight_ref[:, LANES * at : LANES * (at + 1)] = block[:CONV]
            bias_ref[:, LANES * at : LANES * (at + 1)] = block[CONV : CONV + 1]
        else:
            heads_out_ref[...] = block


def total_stage(shards, groups, scale, *operands):
    depth = 8 * pl.cdiv(CH // LANES + 1, shards)
    in_vmem = pl.BlockSpec(memory_space=pltpu.VMEM)
    shapes = (
        jax.ShapeDtypeStruct((CONV, CH), F32),
        jax.ShapeDtypeStruct((1, CH), F32),
        jax.ShapeDtypeStruct((8, LANES), F32),
        jax.ShapeDtypeStruct((16, CH), BF16),
    )
    dma = pltpu.SemaphoreType.DMA
    return pl.pallas_call(
        functools.partial(total_kernel, shards, groups, scale),
        in_specs=[in_vmem] * len(operands),
        out_specs=[in_vmem] * len(shapes),
        out_shape=shapes,
        scratch_shapes=[
            pltpu.VMEM((shards, depth, LANES), F32), pltpu.VMEM((shards, depth, LANES), F32),
            pltpu.VMEM((depth, LANES), F32), pltpu.VMEM((groups, depth, LANES), F32),
            pltpu.VMEM((shards, depth, LANES), F32),
            pltpu.VMEM((8, INNER), F32), pltpu.VMEM((8, 2 * STATE), F32),
            dma((shards,)), dma((shards,)), dma((groups,)), dma((groups,)), dma((shards,)), dma((shards,)),
            dma((2,)), dma((2,)),
        ],
        compiler_params=pltpu.CompilerParams(
            vmem_limit_bytes=VMEM_BYTES, collective_id=1, has_side_effects=True
        ),
        name="totals",
    )(*operands)


def swap(array):
    return lax.ppermute(array, "seq", [(i, i ^ 1) for i in range(lax.axis_size("seq"))])


def between_chips(array):
    size = lax.axis_size("seq")
    groups = [list(range(0, size, 2)), list(range(1, size, 2))]
    return lax.all_to_all(array, "seq", 0, 0, axis_index_groups=groups, tiled=True)


def on_device(conv_input, doc_start, conv_weight, conv_bias, dt_raw, dt_bias, a_log, skip_gain, cotangent):
    shards, place = lax.axis_size("seq"), lax.axis_index("seq")
    group = 2 * STATE // shards
    core = lax.rem(place, 2)
    half = jnp.stack([core, place // 2, core])
    other_half = jnp.stack([1 - core, place // 2, core])
    taps = jnp.concatenate([conv_weight, conv_bias[None], jnp.zeros((3, CH), F32)], axis=0)
    small = jnp.pad(jnp.stack([dt_bias, a_log, skip_gain]), ((0, 5), (0, LANES - HEADS)))

    run, runT, dt, dtT, both, sig, sigsum, all_through, mask, valid, keep, tail, through = head_stage(
        shards, dt_raw.T, small, doc_start[None], conv_input[ROWS - 16 :]
    )
    theirs, bc = local_stage(group, other_half, conv_input, tail, taps, valid, cotangent, both)
    other = swap(theirs)
    mine, _ = local_stage(group, half, conv_input, tail, taps, valid, cotangent, both)
    other_second = swap(mine)
    gathered = between_chips(join_stage(group, half, mine, other, all_through))
    out_in, grad_in, score_grad = within_stage(
        half, conv_input, tail, taps, valid, cotangent, bc, run, runT, dt, dtT, mask
    )
    gathered, out_in, grad_in = lax.optimization_barrier((gathered, out_in, grad_in))
    chip = between_chips(carry_stage(group, half, gathered, all_through))
    chip_second = swap(chip)
    operands = (conv_input, tail, taps, conv_input, tail, taps, valid, cotangent, both, out_in, grad_in)
    first = finish_stage(group, half, operands, chip, other, bc, small, all_through)
    out, grad, end, borrowed, taps_grad, grads, ends, borroweds, tapss_grad, heads = finish_stage(
        group, other_half, operands, chip_second, other_second, bc, small, all_through,
        (score_grad, run, dt, sig, sigsum, through), first,
    )
    groups = lax.axis_size("dp")
    weight_grad, bias_grad, heads, last = total_stage(
        shards, groups, float(groups * shards * ROWS) ** (-0.5), taps_grad, tapss_grad, heads, borrowed, borroweds,
        end, ends, keep,
    )
    whole_grad = jnp.concatenate(
        [jnp.concatenate([grad[: ROWS - 16], grads[: ROWS - 16]], axis=1), last], axis=0
    )
    return (out, whole_grad, weight_grad, bias_grad[0], heads[0, :HEADS], heads[1, :HEADS], heads[2, :HEADS])


def solution(mesh):
    sharded = P(("dp", "seq"), None)
    return jax.shard_map(
        on_device,
        mesh=mesh,
        in_specs=(sharded, P(("dp", "seq")), P(), P(), sharded, P(), P(), P(), sharded),
        out_specs=(sharded, sharded, P(), P(), P(), P(), P()),
        check_vma=False,
    )
```

```python
import functools

import jax
import jax.numpy as jnp
from jax import lax
from jax.experimental import pallas as pl
from jax.experimental.pallas import tpu as pltpu
from jax.sharding import PartitionSpec as P

HEADS = 80
HEAD_DIM = 64
STATE = 128
CONV = 4
INNER = 5120
CH = 5376
ROWS = 128
TILE = 512
TILES = INNER // TILE
TILE_HEADS = TILE // HEAD_DIM
LANES = 128

F32 = jnp.float32
BF16 = jnp.bfloat16
EXACT = lax.Precision.HIGHEST
HALF_TILES = TILES // 2
VMEM_BYTES = 60 << 20
MESH = pl.DeviceIdType.MESH


def iota(shape, axis):
    return lax.broadcasted_iota(jnp.int32, shape, axis)


def halves(value):
    high = value.astype(BF16)
    return high, (value - high.astype(F32)).astype(BF16)


def mm(a, b):
    return lax.dot_general(a, b, (((1,), (0,)), ((), ())), preferred_element_type=F32)


def mm_nt(a, b):
    return lax.dot_general(a, b, (((1,), (1,)), ((), ())), preferred_element_type=F32)


def exact(a, b):
    return lax.dot_general(
        a, b, (((1,), (0,)), ((), ())), precision=EXACT, preferred_element_type=F32
    )


def spread_exact(rows, one_hot):
    first, rest = rows.astype(BF16), rows
    rest = rest - first.astype(F32)
    second, third = halves(rest)
    return mm(first, one_hot) + mm(second, one_hot) + mm(third, one_hot)


def interleave(group, late):
    row, col = iota((2 * STATE, STATE), 0), iota((2 * STATE, STATE), 1)
    place = row % (2 * group)
    first = group if late else 0
    here = (place >= first) & (place < first + group)
    return jnp.where(here & (col == group * (row // (2 * group)) + place - first), 1.0, 0.0)


def head_columns(tile):
    head, col = iota((LANES, TILE), 0), iota((LANES, TILE), 1)
    return jnp.where(head == TILE_HEADS * tile + col // HEAD_DIM, 1.0, 0.0).astype(BF16)


def spread_heads(both_ref, tile):
    one_hot = head_columns(tile)
    return mm(both_ref[...], jnp.concatenate([one_hot, one_hot], axis=0))


def convolve(tail, rows, taps, valid):
    extended = jnp.concatenate([tail, rows], axis=0)
    total = taps[4:5] + taps[3:4] * rows
    shifted = [rows]
    for back in range(1, CONV):
        moved = extended[8 - back : 8 - back + ROWS] * valid[:, back - 1 : back]
        shifted.append(moved)
        total = total + taps[3 - back : 4 - back] * moved
    return total, shifted


def sigmoid(v):
    return 1.0 / (1.0 + jnp.exp(-v))


def near(k):
    place = lax.axis_index("seq")
    slot = lax.rem(lax.rem(place, 8) + k, 8)
    return (lax.axis_index("dp"), place - lax.rem(place, 8) + slot), slot


def far(k):
    place, group = lax.axis_index("seq"), lax.axis_index("dp")
    runs = lax.axis_size("seq") // 8
    slot = lax.rem(group * runs + place // 8 + k, lax.axis_size("dp") * runs)
    return (slot // runs, lax.rem(slot, runs) * 8 + lax.rem(place, 8)), slot


def send_all(peers, size, source, target, send, receive):
    _, own = peers(0)
    for k in range(1, size):
        peer, slot = peers(k)
        pltpu.make_async_remote_copy(
            src_ref=source(slot), dst_ref=target.at[own], send_sem=send.at[slot], recv_sem=receive.at[own],
            device_id=peer, device_id_type=MESH,
        ).start()


def wait_all(peers, size, source, target, send, receive):
    for k in range(1, size):
        peer, slot = peers(k)
        copy = pltpu.make_async_remote_copy(
            src_ref=source(slot), dst_ref=target.at[slot], send_sem=send.at[slot], recv_sem=receive.at[slot],
            device_id=peer, device_id_type=MESH,
        )
        copy.wait_send()
        copy.wait_recv()


def head_kernel(raw_in_ref, dt_bias_ref, a_log_ref, gain_ref, row_ref, weight_ref, bias_ref, end_ref, run_ref, runT_ref,
                dt_ref, dtT_ref, both_ref, sig_ref, sigsum_ref, mask_ref, valid_ref, keep_ref, tail_ref, own_ref,
                small_ref, taps_ref, raw):
    taps_ref[:CONV, :] = weight_ref[...]
    taps_ref[CONV:, :] = jnp.broadcast_to(bias_ref[...], (8 - CONV, CH))
    small_ref[...] = jnp.zeros_like(small_ref)
    for at, source in enumerate((dt_bias_ref, a_log_ref, gain_ref)):
        small_ref[at : at + 1, :HEADS] = source[...]
    reset_row = row_ref[...].astype(F32)
    token, other = iota((ROWS, ROWS), 0), iota((ROWS, ROWS), 1)
    reset_col = jnp.sum(jnp.where(token == other, reset_row, 0.0), axis=1, keepdims=True)
    low, high = token >= other, token <= other
    segment_col = jnp.sum(jnp.where(low, reset_row, 0.0), axis=1, keepdims=True)
    segment_row = jnp.sum(jnp.where(high, reset_col, 0.0), axis=0, keepdims=True)
    mask_ref[0] = jnp.where(low & (segment_col == segment_row), 1.0, 0.0)
    mask_ref[1] = jnp.where(high & (segment_col == segment_row), 1.0, 0.0)

    kept = jnp.broadcast_to(1.0 - reset_col, (ROWS, LANES))
    one_back = jnp.where(token < 1, 1.0, pltpu.roll(kept, 1, 0))
    two_back = jnp.where(token < 2, 1.0, pltpu.roll(kept, 2, 0))
    valid = jnp.where(other == 0, kept, jnp.where(other == 1, kept * one_back, kept * one_back * two_back))
    valid_ref[...] = valid[:, :8]
    one_on, two_on = pltpu.roll(kept, ROWS - 1, 0), pltpu.roll(kept, ROWS - 2, 0)
    keep = jnp.where(
        token == ROWS - 1, 1.0, jnp.where(token == ROWS - 2, one_on, jnp.where(token == ROWS - 3, one_on * two_on, 0.0))
    )[ROWS - 8 :]
    keep_ref[...] = keep
    tail_ref[...] = (end_ref[8:, :].astype(F32) * keep[:, 0:1]).astype(BF16)

    raw[...] = jnp.zeros_like(raw)
    raw[:HEADS, :] = raw_in_ref[...]
    biased = raw[...].T + small_ref[0:1, :]
    dt = jnp.maximum(biased, 0.0) + jnp.log1p(jnp.exp(-jnp.abs(biased)))
    decay = -jnp.exp(small_ref[1:2, :]) * dt
    lower = jnp.where(low, 1.0, 0.0)
    running = exact(lower, decay)
    last = running[ROWS - 1 : ROWS]
    count = segment_col[ROWS - 1 : ROWS]
    untouched = jnp.where(segment_col == 0.0, 1.0, 0.0)
    entry = jnp.exp(running) * untouched
    own_ref[...] = jnp.broadcast_to(entry[ROWS - 1 : ROWS], own_ref.shape)
    sig = sigmoid(biased)
    sig_ref[...] = sig
    sigsum_ref[...] = exact(lower, sig)
    run_ref[...] = running
    runT_ref[...] = running.T
    dt_ref[...] = dt
    dtT_ref[...] = dt.T
    leave = jnp.exp(last - running) * jnp.where(segment_col == count, 1.0, 0.0) * dt
    for at, part in ((0, leave), (ROWS, entry)):
        first, second = halves(part)
        both_ref[at : at + ROWS, :LANES] = first
        both_ref[at : at + ROWS, LANES:] = second


def head_stage(raw, dt_bias, a_log, gain, row, weight, bias, conv_input):
    square = jax.ShapeDtypeStruct((ROWS, LANES), F32)
    eight = jax.ShapeDtypeStruct((8, LANES), F32)
    shapes = (
        square, square, square, square,
        jax.ShapeDtypeStruct((2 * ROWS, 2 * LANES), BF16),
        square, square,
        jax.ShapeDtypeStruct((2, ROWS, ROWS), F32),
        jax.ShapeDtypeStruct((ROWS, 8), F32),
        eight,
        jax.ShapeDtypeStruct((8, CH), BF16),
        eight, eight,
        jax.ShapeDtypeStruct((8, CH), F32),
    )
    given = (raw, dt_bias, a_log, gain, row, weight, bias)
    return pl.pallas_call(
        head_kernel,
        grid=(1,),
        in_specs=[whole(part.shape) for part in given] + [pl.BlockSpec((16, CH), lambda *at: (ROWS // 16 - 1, 0))],
        out_specs=[whole(part.shape) for part in shapes],
        out_shape=shapes,
        scratch_shapes=[pltpu.VMEM((ROWS, LANES), F32)],
        compiler_params=pltpu.CompilerParams(vmem_limit_bytes=VMEM_BYTES),
        name="heads",
    )(*given, conv_input)


def whole(shape):
    return pl.BlockSpec(shape, lambda *at: (0,) * len(shape))


def call(kernel, name, half, grid, in_specs, out_specs, out_shape, scratch_shapes, operands, aliases={}):
    return pl.pallas_call(
        kernel,
        grid_spec=pltpu.PrefetchScalarGridSpec(
            num_scalar_prefetch=1, grid=(grid,), in_specs=in_specs, out_specs=out_specs, scratch_shapes=scratch_shapes
        ),
        out_shape=out_shape,
        input_output_aliases=aliases,
        compiler_params=pltpu.CompilerParams(vmem_limit_bytes=VMEM_BYTES),
        name=name,
    )(half, *operands)


def tile_at(i, half):
    return lax.rem(i + HALF_TILES * half[0], TILES)


def tile_spec(rows):
    return pl.BlockSpec((rows, TILE), lambda i, half: (0, tile_at(i, half)))


def small_spec(rows):
    return pl.BlockSpec((rows, 2 * STATE), lambda *at: (0, INNER // (2 * STATE)))


def pair_spec(shape, first):
    if first:
        return pl.BlockSpec(shape[:2] + (TILE,), lambda i, half: (0, 0, jnp.minimum(i, HALF_TILES - 1)))
    return pl.BlockSpec(shape[:2] + (TILE,), lambda i, half: (0, 0, jnp.maximum(i - HALF_TILES, 0)))


def local_kernel(group, half_ref, x_ref, tail_ref, taps_ref, xs_ref, tails_ref, tapss_ref, valid_ref, cot_ref,
                 both_ref, pair_ref, bc_ref, lhs_hi, lhs_lo):
    valid = valid_ref[...]

    @pl.when(pl.program_id(0) == 0)
    def _():
        total, _ = convolve(tails_ref[...].astype(F32), xs_ref[...].astype(F32), tapss_ref[...], valid)
        small = total * sigmoid(total)
        bc_ref[...] = small
        for at, late in ((0, False), (STATE, True)):
            pick = interleave(group, late).astype(BF16)
            first, second = halves(small[:, at : at + STATE])
            lhs_hi[:, at : at + ROWS] = mm_nt(pick, first).astype(BF16)
            lhs_lo[:, at : at + ROWS] = mm_nt(pick, second).astype(BF16)

    total, _ = convolve(tail_ref[...].astype(F32), x_ref[...].astype(F32), taps_ref[...], valid)
    act = total * sigmoid(total)
    weight = spread_heads(both_ref, tile_at(pl.program_id(0), half_ref))
    first, second = halves(weight * jnp.concatenate([act, cot_ref[...].astype(F32)], axis=0))
    result = mm(lhs_hi[...], first) + mm(lhs_hi[...], second) + mm(lhs_lo[...], first)
    pair_ref[...] = result.reshape(pair_ref.shape)


def local_stage(group, half, conv_input, tail, taps, valid, cotangent, both):
    shape = (STATE // group, 2 * group, INNER // 2)
    return call(
        functools.partial(local_kernel, group), "local", half, HALF_TILES,
        [
            tile_spec(ROWS), tile_spec(8), tile_spec(8),
            small_spec(ROWS), small_spec(8), small_spec(8),
            whole((ROWS, 8)), tile_spec(ROWS), whole((2 * ROWS, 2 * LANES)),
        ],
        [pair_spec(shape, True), whole((ROWS, 2 * STATE))],
        (jax.ShapeDtypeStruct(shape, F32), jax.ShapeDtypeStruct((ROWS, 2 * STATE), F32)),
        [pltpu.VMEM((2 * STATE, 2 * ROWS), BF16)] * 2,
        (conv_input, tail, taps, conv_input, tail, taps, valid, cotangent, both),
    )


def within_kernel(half_ref, x_ref, tail_ref, taps_ref, valid_ref, cot_ref, bc_ref, run_ref, runT_ref, dt_ref, dtT_ref,
                  mask_ref, out_ref, grad_ref, score_grad_ref, score, scoreT):
    tile = pl.program_id(0)

    @pl.when(tile == 0)
    def _():
        keys, reads = bc_ref[:, :STATE], bc_ref[:, STATE:]
        keys_hi, keys_lo = halves(keys)
        reads_hi, reads_lo = halves(reads)
        score[...] = mask_ref[0] * (mm_nt(reads_hi, keys_hi) + mm_nt(reads_hi, keys_lo) + mm_nt(reads_lo, keys_hi))
        scoreT[...] = mask_ref[1] * (mm_nt(keys_hi, reads_hi) + mm_nt(keys_hi, reads_lo) + mm_nt(keys_lo, reads_hi))
        score_grad_ref[...] = jnp.zeros_like(score_grad_ref)

    total, _ = convolve(tail_ref[...].astype(F32), x_ref[...].astype(F32), taps_ref[...], valid_ref[...])
    act = total * sigmoid(total)
    turn = lax.rem(LANES - TILE_HEADS * tile_at(tile, half_ref), LANES)
    run = pltpu.roll(run_ref[...], turn, 1)
    dt = pltpu.roll(dt_ref[...], turn, 1)
    left = iota((ROWS, LANES), 1) < HEAD_DIM
    left = jnp.where(left, 1.0, 0.0).astype(BF16)
    right = 1.0 - left
    score_grad = score_grad_ref[...]
    for pair in range(TILE_HEADS // 2):
        lanes = slice(LANES * pair, LANES * (pair + 1))
        spread, weights, weightsT = [], [], []
        for head in (2 * pair, 2 * pair + 1):
            run_col, run_row = run[:, head : head + 1], runT_ref[head : head + 1, :]
            difference = run_col - run_row
            step = jnp.exp(jnp.minimum(difference, 0.0)) * dtT_ref[head : head + 1, :]
            spread.append(step)
            weights.append(step * score[...])
            weightsT.append(jnp.exp(jnp.minimum(-difference, 0.0)) * dt[:, head : head + 1] * scoreT[...])
        x_hi, x_lo = halves(act[:, lanes])
        upstream = cot_ref[:, lanes]
        x_hi2 = jnp.concatenate([x_hi * left, x_hi * right], axis=0)
        x_lo2 = jnp.concatenate([x_lo * left, x_lo * right], axis=0)
        upstream2 = jnp.concatenate([upstream * left, upstream * right], axis=0)
        w_hi, w_lo = halves(jnp.concatenate(weights, axis=1))
        wide = mm(w_hi, jnp.concatenate([x_hi2, x_lo2], axis=1))
        out_ref[:, lanes] = wide[:, :LANES] + wide[:, LANES:] + mm(w_lo, x_hi2)
        wt_hi, wt_lo = halves(jnp.concatenate(weightsT, axis=1))
        grad_ref[:, lanes] = mm(wt_hi, upstream2) + mm(wt_lo, upstream2)
        inner = mm_nt(upstream2, jnp.concatenate([x_hi, x_lo], axis=0))
        inner = inner[:, :ROWS] + inner[:, ROWS:]
        score_grad = score_grad + inner[:ROWS] * spread[0] + inner[ROWS:] * spread[1]
    score_grad_ref[...] = score_grad

    @pl.when(tile == TILES - 1)
    def _():
        score_grad_ref[...] = score_grad_ref[...] * mask_ref[0]


def within_stage(half, conv_input, tail, taps, valid, cotangent, bc, run, runT, dt, dtT, mask):
    square = whole((ROWS, LANES))
    rows = pl.BlockSpec((TILE_HEADS, LANES), lambda i, half: (tile_at(i, half), 0))
    wide = jax.ShapeDtypeStruct((ROWS, INNER), F32)
    return call(
        within_kernel, "within", half, TILES,
        [
            tile_spec(ROWS), tile_spec(8), tile_spec(8), whole((ROWS, 8)), tile_spec(ROWS),
            whole((ROWS, 2 * STATE)), square, rows, square, rows, whole((2, ROWS, ROWS)),
        ],
        [tile_spec(ROWS), tile_spec(ROWS), whole((ROWS, ROWS))],
        (wide, wide, jax.ShapeDtypeStruct((ROWS, ROWS), F32)),
        [pltpu.VMEM((ROWS, ROWS), F32)] * 2,
        (conv_input, tail, taps, valid, cotangent, bc, run, runT, dt, dtT, mask),
    )


def even_odd(half_ref, both):
    even = half_ref[2] == 0
    own, partner = both[0:1], both[8:9]
    return jnp.where(even, own, partner)[None], jnp.where(even, partner, own)[None]


def join_kernel(group, half_ref, mine_ref, other_ref, own_ref, partner_ref, out_ref, both):
    @pl.when(pl.program_id(0) == 0)
    def _():
        rows = jnp.concatenate([own_ref[...], partner_ref[...]], axis=0)
        for at in range(HALF_TILES):
            one_hot = head_columns(HALF_TILES * half_ref[0] + at)
            both[:, TILE * at : TILE * (at + 1)] = spread_exact(rows, one_hot)

    even = half_ref[2] == 0
    for at in range(HALF_TILES):
        lanes = slice(TILE * at, TILE * (at + 1))
        earlier, later = even_odd(half_ref, both[:, lanes])
        mine, other = mine_ref[:, :, lanes], other_ref[:, :, lanes]
        first, second = jnp.where(even, mine, other), jnp.where(even, other, mine)
        out_ref[:, :group, lanes] = later * first[:, :group] + second[:, :group]
        out_ref[:, group:, lanes] = first[:, group:] + earlier * second[:, group:]
    decay = own_ref[0:1, :] * partner_ref[0:1, :]
    out_ref[:, :, INNER // 2 :] = jnp.broadcast_to(decay[None], out_ref.shape[:2] + (LANES,))


def join_stage(group, half, mine, other, own, partner):
    chips, rows, width = mine.shape
    step = chips // 4
    spec = pl.BlockSpec((step, rows, width), lambda i, half: (i, 0, 0))
    return call(
        functools.partial(join_kernel, group), "join", half, 4,
        [spec, spec, whole((8, LANES)), whole((8, LANES))],
        pl.BlockSpec((step, rows, width + LANES), lambda i, half: (i, 0, 0)),
        jax.ShapeDtypeStruct((chips, rows, width + LANES), F32), [pltpu.VMEM((16, width), F32)],
        (mine, other, own, partner),
    )


def carry_kernel(group, half_ref, pair_ref, rest_ref, out_ref, decay):
    chips = pair_ref.shape[0]
    one_hot = head_columns(tile_at(pl.program_id(0), half_ref))
    decay[...] = spread_exact(jnp.max(rest_ref[...], axis=1), one_hot)
    state = jnp.zeros((group, TILE), F32)
    adjoint = jnp.zeros((group, TILE), F32)
    for chip in range(chips):
        out_ref[chip, :group, :] = state
        state = decay[chip : chip + 1, :] * state + pair_ref[chip, :group, :]
        back = chips - 1 - chip
        out_ref[back, group:, :] = adjoint
        adjoint = decay[back : back + 1, :] * adjoint + pair_ref[back, group:, :]


def carry_stage(group, half, pairs):
    chips, rows, width = pairs.shape
    shape = (chips, rows, width - LANES)
    return call(
        functools.partial(carry_kernel, group), "carry", half, HALF_TILES,
        [pair_spec(shape, True), pl.BlockSpec((chips, rows, LANES), lambda *at: (0, 0, shape[2] // LANES))],
        pair_spec(shape, True), jax.ShapeDtypeStruct(shape, F32), [pltpu.VMEM((chips, TILE), F32)], (pairs, pairs),
    )


def conv_backward(grad, shifted, taps, valid):
    width = grad.shape[1]
    zeros = jnp.zeros((8, width), F32)
    total = jnp.concatenate([zeros, grad * taps[3:4]], axis=0)
    parts = [jnp.sum(grad * shifted[0], axis=0, keepdims=True)]
    for back in range(1, CONV):
        parts.insert(0, jnp.sum(grad * shifted[back], axis=0, keepdims=True))
        moved = jnp.concatenate([zeros, grad * valid[:, back - 1 : back] * taps[3 - back : 4 - back], zeros], axis=0)
        total = total + moved[back : back + ROWS + 8]
    parts.append(jnp.sum(grad, axis=0, keepdims=True))
    parts.append(jnp.zeros((3, width), F32))
    return total, jnp.concatenate(parts, axis=0)


def finish_kernel(group, final, half_ref, x_ref, tail_ref, taps_ref, xs_ref, tails_ref, tapss_ref, valid_ref, cot_ref, both_ref,
                  out_in_ref, grad_in_ref, chip_ref, local_ref, bc_ref, small_ref, own_ref, partner_ref, *refs):
    if final:
        score_grad_ref, run_ref, dt_ref, sig_ref, sigsum_ref = refs[:5]
        bc_before, head_before, token_before = refs[5:8]
        out_ref, grad_ref, end_ref, borrowed_ref, taps_grad_ref = refs[13:18]
        grads_ref, ends_ref, borroweds_ref, tapss_grad_ref, heads_ref = refs[18:23]
        lhs_hi, lhs_lo, bc_grad, by_head, by_token = refs[23:]
    else:
        out_ref, grad_ref, end_ref, borrowed_ref, taps_grad_ref, bc_grad, by_head, by_token, lhs_hi, lhs_lo = refs
    tile = pl.program_id(0)
    valid = valid_ref[...]

    @pl.when(tile == 0)
    def _():
        for at, source, late in ((0, STATE, False), (ROWS, 0, True)):
            pick = interleave(group, late).astype(BF16)
            first, second = halves(bc_ref[:, source : source + STATE])
            lhs_hi[at : at + ROWS, :] = mm_nt(first, pick).astype(BF16)
            lhs_lo[at : at + ROWS, :] = mm_nt(second, pick).astype(BF16)
        if final:
            bc_grad[...] = bc_before[...]
            by_head[...] = head_before[...]
            by_token[...] = token_before[...]
        else:
            bc_grad[...] = jnp.zeros_like(bc_grad)
            by_head[...] = jnp.zeros_like(by_head)
            by_token[...] = jnp.zeros_like(by_token)

    total, shifted = convolve(tail_ref[...].astype(F32), x_ref[...].astype(F32), taps_ref[...], valid)
    gate = sigmoid(total)
    act = total * gate
    upstream = cot_ref[...].astype(F32)
    here = tile_at(tile, half_ref)
    weight = spread_heads(both_ref, here)
    leave, entry = weight[:ROWS], weight[ROWS:]
    by_row = spread_exact(
        jnp.concatenate([own_ref[...], partner_ref[...], small_ref[...]], axis=0), head_columns(here)
    )
    earlier, later = even_odd(half_ref, by_row)
    even = half_ref[2] == 0
    weight_state, weight_adjoint = jnp.where(even, 1.0, earlier), jnp.where(even, later, 1.0)
    with_state, with_adjoint = jnp.where(even, 0.0, 1.0), jnp.where(even, 1.0, 0.0)
    states = jnp.concatenate(
        [
            weight_state * chip_ref[:, :group, :] + with_state * local_ref[:, :group, :],
            weight_adjoint * chip_ref[:, group:, :] + with_adjoint * local_ref[:, group:, :],
        ],
        axis=1,
    ).reshape(2 * STATE, TILE)
    states_hi, states_lo = halves(states)
    read = mm(lhs_hi[...], states_hi) + mm(lhs_hi[...], states_lo) + mm(lhs_lo[...], states_hi)
    one_hot = head_columns(here)
    gain = by_row[18:19]
    through_state = out_in_ref[...] + entry * read[:ROWS]
    out_ref[...] = (through_state + gain * act).astype(BF16)
    act_grad_late = leave * read[ROWS:]
    act_grad = grad_in_ref[...] + act_grad_late

    first, second = halves(jnp.concatenate([entry * upstream, leave * act], axis=0))
    bc_grad[...] += mm_nt(first, states_hi) + mm_nt(first, states_lo) + mm_nt(second, states_hi)

    first, second = halves(jnp.concatenate([upstream * through_state, act * act_grad], axis=0))
    by_token[...] += mm_nt(first, one_hot) + mm_nt(second, one_hot)
    crossed = states * pltpu.roll(states, group, 0)
    crossed = jnp.where(iota((2 * STATE, TILE), 0) % (2 * group) >= group, crossed, 0.0)
    sums = jnp.concatenate(
        [
            jnp.sum(act * act_grad_late, axis=0, keepdims=True),
            jnp.sum(crossed, axis=0, keepdims=True),
            jnp.sum(upstream * act, axis=0, keepdims=True),
            jnp.zeros((5, TILE), F32),
        ],
        axis=0,
    )
    by_head[...] += lax.dot_general(
        sums, one_hot.astype(F32), (((1,), (1,)), ((), ())), precision=EXACT, preferred_element_type=F32
    )

    act_grad = act_grad + gain * upstream
    conv_grad = act_grad * (gate + act * (1.0 - gate))
    full, taps_grad_ref[...] = conv_backward(conv_grad, shifted, taps_ref[...], valid)
    borrowed_ref[...] = full[:8]
    grad_ref[...] = full[8:].astype(BF16)
    end_ref[...] = full[ROWS - 8 :]

    if not final:
        return

    @pl.when(tile == HALF_TILES - 1)
    def _():
        score_grad = score_grad_ref[...]
        keys, reads = bc_ref[:, :STATE], bc_ref[:, STATE:]
        reads_grad = exact(bc_grad[:ROWS], interleave(group, False)) + exact(score_grad, keys)
        keys_grad = exact(bc_grad[ROWS:], interleave(group, True)) + exact(score_grad.T, reads)
        total, shifted = convolve(tails_ref[...].astype(F32), xs_ref[...].astype(F32), tapss_ref[...], valid)
        gate = sigmoid(total)
        small_grad = jnp.concatenate([keys_grad, reads_grad], axis=1) * (gate + total * gate * (1.0 - gate))
        full, tapss_grad_ref[...] = conv_backward(small_grad, shifted, tapss_ref[...], valid)
        borroweds_ref[...] = full[:8]
        grads_ref[...] = full[8:].astype(BF16)
        ends_ref[...] = full[ROWS - 8 :]

        read_sum, added_sum = by_token[:ROWS], by_token[ROWS:]
        at_end = by_head[0:1, :] + own_ref[0:1, :] * by_head[1:2, :]
        run_grad = read_sum - added_sum + jnp.where(iota((ROWS, LANES), 0) == ROWS - 1, at_end, 0.0)
        alog_grad = jnp.sum(run_grad * run_ref[...], axis=0, keepdims=True)
        bias_grad = jnp.sum(added_sum / dt_ref[...] * sig_ref[...], axis=0, keepdims=True)
        rate = jnp.exp(small_ref[1:2, :])
        bias_grad = bias_grad - rate * jnp.sum(run_grad * sigsum_ref[...], axis=0, keepdims=True)
        heads_ref[...] = jnp.concatenate([bias_grad, alog_grad, by_head[2:3, :], jnp.zeros((5, LANES), F32)], axis=0)


def finish_stage(group, half, operands, chip, local, bc, small, own, partner, last=None, before=None):
    final = last is not None
    square = whole((ROWS, LANES))
    wide = (
        jax.ShapeDtypeStruct((ROWS, INNER), BF16),
        jax.ShapeDtypeStruct((ROWS, INNER), BF16),
        jax.ShapeDtypeStruct((16, INNER), F32),
        jax.ShapeDtypeStruct((8, INNER), F32),
        jax.ShapeDtypeStruct((8, INNER), F32),
    )
    sums = (
        jax.ShapeDtypeStruct((2 * ROWS, 2 * STATE), F32),
        jax.ShapeDtypeStruct((8, LANES), F32),
        jax.ShapeDtypeStruct((2 * ROWS, LANES), F32),
    )
    ends = (
        jax.ShapeDtypeStruct((ROWS, 2 * STATE), BF16),
        jax.ShapeDtypeStruct((16, 2 * STATE), F32),
        jax.ShapeDtypeStruct((8, 2 * STATE), F32),
        jax.ShapeDtypeStruct((8, 2 * STATE), F32),
        jax.ShapeDtypeStruct((8, LANES), F32),
    )
    in_specs = [
        tile_spec(ROWS), tile_spec(8), tile_spec(8),
        small_spec(ROWS), small_spec(8), small_spec(8),
        whole((ROWS, 8)), tile_spec(ROWS), whole((2 * ROWS, 2 * LANES)),
        tile_spec(ROWS), tile_spec(ROWS), pair_spec(chip.shape, True), pair_spec(local.shape, True),
        whole((ROWS, 2 * STATE)), whole((8, LANES)), whole((8, LANES)), whole((8, LANES)),
    ]
    given = tuple(operands) + (chip, local, bc, small, own, partner)
    lhs = [pltpu.VMEM((2 * ROWS, 2 * STATE), BF16)] * 2
    aliases = {}
    if final:
        in_specs += [whole((ROWS, ROWS)), square, square, square, square]
        in_specs += [whole(part.shape) for part in sums] + [pl.BlockSpec(memory_space=pl.ANY)] * len(wide)
        aliases = {1 + len(given) + len(last) + len(sums) + at: at for at in range(len(wide))}
        given += tuple(last) + tuple(before[len(wide):]) + tuple(before[: len(wide)])
        rest, scratch = ends, lhs + [pltpu.VMEM(part.shape, F32) for part in sums]
    else:
        rest, scratch = sums, lhs
    return call(
        functools.partial(finish_kernel, group, final), "finish_second" if final else "finish_first", half, HALF_TILES,
        in_specs, [tile_spec(part.shape[0]) for part in wide] + [whole(part.shape) for part in rest], wide + rest,
        scratch, given, aliases,
    )


def total_kernel(scale, taps_ref, small_ref, heads_ref, borrowed_ref, borroweds_ref, end_ref, ends_ref, keep_ref, grad_ref,
                 grads_ref, weight_ref, bias_ref, heads_out_ref, whole_ref,
                 parts, slots, piece, far_slots, result, got, got_small, send, receive, far_send, far_receive, back_send,
                 back_receive, rows_send, rows_receive):
    shards, groups = lax.axis_size("seq"), lax.axis_size("dp")
    others = groups * shards // 8
    place, group = lax.axis_index("seq"), lax.axis_index("dp")
    before = (group, lax.rem(place + shards - 1, shards))
    after = (group, lax.rem(place + 1, shards))
    barrier = pltpu.get_barrier_semaphore()
    for peers, size in ((near, 8), (far, others)):
        for k in range(1, size):
            pl.semaphore_signal(barrier, inc=1, device_id=peers(k)[0], device_id_type=MESH)
    for peer in (before, after):
        pl.semaphore_signal(barrier, inc=1, device_id=peer, device_id_type=MESH)
    pl.semaphore_wait(barrier, 7 + others - 1 + 2)

    depth = parts.shape[1]
    wide = CH // LANES
    for at in range(8 * depth // 8):
        if at < INNER // LANES:
            block = taps_ref[:, LANES * at : LANES * (at + 1)]
        elif at < wide:
            block = small_ref[:, LANES * at - INNER : LANES * (at + 1) - INNER]
        elif at == wide:
            block = heads_ref[...]
        else:
            block = jnp.zeros((8, LANES), F32)
        parts[at % 8, 8 * (at // 8) : 8 * (at // 8) + 8, :] = block
    send_all(near, 8, lambda slot: parts.at[slot], slots, send, receive)
    returns = [
        pltpu.make_async_remote_copy(
            src_ref=source, dst_ref=target, send_sem=rows_send.at[at], recv_sem=rows_receive.at[at], device_id=before,
            device_id_type=MESH,
        )
        for at, (source, target) in enumerate(((borrowed_ref, got), (borroweds_ref, got_small)))
    ]

    @pl.when(place > 0)
    def _():
        for copy in returns:
            copy.start()

    _, own = near(0)
    _, far_own = far(0)
    slots[own] = parts[own]
    wait_all(near, 8, lambda slot: parts.at[slot], slots, send, receive)
    piece[...] = jnp.sum(slots[...], axis=0)
    send_all(far, others, lambda slot: piece, far_slots, far_send, far_receive)
    whole_ref[:, :INNER] = grad_ref[...]
    whole_ref[:, INNER:] = grads_ref[...]
    far_slots[far_own] = piece[...]
    wait_all(far, others, lambda slot: piece, far_slots, far_send, far_receive)
    piece[...] = jnp.sum(far_slots[...], axis=0) * scale
    send_all(near, 8, lambda slot: piece, result, back_send, back_receive)
    result[own] = piece[...]

    @pl.when(place > 0)
    def _():
        for copy in returns:
            copy.wait_send()

    @pl.when(place < shards - 1)
    def _():
        for copy in returns:
            copy.wait_recv()
        keep = keep_ref[:, 0:1]
        for lanes, source, end in ((slice(0, INNER), got, end_ref), (slice(INNER, CH), got_small, ends_ref)):
            late = iota(source.shape, 0) >= 8 - CONV + 1
            rows = jnp.concatenate([end[:8, :], end[8:, :] + jnp.where(late, source[...] * keep, 0.0)], axis=0)
            whole_ref[ROWS - 16 :, lanes] = rows.astype(BF16)

    wait_all(near, 8, lambda slot: piece, result, back_send, back_receive)
    for at in range(wide + 1):
        block = result[at % 8, 8 * (at // 8) : 8 * (at // 8) + 8, :]
        if at < wide:
            weight_ref[:, LANES * at : LANES * (at + 1)] = block[:CONV]
            bias_ref[:, LANES * at : LANES * (at + 1)] = block[CONV : CONV + 1]
        else:
            heads_out_ref[...] = block


def total_stage(others, scale, *operands):
    depth = 8 * pl.cdiv(CH // LANES + 1, 8)
    in_vmem = pl.BlockSpec(memory_space=pltpu.VMEM)
    shapes = (
        jax.ShapeDtypeStruct((CONV, CH), F32),
        jax.ShapeDtypeStruct((1, CH), F32),
        jax.ShapeDtypeStruct((8, LANES), F32),
        jax.ShapeDtypeStruct((ROWS, CH), BF16),
    )
    dma = pltpu.SemaphoreType.DMA
    return pl.pallas_call(
        functools.partial(total_kernel, scale),
        in_specs=[in_vmem] * len(operands),
        out_specs=[in_vmem] * len(shapes),
        out_shape=shapes,
        scratch_shapes=[
            pltpu.VMEM((8, depth, LANES), F32), pltpu.VMEM((8, depth, LANES), F32),
            pltpu.VMEM((depth, LANES), F32), pltpu.VMEM((others, depth, LANES), F32),
            pltpu.VMEM((8, depth, LANES), F32),
            pltpu.VMEM((8, INNER), F32), pltpu.VMEM((8, 2 * STATE), F32),
            dma((8,)), dma((8,)), dma((others,)), dma((others,)), dma((8,)), dma((8,)), dma((2,)), dma((2,)),
        ],
        compiler_params=pltpu.CompilerParams(
            vmem_limit_bytes=VMEM_BYTES, collective_id=1, has_side_effects=True
        ),
        name="totals",
    )(*operands)


def swap(array):
    return lax.ppermute(array, "seq", [(i, i ^ 1) for i in range(lax.axis_size("seq"))])


def between_chips(array):
    size = lax.axis_size("seq")
    groups = [list(range(0, size, 2)), list(range(1, size, 2))]
    return lax.all_to_all(array, "seq", 0, 0, axis_index_groups=groups, tiled=True)


def on_device(conv_input, doc_start, conv_weight, conv_bias, dt_raw, dt_bias, a_log, skip_gain, cotangent):
    shards, place = lax.axis_size("seq"), lax.axis_index("seq")
    group = 2 * STATE // shards
    core = lax.rem(place, 2)
    half = jnp.stack([core, place // 2, core])
    other_half = jnp.stack([1 - core, place // 2, core])
    run, runT, dt, dtT, both, sig, sigsum, mask, valid, keep, tail, own, small, taps = head_stage(
        dt_raw.T, dt_bias[None], a_log[None], skip_gain[None], doc_start[None], conv_weight, conv_bias[None], conv_input
    )
    tail = lax.ppermute(tail, "seq", [(i, i + 1) for i in range(shards - 1)])
    partner = swap(own)
    theirs, bc = local_stage(group, other_half, conv_input, tail, taps, valid, cotangent, both)
    other = swap(theirs)
    mine, _ = local_stage(group, half, conv_input, tail, taps, valid, cotangent, both)
    other_second = swap(mine)
    gathered = between_chips(join_stage(group, half, mine, other, own, partner))
    out_in, grad_in, score_grad = within_stage(
        half, conv_input, tail, taps, valid, cotangent, bc, run, runT, dt, dtT, mask
    )
    gathered, out_in, grad_in = lax.optimization_barrier((gathered, out_in, grad_in))
    chip = between_chips(carry_stage(group, half, gathered))
    chip_second = swap(chip)
    operands = (conv_input, tail, taps, conv_input, tail, taps, valid, cotangent, both, out_in, grad_in)
    first = finish_stage(group, half, operands, chip, other, bc, small, own, partner)
    out, grad, end, borrowed, taps_grad, grads, ends, borroweds, tapss_grad, heads = finish_stage(
        group, other_half, operands, chip_second, other_second, bc, small, own, partner,
        (score_grad, run, dt, sig, sigsum), first,
    )
    groups = lax.axis_size("dp")
    weight_grad, bias_grad, heads, whole_grad = total_stage(
        groups * shards // 8, float(groups * shards * ROWS) ** (-0.5), taps_grad, tapss_grad, heads, borrowed, borroweds,
        end, ends, keep, grad, grads,
    )
    return (out, whole_grad, weight_grad, bias_grad.reshape(-1), heads[0, :HEADS], heads[1, :HEADS], heads[2, :HEADS])


def solution(mesh):
    sharded = P(("dp", "seq"), None)
    return jax.shard_map(
        on_device,
        mesh=mesh,
        in_specs=(sharded, P(("dp", "seq")), P(), P(), sharded, P(), P(), P(), sharded),
        out_specs=(sharded, sharded, P(), P(), P(), P(), P()),
        check_vma=False,
    )
```

```python
import functools

import jax
import jax.numpy as jnp
from jax import lax
from jax.experimental import pallas as pl
from jax.experimental.pallas import tpu as pltpu
from jax.sharding import PartitionSpec as P

HEADS = 80
HEAD_DIM = 64
STATE = 128
CONV = 4
INNER = 5120
CH = 5376
ROWS = 128
TILE = 512
TILES = INNER // TILE
TILE_HEADS = TILE // HEAD_DIM
LANES = 128

F32 = jnp.float32
BF16 = jnp.bfloat16
EXACT = lax.Precision.HIGHEST
HALF_TILES = TILES // 2
VMEM_BYTES = 60 << 20
MESH = pl.DeviceIdType.MESH


def iota(shape, axis):
    return lax.broadcasted_iota(jnp.int32, shape, axis)


def halves(value):
    high = value.astype(BF16)
    return high, (value - high.astype(F32)).astype(BF16)


def mm(a, b):
    return lax.dot_general(a, b, (((1,), (0,)), ((), ())), preferred_element_type=F32)


def mm_nt(a, b):
    return lax.dot_general(a, b, (((1,), (1,)), ((), ())), preferred_element_type=F32)


def exact(a, b):
    return lax.dot_general(
        a, b, (((1,), (0,)), ((), ())), precision=EXACT, preferred_element_type=F32
    )


def spread_exact(rows, one_hot):
    first, rest = rows.astype(BF16), rows
    rest = rest - first.astype(F32)
    second, third = halves(rest)
    return mm(first, one_hot) + mm(second, one_hot) + mm(third, one_hot)


def interleave(group, late):
    row, col = iota((2 * STATE, STATE), 0), iota((2 * STATE, STATE), 1)
    place = row % (2 * group)
    first = group if late else 0
    here = (place >= first) & (place < first + group)
    return jnp.where(here & (col == group * (row // (2 * group)) + place - first), 1.0, 0.0)


def head_columns(tile):
    head, col = iota((LANES, TILE), 0), iota((LANES, TILE), 1)
    return jnp.where(head == TILE_HEADS * tile + col // HEAD_DIM, 1.0, 0.0).astype(BF16)


def spread_heads(both_ref, tile):
    one_hot = head_columns(tile)
    return mm(both_ref[...], jnp.concatenate([one_hot, one_hot], axis=0))


def convolve(tail, rows, taps, valid):
    extended = jnp.concatenate([tail, rows], axis=0)
    total = taps[4:5] + taps[3:4] * rows
    shifted = [rows]
    for back in range(1, CONV):
        moved = extended[8 - back : 8 - back + ROWS] * valid[:, back - 1 : back]
        shifted.append(moved)
        total = total + taps[3 - back : 4 - back] * moved
    return total, shifted


def sigmoid(v):
    return 1.0 / (1.0 + jnp.exp(-v))


def near(k):
    place = lax.axis_index("seq")
    slot = lax.rem(lax.rem(place, 8) + k, 8)
    return (lax.axis_index("dp"), place - lax.rem(place, 8) + slot), slot


def far(k):
    place, group = lax.axis_index("seq"), lax.axis_index("dp")
    runs = lax.axis_size("seq") // 8
    slot = lax.rem(group * runs + place // 8 + k, lax.axis_size("dp") * runs)
    return (slot // runs, lax.rem(slot, runs) * 8 + lax.rem(place, 8)), slot


def send_all(peers, size, source, target, send, receive):
    _, own = peers(0)
    for k in range(1, size):
        peer, slot = peers(k)
        pltpu.make_async_remote_copy(
            src_ref=source(slot), dst_ref=target.at[own], send_sem=send.at[slot], recv_sem=receive.at[own],
            device_id=peer, device_id_type=MESH,
        ).start()


def wait_all(peers, size, source, target, send, receive):
    for k in range(1, size):
        peer, slot = peers(k)
        copy = pltpu.make_async_remote_copy(
            src_ref=source(slot), dst_ref=target.at[slot], send_sem=send.at[slot], recv_sem=receive.at[slot],
            device_id=peer, device_id_type=MESH,
        )
        copy.wait_send()
        copy.wait_recv()


def head_kernel(raw_in_ref, dt_bias_ref, a_log_ref, gain_ref, row_ref, weight_ref, bias_ref, end_ref, run_ref, runT_ref,
                dt_ref, dtT_ref, both_ref, sig_ref, sigsum_ref, mask_ref, valid_ref, keep_ref, tail_ref, own_ref,
                small_ref, taps_ref, raw):
    taps_ref[:CONV, :] = weight_ref[...]
    taps_ref[CONV:, :] = jnp.broadcast_to(bias_ref[...], (8 - CONV, CH))
    small_ref[...] = jnp.zeros_like(small_ref)
    for at, source in enumerate((dt_bias_ref, a_log_ref, gain_ref)):
        small_ref[at : at + 1, :HEADS] = source[...]
    reset_row = row_ref[...].astype(F32)
    token, other = iota((ROWS, ROWS), 0), iota((ROWS, ROWS), 1)
    reset_col = jnp.sum(jnp.where(token == other, reset_row, 0.0), axis=1, keepdims=True)
    low, high = token >= other, token <= other
    segment_col = jnp.sum(jnp.where(low, reset_row, 0.0), axis=1, keepdims=True)
    segment_row = jnp.sum(jnp.where(high, reset_col, 0.0), axis=0, keepdims=True)
    mask_ref[0] = jnp.where(low & (segment_col == segment_row), 1.0, 0.0)
    mask_ref[1] = jnp.where(high & (segment_col == segment_row), 1.0, 0.0)

    kept = jnp.broadcast_to(1.0 - reset_col, (ROWS, LANES))
    one_back = jnp.where(token < 1, 1.0, pltpu.roll(kept, 1, 0))
    two_back = jnp.where(token < 2, 1.0, pltpu.roll(kept, 2, 0))
    valid = jnp.where(other == 0, kept, jnp.where(other == 1, kept * one_back, kept * one_back * two_back))
    valid_ref[...] = valid[:, :8]
    one_on, two_on = pltpu.roll(kept, ROWS - 1, 0), pltpu.roll(kept, ROWS - 2, 0)
    keep = jnp.where(
        token == ROWS - 1, 1.0, jnp.where(token == ROWS - 2, one_on, jnp.where(token == ROWS - 3, one_on * two_on, 0.0))
    )[ROWS - 8 :]
    keep_ref[...] = keep
    tail_ref[...] = (end_ref[8:, :].astype(F32) * keep[:, 0:1]).astype(BF16)

    raw[...] = jnp.zeros_like(raw)
    raw[:HEADS, :] = raw_in_ref[...]
    biased = raw[...].T + small_ref[0:1, :]
    dt = jnp.maximum(biased, 0.0) + jnp.log1p(jnp.exp(-jnp.abs(biased)))
    decay = -jnp.exp(small_ref[1:2, :]) * dt
    lower = jnp.where(low, 1.0, 0.0)
    running = exact(lower, decay)
    last = running[ROWS - 1 : ROWS]
    count = segment_col[ROWS - 1 : ROWS]
    untouched = jnp.where(segment_col == 0.0, 1.0, 0.0)
    entry = jnp.exp(running) * untouched
    own_ref[...] = jnp.broadcast_to(entry[ROWS - 1 : ROWS], own_ref.shape)
    sig = sigmoid(biased)
    sig_ref[...] = sig
    sigsum_ref[...] = exact(lower, sig)
    run_ref[...] = running
    runT_ref[...] = running.T
    dt_ref[...] = dt
    dtT_ref[...] = dt.T
    leave = jnp.exp(last - running) * jnp.where(segment_col == count, 1.0, 0.0) * dt
    for at, part in ((0, leave), (ROWS, entry)):
        first, second = halves(part)
        both_ref[at : at + ROWS, :LANES] = first
        both_ref[at : at + ROWS, LANES:] = second


def head_stage(raw, dt_bias, a_log, gain, row, weight, bias, conv_input):
    square = jax.ShapeDtypeStruct((ROWS, LANES), F32)
    eight = jax.ShapeDtypeStruct((8, LANES), F32)
    shapes = (
        square, square, square, square,
        jax.ShapeDtypeStruct((2 * ROWS, 2 * LANES), BF16),
        square, square,
        jax.ShapeDtypeStruct((2, ROWS, ROWS), F32),
        jax.ShapeDtypeStruct((ROWS, 8), F32),
        eight,
        jax.ShapeDtypeStruct((8, CH), BF16),
        eight, eight,
        jax.ShapeDtypeStruct((8, CH), F32),
    )
    given = (raw, dt_bias, a_log, gain, row, weight, bias)
    return pl.pallas_call(
        head_kernel,
        grid=(1,),
        in_specs=[whole(part.shape) for part in given] + [pl.BlockSpec((16, CH), lambda *at: (ROWS // 16 - 1, 0))],
        out_specs=[whole(part.shape) for part in shapes],
        out_shape=shapes,
        scratch_shapes=[pltpu.VMEM((ROWS, LANES), F32)],
        compiler_params=pltpu.CompilerParams(vmem_limit_bytes=VMEM_BYTES),
        name="heads",
    )(*given, conv_input)


def whole(shape):
    return pl.BlockSpec(shape, lambda *at: (0,) * len(shape))


def call(kernel, name, half, grid, in_specs, out_specs, out_shape, scratch_shapes, operands, aliases={}):
    return pl.pallas_call(
        kernel,
        grid_spec=pltpu.PrefetchScalarGridSpec(
            num_scalar_prefetch=1, grid=(grid,), in_specs=in_specs, out_specs=out_specs, scratch_shapes=scratch_shapes
        ),
        out_shape=out_shape,
        input_output_aliases=aliases,
        compiler_params=pltpu.CompilerParams(vmem_limit_bytes=VMEM_BYTES),
        name=name,
    )(half, *operands)


def tile_at(i, half):
    return lax.rem(i + HALF_TILES * half[0], TILES)


def tile_spec(rows):
    return pl.BlockSpec((rows, TILE), lambda i, half: (0, tile_at(i, half)))


def small_spec(rows):
    return pl.BlockSpec((rows, 2 * STATE), lambda *at: (0, INNER // (2 * STATE)))


def pair_spec(shape, first):
    if first:
        return pl.BlockSpec(shape[:2] + (TILE,), lambda i, half: (0, 0, jnp.minimum(i, HALF_TILES - 1)))
    return pl.BlockSpec(shape[:2] + (TILE,), lambda i, half: (0, 0, jnp.maximum(i - HALF_TILES, 0)))


def local_kernel(group, half_ref, x_ref, tail_ref, taps_ref, xs_ref, tails_ref, tapss_ref, valid_ref, cot_ref,
                 both_ref, pair_ref, bc_ref, lhs_hi, lhs_lo):
    valid = valid_ref[...]

    @pl.when(pl.program_id(0) == 0)
    def _():
        total, _ = convolve(tails_ref[...].astype(F32), xs_ref[...].astype(F32), tapss_ref[...], valid)
        small = total * sigmoid(total)
        bc_ref[...] = small
        for at, late in ((0, False), (STATE, True)):
            pick = interleave(group, late).astype(BF16)
            first, second = halves(small[:, at : at + STATE])
            lhs_hi[:, at : at + ROWS] = mm_nt(pick, first).astype(BF16)
            lhs_lo[:, at : at + ROWS] = mm_nt(pick, second).astype(BF16)

    total, _ = convolve(tail_ref[...].astype(F32), x_ref[...].astype(F32), taps_ref[...], valid)
    act = total * sigmoid(total)
    weight = spread_heads(both_ref, tile_at(pl.program_id(0), half_ref))
    first, second = halves(weight * jnp.concatenate([act, cot_ref[...].astype(F32)], axis=0))
    result = mm(lhs_hi[...], first) + mm(lhs_hi[...], second) + mm(lhs_lo[...], first)
    pair_ref[...] = result.reshape(pair_ref.shape)


def local_stage(group, half, conv_input, tail, taps, valid, cotangent, both):
    shape = (STATE // group, 2 * group, INNER // 2)
    return call(
        functools.partial(local_kernel, group), "local", half, HALF_TILES,
        [
            tile_spec(ROWS), tile_spec(8), tile_spec(8),
            small_spec(ROWS), small_spec(8), small_spec(8),
            whole((ROWS, 8)), tile_spec(ROWS), whole((2 * ROWS, 2 * LANES)),
        ],
        [pair_spec(shape, True), whole((ROWS, 2 * STATE))],
        (jax.ShapeDtypeStruct(shape, F32), jax.ShapeDtypeStruct((ROWS, 2 * STATE), F32)),
        [pltpu.VMEM((2 * STATE, 2 * ROWS), BF16)] * 2,
        (conv_input, tail, taps, conv_input, tail, taps, valid, cotangent, both),
    )


def within_kernel(half_ref, x_ref, tail_ref, taps_ref, valid_ref, cot_ref, bc_ref, run_ref, runT_ref, dt_ref, dtT_ref,
                  mask_ref, out_ref, grad_ref, score_grad_ref, score, scoreT):
    tile = pl.program_id(0)

    @pl.when(tile == 0)
    def _():
        keys, reads = bc_ref[:, :STATE], bc_ref[:, STATE:]
        keys_hi, keys_lo = halves(keys)
        reads_hi, reads_lo = halves(reads)
        score[...] = mask_ref[0] * (mm_nt(reads_hi, keys_hi) + mm_nt(reads_hi, keys_lo) + mm_nt(reads_lo, keys_hi))
        scoreT[...] = mask_ref[1] * (mm_nt(keys_hi, reads_hi) + mm_nt(keys_hi, reads_lo) + mm_nt(keys_lo, reads_hi))
        score_grad_ref[...] = jnp.zeros_like(score_grad_ref)

    total, _ = convolve(tail_ref[...].astype(F32), x_ref[...].astype(F32), taps_ref[...], valid_ref[...])
    act = total * sigmoid(total)
    turn = lax.rem(LANES - TILE_HEADS * tile_at(tile, half_ref), LANES)
    run = pltpu.roll(run_ref[...], turn, 1)
    dt = pltpu.roll(dt_ref[...], turn, 1)
    left = iota((ROWS, LANES), 1) < HEAD_DIM
    left = jnp.where(left, 1.0, 0.0).astype(BF16)
    right = 1.0 - left
    score_grad = score_grad_ref[...]
    for pair in range(TILE_HEADS // 2):
        lanes = slice(LANES * pair, LANES * (pair + 1))
        spread, weights, weightsT = [], [], []
        for head in (2 * pair, 2 * pair + 1):
            run_col, run_row = run[:, head : head + 1], runT_ref[head : head + 1, :]
            difference = run_col - run_row
            step = jnp.exp(jnp.minimum(difference, 0.0)) * dtT_ref[head : head + 1, :]
            spread.append(step)
            weights.append(step * score[...])
            weightsT.append(jnp.exp(jnp.minimum(-difference, 0.0)) * dt[:, head : head + 1] * scoreT[...])
        x_hi, x_lo = halves(act[:, lanes])
        upstream = cot_ref[:, lanes]
        x_hi2 = jnp.concatenate([x_hi * left, x_hi * right], axis=0)
        x_lo2 = jnp.concatenate([x_lo * left, x_lo * right], axis=0)
        upstream2 = jnp.concatenate([upstream * left, upstream * right], axis=0)
        w_hi, w_lo = halves(jnp.concatenate(weights, axis=1))
        wide = mm(w_hi, jnp.concatenate([x_hi2, x_lo2], axis=1))
        out_ref[:, lanes] = wide[:, :LANES] + wide[:, LANES:] + mm(w_lo, x_hi2)
        wt_hi, wt_lo = halves(jnp.concatenate(weightsT, axis=1))
        grad_ref[:, lanes] = mm(wt_hi, upstream2) + mm(wt_lo, upstream2)
        inner = mm_nt(upstream2, jnp.concatenate([x_hi, x_lo], axis=0))
        inner = inner[:, :ROWS] + inner[:, ROWS:]
        score_grad = score_grad + inner[:ROWS] * spread[0] + inner[ROWS:] * spread[1]
    score_grad_ref[...] = score_grad

    @pl.when(tile == TILES - 1)
    def _():
        score_grad_ref[...] = score_grad_ref[...] * mask_ref[0]


def within_stage(half, conv_input, tail, taps, valid, cotangent, bc, run, runT, dt, dtT, mask):
    square = whole((ROWS, LANES))
    rows = pl.BlockSpec((TILE_HEADS, LANES), lambda i, half: (tile_at(i, half), 0))
    wide = jax.ShapeDtypeStruct((ROWS, INNER), F32)
    return call(
        within_kernel, "within", half, TILES,
        [
            tile_spec(ROWS), tile_spec(8), tile_spec(8), whole((ROWS, 8)), tile_spec(ROWS),
            whole((ROWS, 2 * STATE)), square, rows, square, rows, whole((2, ROWS, ROWS)),
        ],
        [tile_spec(ROWS), tile_spec(ROWS), whole((ROWS, ROWS))],
        (wide, wide, jax.ShapeDtypeStruct((ROWS, ROWS), F32)),
        [pltpu.VMEM((ROWS, ROWS), F32)] * 2,
        (conv_input, tail, taps, valid, cotangent, bc, run, runT, dt, dtT, mask),
    )


def even_odd(half_ref, both):
    even = half_ref[2] == 0
    own, partner = both[0:1], both[8:9]
    return jnp.where(even, own, partner)[None], jnp.where(even, partner, own)[None]


def join_kernel(group, half_ref, mine_ref, other_ref, own_ref, partner_ref, out_ref, both):
    @pl.when(pl.program_id(0) == 0)
    def _():
        rows = jnp.concatenate([own_ref[...], partner_ref[...]], axis=0)
        for at in range(HALF_TILES):
            one_hot = head_columns(HALF_TILES * half_ref[0] + at)
            both[:, TILE * at : TILE * (at + 1)] = spread_exact(rows, one_hot)

    even = half_ref[2] == 0
    for at in range(HALF_TILES):
        lanes = slice(TILE * at, TILE * (at + 1))
        earlier, later = even_odd(half_ref, both[:, lanes])
        mine, other = mine_ref[:, :, lanes], other_ref[:, :, lanes]
        first, second = jnp.where(even, mine, other), jnp.where(even, other, mine)
        out_ref[:, :group, lanes] = later * first[:, :group] + second[:, :group]
        out_ref[:, group:, lanes] = first[:, group:] + earlier * second[:, group:]
    decay = own_ref[0:1, :] * partner_ref[0:1, :]
    out_ref[:, :, INNER // 2 :] = jnp.broadcast_to(decay[None], out_ref.shape[:2] + (LANES,))


def join_stage(group, half, mine, other, own, partner):
    chips, rows, width = mine.shape
    step = chips // 4
    spec = pl.BlockSpec((step, rows, width), lambda i, half: (i, 0, 0))
    return call(
        functools.partial(join_kernel, group), "join", half, 4,
        [spec, spec, whole((8, LANES)), whole((8, LANES))],
        pl.BlockSpec((step, rows, width + LANES), lambda i, half: (i, 0, 0)),
        jax.ShapeDtypeStruct((chips, rows, width + LANES), F32), [pltpu.VMEM((16, width), F32)],
        (mine, other, own, partner),
    )


ORDER = (10, 1, 4, 3, 12, 11, 9, 14, 6, 2, 8, 5, 15, 7, 13)


def chip_after(k):
    chip = lax.axis_index("seq") // 2
    return lax.rem(chip // 4 + k // 4, 4) * 4 + lax.rem(lax.rem(chip, 4) + k % 4, 4)


def carry_kernel(group, pair_ref, out_ref, ready, decay, send, receive):
    chips = pair_ref.shape[0]
    chip, core = lax.axis_index("seq") // 2, lax.rem(lax.axis_index("seq"), 2)

    def device(other):
        return (lax.axis_index("dp"), 2 * other + core)

    barrier = pltpu.get_barrier_semaphore()
    for k in ORDER:
        pl.semaphore_signal(barrier, inc=1, device_id=device(chip_after(k)), device_id_type=MESH)
    by_head = jnp.max(pair_ref[:, :, INNER // 2 :], axis=1)
    for at in range(HALF_TILES):
        lanes = slice(TILE * at, TILE * (at + 1))
        decay[:, lanes] = spread_exact(by_head, head_columns(HALF_TILES * core + at))
        state = jnp.zeros((group, TILE), F32)
        adjoint = jnp.zeros((group, TILE), F32)
        for here in range(chips):
            ready[here, :group, lanes] = state
            state = decay[here : here + 1, lanes] * state + pair_ref[here, :group, lanes]
            back = chips - 1 - here
            ready[back, group:, lanes] = adjoint
            adjoint = decay[back : back + 1, lanes] * adjoint + pair_ref[back, group:, lanes]
    pl.semaphore_wait(barrier, len(ORDER))
    for k in ORDER:
        other = chip_after(k)
        pltpu.make_async_remote_copy(
            src_ref=ready.at[other], dst_ref=out_ref.at[chip], send_sem=send.at[other], recv_sem=receive.at[chip],
            device_id=device(other), device_id_type=MESH,
        ).start()
    out_ref[chip] = ready[chip]
    for k in ORDER:
        other = chip_after(k)
        copy = pltpu.make_async_remote_copy(
            src_ref=ready.at[other], dst_ref=out_ref.at[other], send_sem=send.at[other], recv_sem=receive.at[other],
            device_id=device(other), device_id_type=MESH,
        )
        copy.wait_send()
        copy.wait_recv()


def carry_stage(group, pairs):
    chips, rows, width = pairs.shape
    shape = (chips, rows, width - LANES)
    in_vmem = pl.BlockSpec(memory_space=pltpu.VMEM)
    return pl.pallas_call(
        functools.partial(carry_kernel, group),
        in_specs=[in_vmem],
        out_specs=in_vmem,
        out_shape=jax.ShapeDtypeStruct(shape, F32),
        scratch_shapes=[
            pltpu.VMEM(shape, F32), pltpu.VMEM((chips, shape[2]), F32),
            pltpu.SemaphoreType.DMA((chips,)), pltpu.SemaphoreType.DMA((chips,)),
        ],
        compiler_params=pltpu.CompilerParams(vmem_limit_bytes=24 << 20, collective_id=2, has_side_effects=True),
        name="carry",
    )(pairs)


def conv_backward(grad, shifted, taps, valid):
    width = grad.shape[1]
    zeros = jnp.zeros((8, width), F32)
    total = jnp.concatenate([zeros, grad * taps[3:4]], axis=0)
    parts = [jnp.sum(grad * shifted[0], axis=0, keepdims=True)]
    for back in range(1, CONV):
        parts.insert(0, jnp.sum(grad * shifted[back], axis=0, keepdims=True))
        moved = jnp.concatenate([zeros, grad * valid[:, back - 1 : back] * taps[3 - back : 4 - back], zeros], axis=0)
        total = total + moved[back : back + ROWS + 8]
    parts.append(jnp.sum(grad, axis=0, keepdims=True))
    parts.append(jnp.zeros((3, width), F32))
    return total, jnp.concatenate(parts, axis=0)


def finish_kernel(group, final, half_ref, x_ref, tail_ref, taps_ref, xs_ref, tails_ref, tapss_ref, valid_ref, cot_ref, both_ref,
                  out_in_ref, grad_in_ref, chip_ref, local_ref, bc_ref, small_ref, own_ref, partner_ref, *refs):
    if final:
        score_grad_ref, run_ref, dt_ref, sig_ref, sigsum_ref = refs[:5]
        bc_before, head_before, token_before = refs[5:8]
        out_ref, grad_ref, end_ref, borrowed_ref, taps_grad_ref = refs[13:18]
        grads_ref, ends_ref, borroweds_ref, tapss_grad_ref, heads_ref = refs[18:23]
        lhs_hi, lhs_lo, bc_grad, by_head, by_token = refs[23:]
    else:
        out_ref, grad_ref, end_ref, borrowed_ref, taps_grad_ref, bc_grad, by_head, by_token, lhs_hi, lhs_lo = refs
    tile = pl.program_id(0)
    valid = valid_ref[...]

    @pl.when(tile == 0)
    def _():
        for at, source, late in ((0, STATE, False), (ROWS, 0, True)):
            pick = interleave(group, late).astype(BF16)
            first, second = halves(bc_ref[:, source : source + STATE])
            lhs_hi[at : at + ROWS, :] = mm_nt(first, pick).astype(BF16)
            lhs_lo[at : at + ROWS, :] = mm_nt(second, pick).astype(BF16)
        if final:
            bc_grad[...] = bc_before[...]
            by_head[...] = head_before[...]
            by_token[...] = token_before[...]
        else:
            bc_grad[...] = jnp.zeros_like(bc_grad)
            by_head[...] = jnp.zeros_like(by_head)
            by_token[...] = jnp.zeros_like(by_token)

    total, shifted = convolve(tail_ref[...].astype(F32), x_ref[...].astype(F32), taps_ref[...], valid)
    gate = sigmoid(total)
    act = total * gate
    upstream = cot_ref[...].astype(F32)
    here = tile_at(tile, half_ref)
    weight = spread_heads(both_ref, here)
    leave, entry = weight[:ROWS], weight[ROWS:]
    by_row = spread_exact(
        jnp.concatenate([own_ref[...], partner_ref[...], small_ref[...]], axis=0), head_columns(here)
    )
    earlier, later = even_odd(half_ref, by_row)
    even = half_ref[2] == 0
    weight_state, weight_adjoint = jnp.where(even, 1.0, earlier), jnp.where(even, later, 1.0)
    with_state, with_adjoint = jnp.where(even, 0.0, 1.0), jnp.where(even, 1.0, 0.0)
    states = jnp.concatenate(
        [
            weight_state * chip_ref[:, :group, :] + with_state * local_ref[:, :group, :],
            weight_adjoint * chip_ref[:, group:, :] + with_adjoint * local_ref[:, group:, :],
        ],
        axis=1,
    ).reshape(2 * STATE, TILE)
    states_hi, states_lo = halves(states)
    read = mm(lhs_hi[...], states_hi) + mm(lhs_hi[...], states_lo) + mm(lhs_lo[...], states_hi)
    one_hot = head_columns(here)
    gain = by_row[18:19]
    through_state = out_in_ref[...] + entry * read[:ROWS]
    out_ref[...] = (through_state + gain * act).astype(BF16)
    act_grad_late = leave * read[ROWS:]
    act_grad = grad_in_ref[...] + act_grad_late

    first, second = halves(jnp.concatenate([entry * upstream, leave * act], axis=0))
    bc_grad[...] += mm_nt(first, states_hi) + mm_nt(first, states_lo) + mm_nt(second, states_hi)

    first, second = halves(jnp.concatenate([upstream * through_state, act * act_grad], axis=0))
    by_token[...] += mm_nt(first, one_hot) + mm_nt(second, one_hot)
    crossed = states * pltpu.roll(states, group, 0)
    crossed = jnp.where(iota((2 * STATE, TILE), 0) % (2 * group) >= group, crossed, 0.0)
    sums = jnp.concatenate(
        [
            jnp.sum(act * act_grad_late, axis=0, keepdims=True),
            jnp.sum(crossed, axis=0, keepdims=True),
            jnp.sum(upstream * act, axis=0, keepdims=True),
            jnp.zeros((5, TILE), F32),
        ],
        axis=0,
    )
    by_head[...] += lax.dot_general(
        sums, one_hot.astype(F32), (((1,), (1,)), ((), ())), precision=EXACT, preferred_element_type=F32
    )

    act_grad = act_grad + gain * upstream
    conv_grad = act_grad * (gate + act * (1.0 - gate))
    full, taps_grad_ref[...] = conv_backward(conv_grad, shifted, taps_ref[...], valid)
    borrowed_ref[...] = full[:8]
    grad_ref[...] = full[8:].astype(BF16)
    end_ref[...] = full[ROWS - 8 :]

    if not final:
        return

    @pl.when(tile == HALF_TILES - 1)
    def _():
        score_grad = score_grad_ref[...]
        keys, reads = bc_ref[:, :STATE], bc_ref[:, STATE:]
        reads_grad = exact(bc_grad[:ROWS], interleave(group, False)) + exact(score_grad, keys)
        keys_grad = exact(bc_grad[ROWS:], interleave(group, True)) + exact(score_grad.T, reads)
        total, shifted = convolve(tails_ref[...].astype(F32), xs_ref[...].astype(F32), tapss_ref[...], valid)
        gate = sigmoid(total)
        small_grad = jnp.concatenate([keys_grad, reads_grad], axis=1) * (gate + total * gate * (1.0 - gate))
        full, tapss_grad_ref[...] = conv_backward(small_grad, shifted, tapss_ref[...], valid)
        borroweds_ref[...] = full[:8]
        grads_ref[...] = full[8:].astype(BF16)
        ends_ref[...] = full[ROWS - 8 :]

        read_sum, added_sum = by_token[:ROWS], by_token[ROWS:]
        at_end = by_head[0:1, :] + own_ref[0:1, :] * by_head[1:2, :]
        run_grad = read_sum - added_sum + jnp.where(iota((ROWS, LANES), 0) == ROWS - 1, at_end, 0.0)
        alog_grad = jnp.sum(run_grad * run_ref[...], axis=0, keepdims=True)
        bias_grad = jnp.sum(added_sum / dt_ref[...] * sig_ref[...], axis=0, keepdims=True)
        rate = jnp.exp(small_ref[1:2, :])
        bias_grad = bias_grad - rate * jnp.sum(run_grad * sigsum_ref[...], axis=0, keepdims=True)
        heads_ref[...] = jnp.concatenate([bias_grad, alog_grad, by_head[2:3, :], jnp.zeros((5, LANES), F32)], axis=0)


def finish_stage(group, half, operands, chip, local, bc, small, own, partner, last=None, before=None):
    final = last is not None
    square = whole((ROWS, LANES))
    wide = (
        jax.ShapeDtypeStruct((ROWS, INNER), BF16),
        jax.ShapeDtypeStruct((ROWS, INNER), BF16),
        jax.ShapeDtypeStruct((16, INNER), F32),
        jax.ShapeDtypeStruct((8, INNER), F32),
        jax.ShapeDtypeStruct((8, INNER), F32),
    )
    sums = (
        jax.ShapeDtypeStruct((2 * ROWS, 2 * STATE), F32),
        jax.ShapeDtypeStruct((8, LANES), F32),
        jax.ShapeDtypeStruct((2 * ROWS, LANES), F32),
    )
    ends = (
        jax.ShapeDtypeStruct((ROWS, 2 * STATE), BF16),
        jax.ShapeDtypeStruct((16, 2 * STATE), F32),
        jax.ShapeDtypeStruct((8, 2 * STATE), F32),
        jax.ShapeDtypeStruct((8, 2 * STATE), F32),
        jax.ShapeDtypeStruct((8, LANES), F32),
    )
    in_specs = [
        tile_spec(ROWS), tile_spec(8), tile_spec(8),
        small_spec(ROWS), small_spec(8), small_spec(8),
        whole((ROWS, 8)), tile_spec(ROWS), whole((2 * ROWS, 2 * LANES)),
        tile_spec(ROWS), tile_spec(ROWS), pair_spec(chip.shape, True), pair_spec(local.shape, True),
        whole((ROWS, 2 * STATE)), whole((8, LANES)), whole((8, LANES)), whole((8, LANES)),
    ]
    given = tuple(operands) + (chip, local, bc, small, own, partner)
    lhs = [pltpu.VMEM((2 * ROWS, 2 * STATE), BF16)] * 2
    aliases = {}
    if final:
        in_specs += [whole((ROWS, ROWS)), square, square, square, square]
        in_specs += [whole(part.shape) for part in sums] + [pl.BlockSpec(memory_space=pl.ANY)] * len(wide)
        aliases = {1 + len(given) + len(last) + len(sums) + at: at for at in range(len(wide))}
        given += tuple(last) + tuple(before[len(wide):]) + tuple(before[: len(wide)])
        rest, scratch = ends, lhs + [pltpu.VMEM(part.shape, F32) for part in sums]
    else:
        rest, scratch = sums, lhs
    return call(
        functools.partial(finish_kernel, group, final), "finish_second" if final else "finish_first", half, HALF_TILES,
        in_specs, [tile_spec(part.shape[0]) for part in wide] + [whole(part.shape) for part in rest], wide + rest,
        scratch, given, aliases,
    )


def total_kernel(scale, taps_ref, small_ref, heads_ref, borrowed_ref, borroweds_ref, end_ref, ends_ref, keep_ref,
                 sums_ref, last_ref,
                 parts, slots, piece, far_slots, result, got, got_small, send, receive, far_send, far_receive, back_send,
                 back_receive, rows_send, rows_receive):
    shards, groups = lax.axis_size("seq"), lax.axis_size("dp")
    others = groups * shards // 8
    place, group = lax.axis_index("seq"), lax.axis_index("dp")
    before = (group, lax.rem(place + shards - 1, shards))
    after = (group, lax.rem(place + 1, shards))
    barrier = pltpu.get_barrier_semaphore()
    for peers, size in ((near, 8), (far, others)):
        for k in range(1, size):
            pl.semaphore_signal(barrier, inc=1, device_id=peers(k)[0], device_id_type=MESH)
    for peer in (before, after):
        pl.semaphore_signal(barrier, inc=1, device_id=peer, device_id_type=MESH)
    pl.semaphore_wait(barrier, 7 + others - 1 + 2)

    depth = parts.shape[1]
    wide = CH // LANES
    for at in range(8 * depth // 8):
        if at < INNER // LANES:
            block = taps_ref[:, LANES * at : LANES * (at + 1)]
        elif at < wide:
            block = small_ref[:, LANES * at - INNER : LANES * (at + 1) - INNER]
        elif at == wide:
            block = heads_ref[...]
        else:
            block = jnp.zeros((8, LANES), F32)
        parts[at % 8, 8 * (at // 8) : 8 * (at // 8) + 8, :] = block
    send_all(near, 8, lambda slot: parts.at[slot], slots, send, receive)
    returns = [
        pltpu.make_async_remote_copy(
            src_ref=source, dst_ref=target, send_sem=rows_send.at[at], recv_sem=rows_receive.at[at], device_id=before,
            device_id_type=MESH,
        )
        for at, (source, target) in enumerate(((borrowed_ref, got), (borroweds_ref, got_small)))
    ]

    @pl.when(place > 0)
    def _():
        for copy in returns:
            copy.start()

    _, own = near(0)
    _, far_own = far(0)
    slots[own] = parts[own]
    wait_all(near, 8, lambda slot: parts.at[slot], slots, send, receive)
    piece[...] = jnp.sum(slots[...], axis=0)
    send_all(far, others, lambda slot: piece, far_slots, far_send, far_receive)
    far_slots[far_own] = piece[...]
    wait_all(far, others, lambda slot: piece, far_slots, far_send, far_receive)
    piece[...] = jnp.sum(far_slots[...], axis=0) * scale
    send_all(near, 8, lambda slot: piece, result, back_send, back_receive)
    result[own] = piece[...]

    @pl.when(place > 0)
    def _():
        for copy in returns:
            copy.wait_send()

    @pl.when(place < shards - 1)
    def _():
        for copy in returns:
            copy.wait_recv()
        keep = keep_ref[:, 0:1]
        for lanes, source, end in ((slice(0, INNER), got, end_ref), (slice(INNER, CH), got_small, ends_ref)):
            late = iota(source.shape, 0) >= 8 - CONV + 1
            rows = jnp.concatenate([end[:8, :], end[8:, :] + jnp.where(late, source[...] * keep, 0.0)], axis=0)
            last_ref[:, lanes] = rows.astype(BF16)

    @pl.when(place == shards - 1)
    def _():
        last_ref[:, :INNER] = end_ref[...].astype(BF16)
        last_ref[:, INNER:] = ends_ref[...].astype(BF16)

    wait_all(near, 8, lambda slot: piece, result, back_send, back_receive)
    for at in range(wide + 1):
        sums_ref[:, LANES * at : LANES * (at + 1)] = result[at % 8, 8 * (at // 8) : 8 * (at // 8) + 8, :]


def layout_kernel(sums_ref, last_ref, grad_ref, grads_ref, weight_ref, bias_ref, dt_bias_ref, a_log_ref, gain_ref,
                  whole_ref):
    step = pl.program_id(0)

    @pl.when(step == 0)
    def _():
        weight_ref[...] = sums_ref[:CONV, :CH]
        bias_ref[...] = sums_ref[CONV : CONV + 1, :CH].reshape(CH)
        for at, target in enumerate((dt_bias_ref, a_log_ref, gain_ref)):
            target[...] = sums_ref[at : at + 1, CH : CH + HEADS].reshape(HEADS)

    @pl.when(step < pl.num_programs(0) - 1)
    def _():
        whole_ref[:, :INNER] = grad_ref[...]
        whole_ref[:, INNER:] = grads_ref[...]

    @pl.when(step == pl.num_programs(0) - 1)
    def _():
        whole_ref[: whole_ref.shape[0] - 16, :INNER] = grad_ref[: whole_ref.shape[0] - 16, :]
        whole_ref[: whole_ref.shape[0] - 16, INNER:] = grads_ref[: whole_ref.shape[0] - 16, :]
        whole_ref[whole_ref.shape[0] - 16 :, :] = last_ref[...]


def layout_stage(sums, last, grad, grads):
    rows = 32
    shapes = (
        jax.ShapeDtypeStruct((CONV, CH), F32),
        jax.ShapeDtypeStruct((CH,), F32),
        jax.ShapeDtypeStruct((HEADS,), F32),
        jax.ShapeDtypeStruct((HEADS,), F32),
        jax.ShapeDtypeStruct((HEADS,), F32),
        jax.ShapeDtypeStruct((ROWS, CH), BF16),
    )
    blocks = [pl.BlockSpec((rows, width), lambda i: (i, 0)) for width in (INNER, 2 * STATE, CH)]
    return pl.pallas_call(
        layout_kernel,
        grid=(ROWS // rows,),
        in_specs=[whole(sums.shape), whole(last.shape)] + blocks[:2],
        out_specs=[whole(part.shape) for part in shapes[:5]] + blocks[2:],
        out_shape=shapes,
        name="layout",
    )(sums, last, grad, grads)


def total_stage(others, scale, *operands):
    depth = 8 * pl.cdiv(CH // LANES + 1, 8)
    in_vmem = pl.BlockSpec(memory_space=pltpu.VMEM)
    shapes = (jax.ShapeDtypeStruct((8, CH + LANES), F32), jax.ShapeDtypeStruct((16, CH), BF16))
    dma = pltpu.SemaphoreType.DMA
    return pl.pallas_call(
        functools.partial(total_kernel, scale),
        in_specs=[in_vmem] * len(operands),
        out_specs=[in_vmem] * len(shapes),
        out_shape=shapes,
        scratch_shapes=[
            pltpu.VMEM((8, depth, LANES), F32), pltpu.VMEM((8, depth, LANES), F32),
            pltpu.VMEM((depth, LANES), F32), pltpu.VMEM((others, depth, LANES), F32),
            pltpu.VMEM((8, depth, LANES), F32),
            pltpu.VMEM((8, INNER), F32), pltpu.VMEM((8, 2 * STATE), F32),
            dma((8,)), dma((8,)), dma((others,)), dma((others,)), dma((8,)), dma((8,)), dma((2,)), dma((2,)),
        ],
        compiler_params=pltpu.CompilerParams(
            vmem_limit_bytes=VMEM_BYTES, collective_id=1, has_side_effects=True
        ),
        name="totals",
    )(*operands)


def swap(array):
    return lax.ppermute(array, "seq", [(i, i ^ 1) for i in range(lax.axis_size("seq"))])


def between_chips(array):
    size = lax.axis_size("seq")
    groups = [list(range(0, size, 2)), list(range(1, size, 2))]
    return lax.all_to_all(array, "seq", 0, 0, axis_index_groups=groups, tiled=True)


def on_device(conv_input, doc_start, conv_weight, conv_bias, dt_raw, dt_bias, a_log, skip_gain, cotangent):
    shards, place = lax.axis_size("seq"), lax.axis_index("seq")
    group = 2 * STATE // shards
    core = lax.rem(place, 2)
    half = jnp.stack([core, place // 2, core])
    other_half = jnp.stack([1 - core, place // 2, core])
    run, runT, dt, dtT, both, sig, sigsum, mask, valid, keep, tail, own, small, taps = head_stage(
        dt_raw.T, dt_bias[None], a_log[None], skip_gain[None], doc_start[None], conv_weight, conv_bias[None], conv_input
    )
    tail = lax.ppermute(tail, "seq", [(i, i + 1) for i in range(shards - 1)])
    partner = swap(own)
    theirs, bc = local_stage(group, other_half, conv_input, tail, taps, valid, cotangent, both)
    other = swap(theirs)
    mine, _ = local_stage(group, half, conv_input, tail, taps, valid, cotangent, both)
    other_second = swap(mine)
    gathered = between_chips(join_stage(group, half, mine, other, own, partner))
    out_in, grad_in, score_grad = within_stage(
        half, conv_input, tail, taps, valid, cotangent, bc, run, runT, dt, dtT, mask
    )
    gathered, out_in, grad_in = lax.optimization_barrier((gathered, out_in, grad_in))
    chip = carry_stage(group, gathered)
    chip_second = swap(chip)
    operands = (conv_input, tail, taps, conv_input, tail, taps, valid, cotangent, both, out_in, grad_in)
    first = finish_stage(group, half, operands, chip, other, bc, small, own, partner)
    out, grad, end, borrowed, taps_grad, grads, ends, borroweds, tapss_grad, heads = finish_stage(
        group, other_half, operands, chip_second, other_second, bc, small, own, partner,
        (score_grad, run, dt, sig, sigsum), first,
    )
    groups = lax.axis_size("dp")
    sums, last = total_stage(
        groups * shards // 8, float(groups * shards * ROWS) ** (-0.5), taps_grad, tapss_grad, heads, borrowed, borroweds,
        end, ends, keep,
    )
    weight_grad, bias_grad, dt_bias_grad, a_log_grad, gain_grad, whole_grad = layout_stage(sums, last, grad, grads)
    return (out, whole_grad, weight_grad, bias_grad, dt_bias_grad, a_log_grad, gain_grad)


def solution(mesh):
    sharded = P(("dp", "seq"), None)
    return jax.shard_map(
        on_device,
        mesh=mesh,
        in_specs=(sharded, P(("dp", "seq")), P(), P(), sharded, P(), P(), P(), sharded),
        out_specs=(sharded, sharded, P(), P(), P(), P(), P()),
        check_vma=False,
    )
```

```python
import functools

import jax
import jax.numpy as jnp
from jax import lax
from jax.experimental import pallas as pl
from jax.experimental.pallas import tpu as pltpu
from jax.sharding import PartitionSpec as P

HEADS = 80
HEAD_DIM = 64
STATE = 128
CONV = 4
INNER = 5120
CH = 5376
ROWS = 128
TILE = 512
TILES = INNER // TILE
TILE_HEADS = TILE // HEAD_DIM
LANES = 128

F32 = jnp.float32
BF16 = jnp.bfloat16
EXACT = lax.Precision.HIGHEST
HALF_TILES = TILES // 2
VMEM_BYTES = 20 << 20
CARRY_BYTES = 28 << 20
MESH = pl.DeviceIdType.MESH


def iota(shape, axis):
    return lax.broadcasted_iota(jnp.int32, shape, axis)


def halves(value):
    high = value.astype(BF16)
    return high, (value - high.astype(F32)).astype(BF16)


def mm(a, b):
    return lax.dot_general(a, b, (((1,), (0,)), ((), ())), preferred_element_type=F32)


def mm_nt(a, b):
    return lax.dot_general(a, b, (((1,), (1,)), ((), ())), preferred_element_type=F32)


def exact(a, b):
    return lax.dot_general(
        a, b, (((1,), (0,)), ((), ())), precision=EXACT, preferred_element_type=F32
    )


def spread_exact(rows, one_hot):
    first, rest = rows.astype(BF16), rows
    rest = rest - first.astype(F32)
    second, third = halves(rest)
    return mm(first, one_hot) + mm(second, one_hot) + mm(third, one_hot)


def interleave(group, late):
    row, col = iota((2 * STATE, STATE), 0), iota((2 * STATE, STATE), 1)
    place = row % (2 * group)
    first = group if late else 0
    here = (place >= first) & (place < first + group)
    return jnp.where(here & (col == group * (row // (2 * group)) + place - first), 1.0, 0.0)


def head_columns(tile):
    head, col = iota((LANES, TILE), 0), iota((LANES, TILE), 1)
    return jnp.where(head == TILE_HEADS * tile + col // HEAD_DIM, 1.0, 0.0).astype(BF16)


def spread_heads(both_ref, tile):
    one_hot = head_columns(tile)
    return mm(both_ref[...], jnp.concatenate([one_hot, one_hot], axis=0))


def convolve(tail, rows, taps, valid):
    extended = jnp.concatenate([tail, rows], axis=0)
    total = taps[4:5] + taps[3:4] * rows
    shifted = [rows]
    for back in range(1, CONV):
        moved = extended[8 - back : 8 - back + ROWS] * valid[:, back - 1 : back]
        shifted.append(moved)
        total = total + taps[3 - back : 4 - back] * moved
    return total, shifted


def sigmoid(v):
    return 1.0 / (1.0 + jnp.exp(-v))


def near(k):
    place = lax.axis_index("seq")
    slot = lax.rem(lax.rem(place, 8) + k, 8)
    return (lax.axis_index("dp"), place - lax.rem(place, 8) + slot), slot


def far(k):
    place, group = lax.axis_index("seq"), lax.axis_index("dp")
    runs = lax.axis_size("seq") // 8
    slot = lax.rem(group * runs + place // 8 + k, lax.axis_size("dp") * runs)
    return (slot // runs, lax.rem(slot, runs) * 8 + lax.rem(place, 8)), slot


def send_all(peers, size, source, target, send, receive):
    _, own = peers(0)
    for k in range(1, size):
        peer, slot = peers(k)
        pltpu.make_async_remote_copy(
            src_ref=source(slot), dst_ref=target.at[own], send_sem=send.at[slot], recv_sem=receive.at[own],
            device_id=peer, device_id_type=MESH,
        ).start()


def wait_all(peers, size, source, target, send, receive):
    for k in range(1, size):
        peer, slot = peers(k)
        copy = pltpu.make_async_remote_copy(
            src_ref=source(slot), dst_ref=target.at[slot], send_sem=send.at[slot], recv_sem=receive.at[slot],
            device_id=peer, device_id_type=MESH,
        )
        copy.wait_send()
        copy.wait_recv()


def head_kernel(raw_in_ref, dt_bias_ref, a_log_ref, gain_ref, row_ref, weight_ref, bias_ref, end_ref, run_ref, runT_ref,
                dt_ref, dtT_ref, both_ref, sig_ref, sigsum_ref, mask_ref, valid_ref, keep_ref, tail_ref, own_ref,
                small_ref, taps_ref, raw):
    taps_ref[:CONV, :] = weight_ref[...]
    taps_ref[CONV:, :] = jnp.broadcast_to(bias_ref[...], (8 - CONV, CH))
    small_ref[...] = jnp.zeros_like(small_ref)
    for at, source in enumerate((dt_bias_ref, a_log_ref, gain_ref)):
        small_ref[at : at + 1, :HEADS] = source[...]
    reset_row = row_ref[...].astype(F32)
    token, other = iota((ROWS, ROWS), 0), iota((ROWS, ROWS), 1)
    reset_col = jnp.sum(jnp.where(token == other, reset_row, 0.0), axis=1, keepdims=True)
    low, high = token >= other, token <= other
    segment_col = jnp.sum(jnp.where(low, reset_row, 0.0), axis=1, keepdims=True)
    segment_row = jnp.sum(jnp.where(high, reset_col, 0.0), axis=0, keepdims=True)
    mask_ref[0] = jnp.where(low & (segment_col == segment_row), 1.0, 0.0)
    mask_ref[1] = jnp.where(high & (segment_col == segment_row), 1.0, 0.0)

    kept = jnp.broadcast_to(1.0 - reset_col, (ROWS, LANES))
    one_back = jnp.where(token < 1, 1.0, pltpu.roll(kept, 1, 0))
    two_back = jnp.where(token < 2, 1.0, pltpu.roll(kept, 2, 0))
    valid = jnp.where(other == 0, kept, jnp.where(other == 1, kept * one_back, kept * one_back * two_back))
    valid_ref[...] = valid[:, :8]
    one_on, two_on = pltpu.roll(kept, ROWS - 1, 0), pltpu.roll(kept, ROWS - 2, 0)
    keep = jnp.where(
        token == ROWS - 1, 1.0, jnp.where(token == ROWS - 2, one_on, jnp.where(token == ROWS - 3, one_on * two_on, 0.0))
    )[ROWS - 8 :]
    keep_ref[...] = keep
    tail_ref[...] = (end_ref[8:, :].astype(F32) * keep[:, 0:1]).astype(BF16)

    raw[...] = jnp.zeros_like(raw)
    raw[:HEADS, :] = raw_in_ref[...]
    biased = raw[...].T + small_ref[0:1, :]
    dt = jnp.maximum(biased, 0.0) + jnp.log1p(jnp.exp(-jnp.abs(biased)))
    decay = -jnp.exp(small_ref[1:2, :]) * dt
    lower = jnp.where(low, 1.0, 0.0)
    running = exact(lower, decay)
    last = running[ROWS - 1 : ROWS]
    count = segment_col[ROWS - 1 : ROWS]
    untouched = jnp.where(segment_col == 0.0, 1.0, 0.0)
    entry = jnp.exp(running) * untouched
    own_ref[...] = jnp.broadcast_to(entry[ROWS - 1 : ROWS], own_ref.shape)
    sig = sigmoid(biased)
    sig_ref[...] = sig
    sigsum_ref[...] = exact(lower, sig)
    run_ref[...] = running
    runT_ref[...] = running.T
    dt_ref[...] = dt
    dtT_ref[...] = dt.T
    leave = jnp.exp(last - running) * jnp.where(segment_col == count, 1.0, 0.0) * dt
    for at, part in ((0, leave), (ROWS, entry)):
        first, second = halves(part)
        both_ref[at : at + ROWS, :LANES] = first
        both_ref[at : at + ROWS, LANES:] = second


def head_stage(raw, dt_bias, a_log, gain, row, weight, bias, conv_input):
    square = jax.ShapeDtypeStruct((ROWS, LANES), F32)
    eight = jax.ShapeDtypeStruct((8, LANES), F32)
    shapes = (
        square, square, square, square,
        jax.ShapeDtypeStruct((2 * ROWS, 2 * LANES), BF16),
        square, square,
        jax.ShapeDtypeStruct((2, ROWS, ROWS), F32),
        jax.ShapeDtypeStruct((ROWS, 8), F32),
        eight,
        jax.ShapeDtypeStruct((8, CH), BF16),
        eight, eight,
        jax.ShapeDtypeStruct((8, CH), F32),
    )
    given = (raw, dt_bias, a_log, gain, row, weight, bias)
    return pl.pallas_call(
        head_kernel,
        grid=(1,),
        in_specs=[whole(part.shape) for part in given] + [pl.BlockSpec((16, CH), lambda *at: (ROWS // 16 - 1, 0))],
        out_specs=[whole(part.shape) for part in shapes],
        out_shape=shapes,
        scratch_shapes=[pltpu.VMEM((ROWS, LANES), F32)],
        compiler_params=pltpu.CompilerParams(vmem_limit_bytes=VMEM_BYTES),
        name="heads",
    )(*given, conv_input)


def whole(shape):
    return pl.BlockSpec(shape, lambda *at: (0,) * len(shape))


def call(kernel, name, half, grid, in_specs, out_specs, out_shape, scratch_shapes, operands, aliases={}):
    return pl.pallas_call(
        kernel,
        grid_spec=pltpu.PrefetchScalarGridSpec(
            num_scalar_prefetch=1, grid=(grid,), in_specs=in_specs, out_specs=out_specs, scratch_shapes=scratch_shapes
        ),
        out_shape=out_shape,
        input_output_aliases=aliases,
        compiler_params=pltpu.CompilerParams(vmem_limit_bytes=VMEM_BYTES),
        name=name,
    )(half, *operands)


def tile_at(i, half):
    return lax.rem(i + HALF_TILES * half[0], TILES)


def tile_spec(rows):
    return pl.BlockSpec((rows, TILE), lambda i, half: (0, tile_at(i, half)))


def small_spec(rows):
    return pl.BlockSpec((rows, 2 * STATE), lambda *at: (0, INNER // (2 * STATE)))


def pair_spec(shape, first):
    if first:
        return pl.BlockSpec(shape[:2] + (TILE,), lambda i, half: (0, 0, jnp.minimum(i, HALF_TILES - 1)))
    return pl.BlockSpec(shape[:2] + (TILE,), lambda i, half: (0, 0, jnp.maximum(i - HALF_TILES, 0)))


def local_start(group, xs, tails, tapss, valid, bc_ref, lhs_hi, lhs_lo):
    total, _ = convolve(tails.astype(F32), xs.astype(F32), tapss, valid)
    small = total * sigmoid(total)
    bc_ref[...] = small
    for at, late in ((0, False), (STATE, True)):
        pick = interleave(group, late).astype(BF16)
        first, second = halves(small[:, at : at + STATE])
        lhs_hi[:, at : at + ROWS] = mm_nt(pick, first).astype(BF16)
        lhs_lo[:, at : at + ROWS] = mm_nt(pick, second).astype(BF16)


def local_tile(tile, x_ref, tail_ref, taps_ref, valid_ref, cot_ref, both_ref, lhs_hi, lhs_lo):
    columns = pl.ds(pl.multiple_of(TILE * tile, TILE), TILE)
    total, _ = convolve(
        tail_ref[:, columns].astype(F32), x_ref[:, columns].astype(F32), taps_ref[:, columns], valid_ref[...]
    )
    act = total * sigmoid(total)
    weight = spread_heads(both_ref, tile)
    first, second = halves(weight * jnp.concatenate([act, cot_ref[:, columns].astype(F32)], axis=0))
    return mm(lhs_hi[...], first) + mm(lhs_hi[...], second) + mm(lhs_lo[...], first)


def within_start(bc_ref, mask_ref, score_grad_ref, score, scoreT):
    keys, reads = bc_ref[:, :STATE], bc_ref[:, STATE:]
    keys_hi, keys_lo = halves(keys)
    reads_hi, reads_lo = halves(reads)
    score[...] = mask_ref[0] * (mm_nt(reads_hi, keys_hi) + mm_nt(reads_hi, keys_lo) + mm_nt(reads_lo, keys_hi))
    scoreT[...] = mask_ref[1] * (mm_nt(keys_hi, reads_hi) + mm_nt(keys_hi, reads_lo) + mm_nt(keys_lo, reads_hi))
    score_grad_ref[...] = jnp.zeros_like(score_grad_ref)


def within_tile(tile, x_ref, tail_ref, taps_ref, valid_ref, cot_ref, runT_ref, dtT_ref, out_ref, grad_ref,
                score_grad_ref, score, scoreT):
    at = pl.multiple_of(TILE * tile, TILE)
    columns = pl.ds(at, TILE)
    total, _ = convolve(
        tail_ref[:, columns].astype(F32), x_ref[:, columns].astype(F32), taps_ref[:, columns], valid_ref[...]
    )
    act = total * sigmoid(total)
    rows = pl.ds(pl.multiple_of(TILE_HEADS * tile, TILE_HEADS), TILE_HEADS)
    run_rows, dt_rows = runT_ref[rows, :], dtT_ref[rows, :]
    run, dt = run_rows.T, dt_rows.T
    left = iota((ROWS, LANES), 1) < HEAD_DIM
    left = jnp.where(left, 1.0, 0.0).astype(BF16)
    right = 1.0 - left
    score_grad = score_grad_ref[...]
    for pair in range(TILE_HEADS // 2):
        lanes = slice(LANES * pair, LANES * (pair + 1))
        here = pl.ds(at + LANES * pair, LANES)
        spread, weights, weightsT = [], [], []
        for head in (2 * pair, 2 * pair + 1):
            difference = run[:, head : head + 1] - run_rows[head : head + 1, :]
            step = jnp.exp(jnp.minimum(difference, 0.0)) * dt_rows[head : head + 1, :]
            spread.append(step)
            weights.append(step * score[...])
            weightsT.append(jnp.exp(jnp.minimum(-difference, 0.0)) * dt[:, head : head + 1] * scoreT[...])
        x_hi, x_lo = halves(act[:, lanes])
        upstream = cot_ref[:, here]
        x_hi2 = jnp.concatenate([x_hi * left, x_hi * right], axis=0)
        x_lo2 = jnp.concatenate([x_lo * left, x_lo * right], axis=0)
        upstream2 = jnp.concatenate([upstream * left, upstream * right], axis=0)
        w_hi, w_lo = halves(jnp.concatenate(weights, axis=1))
        wide = mm(w_hi, jnp.concatenate([x_hi2, x_lo2], axis=1))
        out_ref[:, here] = wide[:, :LANES] + wide[:, LANES:] + mm(w_lo, x_hi2)
        wt_hi, wt_lo = halves(jnp.concatenate(weightsT, axis=1))
        grad_ref[:, here] = mm(wt_hi, upstream2) + mm(wt_lo, upstream2)
        inner = mm_nt(upstream2, jnp.concatenate([x_hi, x_lo], axis=0))
        inner = inner[:, :ROWS] + inner[:, ROWS:]
        score_grad = score_grad + inner[:ROWS] * spread[0] + inner[ROWS:] * spread[1]
    score_grad_ref[...] = score_grad


def even_odd(even, both):
    own, partner = both[0:1], both[8:9]
    return jnp.where(even, own, partner)[None], jnp.where(even, partner, own)[None]


ORDER = (10, 1, 4, 3, 12, 11, 9, 14, 6, 2, 8, 5, 15, 7, 13)


def chip_after(k):
    chip = lax.axis_index("seq") // 2
    return lax.rem(chip // 4 + k // 4, 4) * 4 + lax.rem(lax.rem(chip, 4) + k % 4, 4)


def same_core(chip):
    return (lax.axis_index("dp"), 2 * chip + lax.rem(lax.axis_index("seq"), 2))


def chip_copy(source, target, k, slot, send, receive):
    other = chip_after(k)
    slot = other if slot is None else slot
    return pltpu.make_async_remote_copy(
        src_ref=source.at[other], dst_ref=target.at[slot], send_sem=send.at[other], recv_sem=receive.at[slot],
        device_id=same_core(other), device_id_type=MESH,
    )


def pair_copy(source, target, send, receive):
    place = lax.axis_index("seq")
    return pltpu.make_async_remote_copy(
        src_ref=source, dst_ref=target, send_sem=send, recv_sem=receive,
        device_id=(lax.axis_index("dp"), place + 1 - 2 * lax.rem(place, 2)), device_id_type=MESH,
    )


def carry_kernel(group, x_ref, tail_ref, taps_ref, valid_ref, cot_ref, both_ref, own_ref, runT_ref, dtT_ref, mask_ref,
                 chips_ref, others_ref, out_ref, grad_ref, score_grad_ref, bc_ref, partner_ref,
                 mine_ref, theirs_ref, joined, gathered, ready, decay, score, scoreT, lhs_hi, lhs_lo, send, receive,
                 back_send, back_receive, on_send, on_receive, pair_send, pair_receive):
    chips = mine_ref.shape[0]
    place = lax.axis_index("seq")
    chip, core = place // 2, lax.rem(place, 2)
    even = core == 0
    barrier = pltpu.get_barrier_semaphore()
    pl.semaphore_signal(
        barrier, inc=1, device_id=(lax.axis_index("dp"), place + 1 - 2 * core), device_id_type=MESH
    )
    for k in ORDER:
        pl.semaphore_signal(barrier, inc=1, device_id=same_core(chip_after(k)), device_id_type=MESH)
    local_start(
        group, x_ref[:, INNER:], tail_ref[:, INNER:], taps_ref[:, INNER:], valid_ref[...], bc_ref, lhs_hi, lhs_lo
    )

    def local_half(half, target):
        def tile_step(at, carry):
            result = local_tile(
                HALF_TILES * half + at, x_ref, tail_ref, taps_ref, valid_ref, cot_ref, both_ref, lhs_hi, lhs_lo
            )
            target[:, :, pl.ds(pl.multiple_of(TILE * at, TILE), TILE)] = result.reshape(chips, 2 * group, TILE)
            return carry

        lax.fori_loop(0, HALF_TILES, tile_step, 0)

    local_half(1 - core, theirs_ref)
    pl.semaphore_wait(barrier, len(ORDER) + 1)
    swaps = [
        pair_copy(theirs_ref, others_ref.at[0], pair_send.at[0], pair_receive.at[0]),
        pair_copy(own_ref, partner_ref, pair_send.at[1], pair_receive.at[1]),
        pair_copy(mine_ref, others_ref.at[1], pair_send.at[2], pair_receive.at[2]),
    ]
    swaps[0].start()
    swaps[1].start()
    local_half(core, mine_ref)
    swaps[2].start()
    swaps[0].wait_recv()
    swaps[1].wait_recv()
    rows = jnp.concatenate([own_ref[...], partner_ref[...]], axis=0)
    for at in range(HALF_TILES):
        lanes = slice(TILE * at, TILE * (at + 1))
        earlier, later = even_odd(even, spread_exact(rows, head_columns(HALF_TILES * core + at)))
        mine, other = mine_ref[:, :, lanes], others_ref[0, :, :, lanes]
        first, second = jnp.where(even, mine, other), jnp.where(even, other, mine)
        joined[:, :group, lanes] = later * first[:, :group] + second[:, :group]
        joined[:, group:, lanes] = first[:, group:] + earlier * second[:, group:]
    joined[:, :, INNER // 2 :] = jnp.broadcast_to(
        (own_ref[0:1, :] * partner_ref[0:1, :])[None], joined.shape[:2] + (LANES,)
    )
    for k in ORDER:
        chip_copy(joined, gathered, k, chip, send, receive).start()
    gathered[chip] = joined[chip]

    within_start(bc_ref, mask_ref, score_grad_ref, score, scoreT)

    def step(tile, carry):
        within_tile(tile, x_ref, tail_ref, taps_ref, valid_ref, cot_ref, runT_ref, dtT_ref, out_ref, grad_ref,
                    score_grad_ref, score, scoreT)
        return carry

    lax.fori_loop(0, TILES, step, 0)
    score_grad_ref[...] = score_grad_ref[...] * mask_ref[0]

    for k in ORDER:
        copy = chip_copy(joined, gathered, k, None, send, receive)
        copy.wait_send()
        copy.wait_recv()
    by_head = jnp.max(gathered[:, :, INNER // 2 :], axis=1)
    for at in range(HALF_TILES):
        lanes = slice(TILE * at, TILE * (at + 1))
        decay[:, lanes] = spread_exact(by_head, head_columns(HALF_TILES * core + at))
        state = jnp.zeros((group, TILE), F32)
        adjoint = jnp.zeros((group, TILE), F32)
        for here in range(chips):
            ready[here, :group, lanes] = state
            state = decay[here : here + 1, lanes] * state + gathered[here, :group, lanes]
            back = chips - 1 - here
            ready[back, group:, lanes] = adjoint
            adjoint = decay[back : back + 1, lanes] * adjoint + gathered[back, group:, lanes]
    own_half = chips_ref.at[0]
    for k in ORDER:
        chip_copy(ready, own_half, k, chip, back_send, back_receive).start()
    chips_ref[0, chip] = ready[chip]

    def onward(slot):
        return pair_copy(chips_ref.at[0, slot], chips_ref.at[1, slot], on_send.at[slot], on_receive.at[slot])

    onward(chip).start()
    for k in ORDER:
        chip_copy(ready, own_half, k, None, back_send, back_receive).wait_recv()
        onward(chip_after(k)).start()
    for k in ORDER:
        chip_copy(ready, own_half, k, None, back_send, back_receive).wait_send()
    for slot in range(chips):
        copy = onward(slot)
        copy.wait_send()
        copy.wait_recv()
    for copy in swaps:
        copy.wait_send()
    swaps[2].wait_recv()


def carry_stage(group, *operands):
    chips, rows, width = STATE // group, 2 * group, INNER // 2
    wide = jax.ShapeDtypeStruct((ROWS, INNER), F32)
    both = jax.ShapeDtypeStruct((2, chips, rows, width), F32)
    in_vmem = pl.BlockSpec(memory_space=pltpu.VMEM)
    dma = pltpu.SemaphoreType.DMA((chips,))
    three = pltpu.SemaphoreType.DMA((3,))
    half = pltpu.VMEM((chips, rows, width), F32)
    more = pltpu.VMEM((chips, rows, width + LANES), F32)
    square = pltpu.VMEM((ROWS, ROWS), F32)
    lhs = pltpu.VMEM((2 * STATE, 2 * ROWS), BF16)
    shapes = (
        both, both, wide, wide,
        jax.ShapeDtypeStruct((ROWS, ROWS), F32),
        jax.ShapeDtypeStruct((ROWS, 2 * STATE), F32),
        jax.ShapeDtypeStruct((8, LANES), F32),
    )
    return pl.pallas_call(
        functools.partial(carry_kernel, group),
        in_specs=[in_vmem] * len(operands),
        out_specs=[in_vmem] * len(shapes),
        out_shape=shapes,
        scratch_shapes=[
            half, half, more, more, half, pltpu.VMEM((chips, width), F32), square, square, lhs, lhs,
            dma, dma, dma, dma, dma, dma, three, three,
        ],
        compiler_params=pltpu.CompilerParams(vmem_limit_bytes=CARRY_BYTES, collective_id=2, has_side_effects=True),
        name="carry",
    )(*operands)


def conv_backward(grad, shifted, taps, valid):
    width = grad.shape[1]
    zeros = jnp.zeros((8, width), F32)
    total = jnp.concatenate([zeros, grad * taps[3:4]], axis=0)
    parts = [jnp.sum(grad * shifted[0], axis=0, keepdims=True)]
    for back in range(1, CONV):
        parts.insert(0, jnp.sum(grad * shifted[back], axis=0, keepdims=True))
        moved = jnp.concatenate([zeros, grad * valid[:, back - 1 : back] * taps[3 - back : 4 - back], zeros], axis=0)
        total = total + moved[back : back + ROWS + 8]
    parts.append(jnp.sum(grad, axis=0, keepdims=True))
    parts.append(jnp.zeros((3, width), F32))
    return total, jnp.concatenate(parts, axis=0)


def finish_kernel(group, half_ref, x_ref, tail_ref, taps_ref, xs_ref, tails_ref, tapss_ref, valid_ref, cot_ref, both_ref,
                  out_in_ref, grad_in_ref, chip_ref, local_ref, bc_ref, small_ref, own_ref, partner_ref, score_grad_ref,
                  run_ref, dt_ref, sig_ref, sigsum_ref,
                  out_ref, grad_ref, end_ref, borrowed_ref, taps_grad_ref, grads_ref, ends_ref, borroweds_ref,
                  tapss_grad_ref, heads_ref,
                  lhs_hi, lhs_lo, bc_grad, by_head, by_token):
    tile = pl.program_id(0)
    valid = valid_ref[...]

    @pl.when(tile == 0)
    def _():
        for at, source, late in ((0, STATE, False), (ROWS, 0, True)):
            pick = interleave(group, late).astype(BF16)
            first, second = halves(bc_ref[:, source : source + STATE])
            lhs_hi[at : at + ROWS, :] = mm_nt(first, pick).astype(BF16)
            lhs_lo[at : at + ROWS, :] = mm_nt(second, pick).astype(BF16)
        bc_grad[...] = jnp.zeros_like(bc_grad)
        by_head[...] = jnp.zeros_like(by_head)
        by_token[...] = jnp.zeros_like(by_token)

    total, shifted = convolve(tail_ref[...].astype(F32), x_ref[...].astype(F32), taps_ref[...], valid)
    gate = sigmoid(total)
    act = total * gate
    upstream = cot_ref[...].astype(F32)
    here = tile_at(tile, half_ref)
    weight = spread_heads(both_ref, here)
    leave, entry = weight[:ROWS], weight[ROWS:]
    by_row = spread_exact(
        jnp.concatenate([own_ref[...], partner_ref[...], small_ref[...]], axis=0), head_columns(here)
    )
    even = half_ref[2] == 0
    earlier, later = even_odd(even, by_row)
    weight_state, weight_adjoint = jnp.where(even, 1.0, earlier), jnp.where(even, later, 1.0)
    with_state, with_adjoint = jnp.where(even, 0.0, 1.0), jnp.where(even, 1.0, 0.0)
    states = jnp.concatenate(
        [
            weight_state * chip_ref[:, :group, :] + with_state * local_ref[:, :group, :],
            weight_adjoint * chip_ref[:, group:, :] + with_adjoint * local_ref[:, group:, :],
        ],
        axis=1,
    ).reshape(2 * STATE, TILE)
    states_hi, states_lo = halves(states)
    read = mm(lhs_hi[...], states_hi) + mm(lhs_hi[...], states_lo) + mm(lhs_lo[...], states_hi)
    one_hot = head_columns(here)
    gain = by_row[18:19]
    through_state = out_in_ref[...] + entry * read[:ROWS]
    out_ref[...] = (through_state + gain * act).astype(BF16)
    act_grad_late = leave * read[ROWS:]
    act_grad = grad_in_ref[...] + act_grad_late

    first, second = halves(jnp.concatenate([entry * upstream, leave * act], axis=0))
    bc_grad[...] += mm_nt(first, states_hi) + mm_nt(first, states_lo) + mm_nt(second, states_hi)

    first, second = halves(jnp.concatenate([upstream * through_state, act * act_grad], axis=0))
    by_token[...] += mm_nt(first, one_hot) + mm_nt(second, one_hot)
    crossed = states * pltpu.roll(states, group, 0)
    crossed = jnp.where(iota((2 * STATE, TILE), 0) % (2 * group) >= group, crossed, 0.0)
    sums = jnp.concatenate(
        [
            jnp.sum(act * act_grad_late, axis=0, keepdims=True),
            jnp.sum(crossed, axis=0, keepdims=True),
            jnp.sum(upstream * act, axis=0, keepdims=True),
            jnp.zeros((5, TILE), F32),
        ],
        axis=0,
    )
    by_head[...] += lax.dot_general(
        sums, one_hot.astype(F32), (((1,), (1,)), ((), ())), precision=EXACT, preferred_element_type=F32
    )

    act_grad = act_grad + gain * upstream
    conv_grad = act_grad * (gate + act * (1.0 - gate))
    full, taps_grad_ref[...] = conv_backward(conv_grad, shifted, taps_ref[...], valid)
    borrowed_ref[...] = full[:8]
    grad_ref[...] = full[8:].astype(BF16)
    end_ref[...] = full[ROWS - 8 :]

    @pl.when(tile == TILES - 1)
    def _():
        score_grad = score_grad_ref[...]
        keys, reads = bc_ref[:, :STATE], bc_ref[:, STATE:]
        reads_grad = exact(bc_grad[:ROWS], interleave(group, False)) + exact(score_grad, keys)
        keys_grad = exact(bc_grad[ROWS:], interleave(group, True)) + exact(score_grad.T, reads)
        total, shifted = convolve(tails_ref[...].astype(F32), xs_ref[...].astype(F32), tapss_ref[...], valid)
        gate = sigmoid(total)
        small_grad = jnp.concatenate([keys_grad, reads_grad], axis=1) * (gate + total * gate * (1.0 - gate))
        full, tapss_grad_ref[...] = conv_backward(small_grad, shifted, tapss_ref[...], valid)
        borroweds_ref[...] = full[:8]
        grads_ref[...] = full[8:].astype(BF16)
        ends_ref[...] = full[ROWS - 8 :]

        read_sum, added_sum = by_token[:ROWS], by_token[ROWS:]
        at_end = by_head[0:1, :] + own_ref[0:1, :] * by_head[1:2, :]
        run_grad = read_sum - added_sum + jnp.where(iota((ROWS, LANES), 0) == ROWS - 1, at_end, 0.0)
        alog_grad = jnp.sum(run_grad * run_ref[...], axis=0, keepdims=True)
        bias_grad = jnp.sum(added_sum / dt_ref[...] * sig_ref[...], axis=0, keepdims=True)
        rate = jnp.exp(small_ref[1:2, :])
        bias_grad = bias_grad - rate * jnp.sum(run_grad * sigsum_ref[...], axis=0, keepdims=True)
        heads_ref[...] = jnp.concatenate([bias_grad, alog_grad, by_head[2:3, :], jnp.zeros((5, LANES), F32)], axis=0)


def finish_stage(group, half, *operands):
    square = whole((ROWS, LANES))
    eight = whole((8, LANES))
    shapes = (
        jax.ShapeDtypeStruct((ROWS, INNER), BF16),
        jax.ShapeDtypeStruct((ROWS, INNER), BF16),
        jax.ShapeDtypeStruct((16, INNER), F32),
        jax.ShapeDtypeStruct((8, INNER), F32),
        jax.ShapeDtypeStruct((8, INNER), F32),
        jax.ShapeDtypeStruct((ROWS, 2 * STATE), BF16),
        jax.ShapeDtypeStruct((16, 2 * STATE), F32),
        jax.ShapeDtypeStruct((8, 2 * STATE), F32),
        jax.ShapeDtypeStruct((8, 2 * STATE), F32),
        jax.ShapeDtypeStruct((8, LANES), F32),
    )
    states = pl.BlockSpec(
        (None, STATE // group, 2 * group, TILE), lambda i, half: (i // HALF_TILES, 0, 0, lax.rem(i, HALF_TILES))
    )
    return call(
        functools.partial(finish_kernel, group), "finish", half, TILES,
        [
            tile_spec(ROWS), tile_spec(8), tile_spec(8),
            small_spec(ROWS), small_spec(8), small_spec(8),
            whole((ROWS, 8)), tile_spec(ROWS), whole((2 * ROWS, 2 * LANES)),
            tile_spec(ROWS), tile_spec(ROWS), states, states,
            whole((ROWS, 2 * STATE)), eight, eight, eight, whole((ROWS, ROWS)), square, square, square, square,
        ],
        [tile_spec(part.shape[0]) for part in shapes[:5]] + [whole(part.shape) for part in shapes[5:]],
        shapes,
        [
            pltpu.VMEM((2 * ROWS, 2 * STATE), BF16), pltpu.VMEM((2 * ROWS, 2 * STATE), BF16),
            pltpu.VMEM((2 * ROWS, 2 * STATE), F32), pltpu.VMEM((8, LANES), F32), pltpu.VMEM((2 * ROWS, LANES), F32),
        ],
        operands,
    )


def total_kernel(scale, taps_ref, small_ref, heads_ref, borrowed_ref, borroweds_ref, end_ref, ends_ref, keep_ref,
                 sums_ref, last_ref,
                 parts, slots, piece, far_slots, result, got, got_small, send, receive, far_send, far_receive, back_send,
                 back_receive, rows_send, rows_receive):
    shards, groups = lax.axis_size("seq"), lax.axis_size("dp")
    others = groups * shards // 8
    place, group = lax.axis_index("seq"), lax.axis_index("dp")
    before = (group, lax.rem(place + shards - 1, shards))
    after = (group, lax.rem(place + 1, shards))
    barrier = pltpu.get_barrier_semaphore()
    for peers, size in ((near, 8), (far, others)):
        for k in range(1, size):
            pl.semaphore_signal(barrier, inc=1, device_id=peers(k)[0], device_id_type=MESH)
    for peer in (before, after):
        pl.semaphore_signal(barrier, inc=1, device_id=peer, device_id_type=MESH)
    pl.semaphore_wait(barrier, 7 + others - 1 + 2)

    depth = parts.shape[1]
    wide = CH // LANES
    for at in range(8 * depth // 8):
        if at < INNER // LANES:
            block = taps_ref[:, LANES * at : LANES * (at + 1)]
        elif at < wide:
            block = small_ref[:, LANES * at - INNER : LANES * (at + 1) - INNER]
        elif at == wide:
            block = heads_ref[...]
        else:
            block = jnp.zeros((8, LANES), F32)
        parts[at % 8, 8 * (at // 8) : 8 * (at // 8) + 8, :] = block
    send_all(near, 8, lambda slot: parts.at[slot], slots, send, receive)
    returns = [
        pltpu.make_async_remote_copy(
            src_ref=source, dst_ref=target, send_sem=rows_send.at[at], recv_sem=rows_receive.at[at], device_id=before,
            device_id_type=MESH,
        )
        for at, (source, target) in enumerate(((borrowed_ref, got), (borroweds_ref, got_small)))
    ]

    @pl.when(place > 0)
    def _():
        for copy in returns:
            copy.start()

    _, own = near(0)
    _, far_own = far(0)
    slots[own] = parts[own]
    wait_all(near, 8, lambda slot: parts.at[slot], slots, send, receive)
    piece[...] = jnp.sum(slots[...], axis=0)
    send_all(far, others, lambda slot: piece, far_slots, far_send, far_receive)
    far_slots[far_own] = piece[...]
    wait_all(far, others, lambda slot: piece, far_slots, far_send, far_receive)
    piece[...] = jnp.sum(far_slots[...], axis=0) * scale
    send_all(near, 8, lambda slot: piece, result, back_send, back_receive)
    result[own] = piece[...]

    @pl.when(place > 0)
    def _():
        for copy in returns:
            copy.wait_send()

    @pl.when(place < shards - 1)
    def _():
        for copy in returns:
            copy.wait_recv()
        keep = keep_ref[:, 0:1]
        for lanes, source, end in ((slice(0, INNER), got, end_ref), (slice(INNER, CH), got_small, ends_ref)):
            late = iota(source.shape, 0) >= 8 - CONV + 1
            rows = jnp.concatenate([end[:8, :], end[8:, :] + jnp.where(late, source[...] * keep, 0.0)], axis=0)
            last_ref[:, lanes] = rows.astype(BF16)

    @pl.when(place == shards - 1)
    def _():
        last_ref[:, :INNER] = end_ref[...].astype(BF16)
        last_ref[:, INNER:] = ends_ref[...].astype(BF16)

    wait_all(near, 8, lambda slot: piece, result, back_send, back_receive)
    for at in range(wide + 1):
        sums_ref[:, LANES * at : LANES * (at + 1)] = result[at % 8, 8 * (at // 8) : 8 * (at // 8) + 8, :]


def layout_kernel(sums_ref, last_ref, grad_ref, grads_ref, weight_ref, bias_ref, dt_bias_ref, a_log_ref, gain_ref,
                  whole_ref):
    step = pl.program_id(0)

    @pl.when(step == 0)
    def _():
        weight_ref[...] = sums_ref[:CONV, :CH]
        bias_ref[...] = sums_ref[CONV : CONV + 1, :CH].reshape(CH)
        for at, target in enumerate((dt_bias_ref, a_log_ref, gain_ref)):
            target[...] = sums_ref[at : at + 1, CH : CH + HEADS].reshape(HEADS)

    @pl.when(step < pl.num_programs(0) - 1)
    def _():
        whole_ref[:, :INNER] = grad_ref[...]
        whole_ref[:, INNER:] = grads_ref[...]

    @pl.when(step == pl.num_programs(0) - 1)
    def _():
        whole_ref[: whole_ref.shape[0] - 16, :INNER] = grad_ref[: whole_ref.shape[0] - 16, :]
        whole_ref[: whole_ref.shape[0] - 16, INNER:] = grads_ref[: whole_ref.shape[0] - 16, :]
        whole_ref[whole_ref.shape[0] - 16 :, :] = last_ref[...]


def layout_stage(sums, last, grad, grads):
    rows = 32
    shapes = (
        jax.ShapeDtypeStruct((CONV, CH), F32),
        jax.ShapeDtypeStruct((CH,), F32),
        jax.ShapeDtypeStruct((HEADS,), F32),
        jax.ShapeDtypeStruct((HEADS,), F32),
        jax.ShapeDtypeStruct((HEADS,), F32),
        jax.ShapeDtypeStruct((ROWS, CH), BF16),
    )
    blocks = [pl.BlockSpec((rows, width), lambda i: (i, 0)) for width in (INNER, 2 * STATE, CH)]
    return pl.pallas_call(
        layout_kernel,
        grid=(ROWS // rows,),
        in_specs=[whole(sums.shape), whole(last.shape)] + blocks[:2],
        out_specs=[whole(part.shape) for part in shapes[:5]] + blocks[2:],
        out_shape=shapes,
        name="layout",
    )(sums, last, grad, grads)


def total_stage(others, scale, *operands):
    depth = 8 * pl.cdiv(CH // LANES + 1, 8)
    in_vmem = pl.BlockSpec(memory_space=pltpu.VMEM)
    shapes = (jax.ShapeDtypeStruct((8, CH + LANES), F32), jax.ShapeDtypeStruct((16, CH), BF16))
    dma = pltpu.SemaphoreType.DMA
    return pl.pallas_call(
        functools.partial(total_kernel, scale),
        in_specs=[in_vmem] * len(operands),
        out_specs=[in_vmem] * len(shapes),
        out_shape=shapes,
        scratch_shapes=[
            pltpu.VMEM((8, depth, LANES), F32), pltpu.VMEM((8, depth, LANES), F32),
            pltpu.VMEM((depth, LANES), F32), pltpu.VMEM((others, depth, LANES), F32),
            pltpu.VMEM((8, depth, LANES), F32),
            pltpu.VMEM((8, INNER), F32), pltpu.VMEM((8, 2 * STATE), F32),
            dma((8,)), dma((8,)), dma((others,)), dma((others,)), dma((8,)), dma((8,)), dma((2,)), dma((2,)),
        ],
        compiler_params=pltpu.CompilerParams(
            vmem_limit_bytes=VMEM_BYTES, collective_id=1, has_side_effects=True
        ),
        name="totals",
    )(*operands)


def on_device(conv_input, doc_start, conv_weight, conv_bias, dt_raw, dt_bias, a_log, skip_gain, cotangent):
    shards, place = lax.axis_size("seq"), lax.axis_index("seq")
    group = 2 * STATE // shards
    core = lax.rem(place, 2)
    half = jnp.stack([core, place // 2, core])
    run, runT, dt, dtT, both, sig, sigsum, mask, valid, keep, tail, own, small, taps = head_stage(
        dt_raw.T, dt_bias[None], a_log[None], skip_gain[None], doc_start[None], conv_weight, conv_bias[None], conv_input
    )
    tail = lax.ppermute(tail, "seq", [(i, i + 1) for i in range(shards - 1)])
    chips, others, out_in, grad_in, score_grad, bc, partner = carry_stage(
        group, conv_input, tail, taps, valid, cotangent, both, own, runT, dtT, mask
    )
    out, grad, end, borrowed, taps_grad, grads, ends, borroweds, tapss_grad, heads = finish_stage(
        group, half, conv_input, tail, taps, conv_input, tail, taps, valid, cotangent, both, out_in, grad_in, chips,
        others, bc, small, own, partner, score_grad, run, dt, sig, sigsum,
    )
    groups = lax.axis_size("dp")
    sums, last = total_stage(
        groups * shards // 8, float(groups * shards * ROWS) ** (-0.5), taps_grad, tapss_grad, heads, borrowed, borroweds,
        end, ends, keep,
    )
    weight_grad, bias_grad, dt_bias_grad, a_log_grad, gain_grad, whole_grad = layout_stage(sums, last, grad, grads)
    return (out, whole_grad, weight_grad, bias_grad, dt_bias_grad, a_log_grad, gain_grad)


def solution(mesh):
    sharded = P(("dp", "seq"), None)
    return jax.shard_map(
        on_device,
        mesh=mesh,
        in_specs=(sharded, P(("dp", "seq")), P(), P(), sharded, P(), P(), P(), sharded),
        out_specs=(sharded, sharded, P(), P(), P(), P(), P()),
        check_vma=False,
    )
```

```python
import functools

import jax
import jax.numpy as jnp
from jax import lax
from jax.experimental import pallas as pl
from jax.experimental.pallas import tpu as pltpu
from jax.sharding import PartitionSpec as P

HEADS = 80
HEAD_DIM = 64
STATE = 128
CONV = 4
INNER = 5120
CH = 5376
ROWS = 128
TILE = 512
TILES = INNER // TILE
TILE_HEADS = TILE // HEAD_DIM
LANES = 128

F32 = jnp.float32
BF16 = jnp.bfloat16
EXACT = lax.Precision.HIGHEST
HALF_TILES = TILES // 2
VMEM_BYTES = 20 << 20
CARRY_BYTES = 28 << 20
MESH = pl.DeviceIdType.MESH


def iota(shape, axis):
    return lax.broadcasted_iota(jnp.int32, shape, axis)


def halves(value):
    high = value.astype(BF16)
    return high, (value - high.astype(F32)).astype(BF16)


def mm(a, b):
    return lax.dot_general(a, b, (((1,), (0,)), ((), ())), preferred_element_type=F32)


def mm_nt(a, b):
    return lax.dot_general(a, b, (((1,), (1,)), ((), ())), preferred_element_type=F32)


def exact(a, b):
    return lax.dot_general(
        a, b, (((1,), (0,)), ((), ())), precision=EXACT, preferred_element_type=F32
    )


def spread_exact(rows, one_hot):
    first, rest = rows.astype(BF16), rows
    rest = rest - first.astype(F32)
    second, third = halves(rest)
    return mm(first, one_hot) + mm(second, one_hot) + mm(third, one_hot)


def interleave(group, late):
    row, col = iota((2 * STATE, STATE), 0), iota((2 * STATE, STATE), 1)
    place = row % (2 * group)
    first = group if late else 0
    here = (place >= first) & (place < first + group)
    return jnp.where(here & (col == group * (row // (2 * group)) + place - first), 1.0, 0.0)


def head_columns(tile):
    head, col = iota((LANES, TILE), 0), iota((LANES, TILE), 1)
    return jnp.where(head == TILE_HEADS * tile + col // HEAD_DIM, 1.0, 0.0).astype(BF16)


def spread_heads(both_ref, tile):
    one_hot = head_columns(tile)
    return mm(both_ref[...], jnp.concatenate([one_hot, one_hot], axis=0))


def convolve(tail, rows, taps, valid):
    extended = jnp.concatenate([tail, rows], axis=0)
    total = taps[4:5] + taps[3:4] * rows
    shifted = [rows]
    for back in range(1, CONV):
        moved = extended[8 - back : 8 - back + ROWS] * valid[:, back - 1 : back]
        shifted.append(moved)
        total = total + taps[3 - back : 4 - back] * moved
    return total, shifted


def sigmoid(v):
    return 1.0 / (1.0 + jnp.exp(-v))


def near(k):
    place = lax.axis_index("seq")
    slot = lax.rem(lax.rem(place, 8) + k, 8)
    return (lax.axis_index("dp"), place - lax.rem(place, 8) + slot), slot


def far(k):
    place, group = lax.axis_index("seq"), lax.axis_index("dp")
    runs = lax.axis_size("seq") // 8
    slot = lax.rem(group * runs + place // 8 + k, lax.axis_size("dp") * runs)
    return (slot // runs, lax.rem(slot, runs) * 8 + lax.rem(place, 8)), slot


def send_all(peers, size, source, target, send, receive):
    _, own = peers(0)
    for k in range(1, size):
        peer, slot = peers(k)
        pltpu.make_async_remote_copy(
            src_ref=source(slot), dst_ref=target.at[own], send_sem=send.at[slot], recv_sem=receive.at[own],
            device_id=peer, device_id_type=MESH,
        ).start()


def wait_all(peers, size, source, target, send, receive):
    for k in range(1, size):
        peer, slot = peers(k)
        copy = pltpu.make_async_remote_copy(
            src_ref=source(slot), dst_ref=target.at[slot], send_sem=send.at[slot], recv_sem=receive.at[slot],
            device_id=peer, device_id_type=MESH,
        )
        copy.wait_send()
        copy.wait_recv()


def head_kernel(raw_in_ref, dt_bias_ref, a_log_ref, gain_ref, row_ref, weight_ref, bias_ref, end_ref, run_ref, runT_ref,
                dt_ref, dtT_ref, both_ref, sig_ref, sigsum_ref, mask_ref, valid_ref, keep_ref, tail_ref, own_ref,
                small_ref, taps_ref, raw):
    taps_ref[:CONV, :] = weight_ref[...]
    taps_ref[CONV:, :] = jnp.broadcast_to(bias_ref[...], (8 - CONV, CH))
    small_ref[...] = jnp.zeros_like(small_ref)
    for at, source in enumerate((dt_bias_ref, a_log_ref, gain_ref)):
        small_ref[at : at + 1, :HEADS] = source[...]
    reset_row = row_ref[...].astype(F32)
    token, other = iota((ROWS, ROWS), 0), iota((ROWS, ROWS), 1)
    reset_col = jnp.sum(jnp.where(token == other, reset_row, 0.0), axis=1, keepdims=True)
    low, high = token >= other, token <= other
    segment_col = jnp.sum(jnp.where(low, reset_row, 0.0), axis=1, keepdims=True)
    segment_row = jnp.sum(jnp.where(high, reset_col, 0.0), axis=0, keepdims=True)
    mask_ref[0] = jnp.where(low & (segment_col == segment_row), 1.0, 0.0)
    mask_ref[1] = jnp.where(high & (segment_col == segment_row), 1.0, 0.0)

    kept = jnp.broadcast_to(1.0 - reset_col, (ROWS, LANES))
    one_back = jnp.where(token < 1, 1.0, pltpu.roll(kept, 1, 0))
    two_back = jnp.where(token < 2, 1.0, pltpu.roll(kept, 2, 0))
    valid = jnp.where(other == 0, kept, jnp.where(other == 1, kept * one_back, kept * one_back * two_back))
    valid_ref[...] = valid[:, :8]
    one_on, two_on = pltpu.roll(kept, ROWS - 1, 0), pltpu.roll(kept, ROWS - 2, 0)
    keep = jnp.where(
        token == ROWS - 1, 1.0, jnp.where(token == ROWS - 2, one_on, jnp.where(token == ROWS - 3, one_on * two_on, 0.0))
    )[ROWS - 8 :]
    keep_ref[...] = keep
    tail_ref[...] = (end_ref[8:, :].astype(F32) * keep[:, 0:1]).astype(BF16)

    raw[...] = jnp.zeros_like(raw)
    raw[:HEADS, :] = raw_in_ref[...]
    biased = raw[...].T + small_ref[0:1, :]
    dt = jnp.maximum(biased, 0.0) + jnp.log1p(jnp.exp(-jnp.abs(biased)))
    decay = -jnp.exp(small_ref[1:2, :]) * dt
    lower = jnp.where(low, 1.0, 0.0)
    running = exact(lower, decay)
    last = running[ROWS - 1 : ROWS]
    count = segment_col[ROWS - 1 : ROWS]
    untouched = jnp.where(segment_col == 0.0, 1.0, 0.0)
    entry = jnp.exp(running) * untouched
    own_ref[...] = jnp.broadcast_to(entry[ROWS - 1 : ROWS], own_ref.shape)
    sig = sigmoid(biased)
    sig_ref[...] = sig
    sigsum_ref[...] = exact(lower, sig)
    run_ref[...] = running
    runT_ref[...] = running.T
    dt_ref[...] = dt
    dtT_ref[...] = dt.T
    leave = jnp.exp(last - running) * jnp.where(segment_col == count, 1.0, 0.0) * dt
    for at, part in ((0, leave), (ROWS, entry)):
        first, second = halves(part)
        both_ref[at : at + ROWS, :LANES] = first
        both_ref[at : at + ROWS, LANES:] = second


def head_stage(raw, dt_bias, a_log, gain, row, weight, bias, conv_input):
    square = jax.ShapeDtypeStruct((ROWS, LANES), F32)
    eight = jax.ShapeDtypeStruct((8, LANES), F32)
    shapes = (
        square, square, square, square,
        jax.ShapeDtypeStruct((2 * ROWS, 2 * LANES), BF16),
        square, square,
        jax.ShapeDtypeStruct((2, ROWS, ROWS), F32),
        jax.ShapeDtypeStruct((ROWS, 8), F32),
        eight,
        jax.ShapeDtypeStruct((8, CH), BF16),
        eight, eight,
        jax.ShapeDtypeStruct((8, CH), F32),
    )
    given = (raw, dt_bias, a_log, gain, row, weight, bias)
    return pl.pallas_call(
        head_kernel,
        grid=(1,),
        in_specs=[whole(part.shape) for part in given] + [pl.BlockSpec((16, CH), lambda *at: (ROWS // 16 - 1, 0))],
        out_specs=[whole(part.shape) for part in shapes],
        out_shape=shapes,
        scratch_shapes=[pltpu.VMEM((ROWS, LANES), F32)],
        compiler_params=pltpu.CompilerParams(vmem_limit_bytes=VMEM_BYTES),
        name="heads",
    )(*given, conv_input)


def whole(shape):
    return pl.BlockSpec(shape, lambda *at: (0,) * len(shape))


def call(kernel, name, half, grid, in_specs, out_specs, out_shape, scratch_shapes, operands, aliases={}):
    return pl.pallas_call(
        kernel,
        grid_spec=pltpu.PrefetchScalarGridSpec(
            num_scalar_prefetch=1, grid=(grid,), in_specs=in_specs, out_specs=out_specs, scratch_shapes=scratch_shapes
        ),
        out_shape=out_shape,
        input_output_aliases=aliases,
        compiler_params=pltpu.CompilerParams(vmem_limit_bytes=VMEM_BYTES),
        name=name,
    )(half, *operands)


def tile_at(i, half):
    return lax.rem(i + HALF_TILES * half[0], TILES)


def tile_spec(rows):
    return pl.BlockSpec((rows, TILE), lambda i, half: (0, tile_at(i, half)))


def small_spec(rows):
    return pl.BlockSpec((rows, 2 * STATE), lambda *at: (0, INNER // (2 * STATE)))


def pair_spec(shape, first):
    if first:
        return pl.BlockSpec(shape[:2] + (TILE,), lambda i, half: (0, 0, jnp.minimum(i, HALF_TILES - 1)))
    return pl.BlockSpec(shape[:2] + (TILE,), lambda i, half: (0, 0, jnp.maximum(i - HALF_TILES, 0)))


def local_start(group, xs, tails, tapss, valid, bc_ref, lhs_hi, lhs_lo):
    total, _ = convolve(tails.astype(F32), xs.astype(F32), tapss, valid)
    small = total * sigmoid(total)
    bc_ref[...] = small
    for at, late in ((0, False), (STATE, True)):
        pick = interleave(group, late).astype(BF16)
        first, second = halves(small[:, at : at + STATE])
        lhs_hi[:, at : at + ROWS] = mm_nt(pick, first).astype(BF16)
        lhs_lo[:, at : at + ROWS] = mm_nt(pick, second).astype(BF16)


def local_tile(tile, x_ref, tail_ref, taps_ref, valid_ref, cot_ref, both_ref, lhs_hi, lhs_lo):
    columns = pl.ds(pl.multiple_of(TILE * tile, TILE), TILE)
    total, _ = convolve(
        tail_ref[:, columns].astype(F32), x_ref[:, columns].astype(F32), taps_ref[:, columns], valid_ref[...]
    )
    act = total * sigmoid(total)
    weight = spread_heads(both_ref, tile)
    first, second = halves(weight * jnp.concatenate([act, cot_ref[:, columns].astype(F32)], axis=0))
    return mm(lhs_hi[...], first) + mm(lhs_hi[...], second) + mm(lhs_lo[...], first)


def within_start(bc_ref, mask_ref, score_grad_ref, score, scoreT):
    keys, reads = bc_ref[:, :STATE], bc_ref[:, STATE:]
    keys_hi, keys_lo = halves(keys)
    reads_hi, reads_lo = halves(reads)
    score[...] = mask_ref[0] * (mm_nt(reads_hi, keys_hi) + mm_nt(reads_hi, keys_lo) + mm_nt(reads_lo, keys_hi))
    scoreT[...] = mask_ref[1] * (mm_nt(keys_hi, reads_hi) + mm_nt(keys_hi, reads_lo) + mm_nt(keys_lo, reads_hi))
    score_grad_ref[...] = jnp.zeros_like(score_grad_ref)


def within_tile(tile, x_ref, tail_ref, taps_ref, valid_ref, cot_ref, runT_ref, dtT_ref, out_ref, grad_ref,
                score_grad_ref, score, scoreT):
    at = pl.multiple_of(TILE * tile, TILE)
    columns = pl.ds(at, TILE)
    total, _ = convolve(
        tail_ref[:, columns].astype(F32), x_ref[:, columns].astype(F32), taps_ref[:, columns], valid_ref[...]
    )
    act = total * sigmoid(total)
    rows = pl.ds(pl.multiple_of(TILE_HEADS * tile, TILE_HEADS), TILE_HEADS)
    run_rows, dt_rows = runT_ref[rows, :], dtT_ref[rows, :]
    run, dt = run_rows.T, dt_rows.T
    left = iota((ROWS, LANES), 1) < HEAD_DIM
    left = jnp.where(left, 1.0, 0.0).astype(BF16)
    right = 1.0 - left
    score_grad = score_grad_ref[...]
    for pair in range(TILE_HEADS // 2):
        lanes = slice(LANES * pair, LANES * (pair + 1))
        here = pl.ds(at + LANES * pair, LANES)
        spread, weights, weightsT = [], [], []
        for head in (2 * pair, 2 * pair + 1):
            difference = run[:, head : head + 1] - run_rows[head : head + 1, :]
            step = jnp.exp(jnp.minimum(difference, 0.0)) * dt_rows[head : head + 1, :]
            spread.append(step)
            weights.append(step * score[...])
            weightsT.append(jnp.exp(jnp.minimum(-difference, 0.0)) * dt[:, head : head + 1] * scoreT[...])
        x_hi, x_lo = halves(act[:, lanes])
        upstream = cot_ref[:, here]
        x_hi2 = jnp.concatenate([x_hi * left, x_hi * right], axis=0)
        x_lo2 = jnp.concatenate([x_lo * left, x_lo * right], axis=0)
        upstream2 = jnp.concatenate([upstream * left, upstream * right], axis=0)
        w_hi, w_lo = halves(jnp.concatenate(weights, axis=1))
        wide = mm(w_hi, jnp.concatenate([x_hi2, x_lo2], axis=1))
        out_ref[:, here] = wide[:, :LANES] + wide[:, LANES:] + mm(w_lo, x_hi2)
        wt_hi, wt_lo = halves(jnp.concatenate(weightsT, axis=1))
        grad_ref[:, here] = mm(wt_hi, upstream2) + mm(wt_lo, upstream2)
        inner = mm_nt(upstream2, jnp.concatenate([x_hi, x_lo], axis=0))
        inner = inner[:, :ROWS] + inner[:, ROWS:]
        score_grad = score_grad + inner[:ROWS] * spread[0] + inner[ROWS:] * spread[1]
    score_grad_ref[...] = score_grad


def even_odd(even, both):
    own, partner = both[0:1], both[8:9]
    return jnp.where(even, own, partner)[None], jnp.where(even, partner, own)[None]


ORDER = (10, 1, 4, 3, 12, 11, 9, 14, 6, 2, 8, 5, 15, 7, 13)


def chip_after(k):
    chip = lax.axis_index("seq") // 2
    return lax.rem(chip // 4 + k // 4, 4) * 4 + lax.rem(lax.rem(chip, 4) + k % 4, 4)


def same_core(chip):
    return (lax.axis_index("dp"), 2 * chip + lax.rem(lax.axis_index("seq"), 2))


def chip_copy(source, target, k, slot, send, receive):
    other = chip_after(k)
    slot = other if slot is None else slot
    return pltpu.make_async_remote_copy(
        src_ref=source(other), dst_ref=target(slot), send_sem=send.at[other], recv_sem=receive.at[slot],
        device_id=same_core(other), device_id_type=MESH,
    )


PIECES = ((0, 2), (2, 5))


def pair_copy(source, target, send, receive):
    place = lax.axis_index("seq")
    return pltpu.make_async_remote_copy(
        src_ref=source, dst_ref=target, send_sem=send, recv_sem=receive,
        device_id=(lax.axis_index("dp"), place + 1 - 2 * lax.rem(place, 2)), device_id_type=MESH,
    )


def carry_kernel(group, x_ref, tail_ref, taps_ref, valid_ref, cot_ref, both_ref, own_ref, runT_ref, dtT_ref, mask_ref,
                 chips_ref, others_ref, out_ref, grad_ref, score_grad_ref, bc_ref, partner_ref,
                 mine_ref, theirs_ref, joined, gathered, ready, decay, score, scoreT, lhs_hi, lhs_lo, send, receive,
                 back_send, back_receive, on_send, on_receive, pair_send, pair_receive):
    chips = mine_ref.shape[0]
    place = lax.axis_index("seq")
    chip, core = place // 2, lax.rem(place, 2)
    even = core == 0
    barrier = pltpu.get_barrier_semaphore()
    pl.semaphore_signal(
        barrier, inc=1, device_id=(lax.axis_index("dp"), place + 1 - 2 * core), device_id_type=MESH
    )
    for k in ORDER:
        pl.semaphore_signal(barrier, inc=1, device_id=same_core(chip_after(k)), device_id_type=MESH)
    local_start(
        group, x_ref[:, INNER:], tail_ref[:, INNER:], taps_ref[:, INNER:], valid_ref[...], bc_ref, lhs_hi, lhs_lo
    )

    def local_piece(half, piece, target):
        def tile_step(at, carry):
            result = local_tile(
                HALF_TILES * half + at, x_ref, tail_ref, taps_ref, valid_ref, cot_ref, both_ref, lhs_hi, lhs_lo
            )
            target[:, :, pl.ds(pl.multiple_of(TILE * at, TILE), TILE)] = result.reshape(chips, 2 * group, TILE)
            return carry

        lax.fori_loop(*PIECES[piece], tile_step, 0)

    def lanes_of(piece):
        first, last = PIECES[piece]
        return slice(TILE * first, TILE * last)

    def sent_lanes(piece):
        first, last = PIECES[piece]
        return slice(0 if piece == 0 else LANES + TILE * first, LANES + TILE * last)

    def swap(piece, source, at):
        lanes, slot = lanes_of(piece), 2 * piece + at
        return pair_copy(
            source.at[:, :, lanes], others_ref.at[at, :, :, lanes], pair_send.at[slot], pair_receive.at[slot]
        )

    def out_copy(piece, k, slot):
        lanes = sent_lanes(piece)
        return chip_copy(
            lambda at: joined.at[at, :, lanes], lambda at: gathered.at[at, :, lanes], k, slot, send.at[piece],
            receive.at[piece],
        )

    def back_copy(piece, k, slot):
        lanes = lanes_of(piece)
        return chip_copy(
            lambda at: ready.at[at, :, lanes], lambda at: chips_ref.at[0, at, :, lanes], k, slot, back_send.at[piece],
            back_receive.at[piece],
        )

    def onward(piece, slot):
        lanes = lanes_of(piece)
        return pair_copy(
            chips_ref.at[0, slot, :, lanes], chips_ref.at[1, slot, :, lanes], on_send.at[piece, slot],
            on_receive.at[piece, slot],
        )

    pieces = range(len(PIECES))
    own_decay = pair_copy(own_ref, partner_ref, pair_send.at[2 * len(PIECES)], pair_receive.at[2 * len(PIECES)])
    for piece in pieces:
        local_piece(1 - core, piece, theirs_ref)
        if piece == 0:
            pl.semaphore_wait(barrier, len(ORDER) + 1)
            own_decay.start()
        swap(piece, theirs_ref, 0).start()
        local_piece(core, piece, mine_ref)
        swap(piece, mine_ref, 1).start()
        if piece == 0:
            own_decay.wait_recv()
            joined[:, :, :LANES] = jnp.broadcast_to(
                (own_ref[0:1, :] * partner_ref[0:1, :])[None], joined.shape[:2] + (LANES,)
            )
        swap(piece, theirs_ref, 0).wait_recv()
        rows = jnp.concatenate([own_ref[...], partner_ref[...]], axis=0)
        for at in range(*PIECES[piece]):
            lanes = slice(TILE * at, TILE * (at + 1))
            target = slice(LANES + TILE * at, LANES + TILE * (at + 1))
            earlier, later = even_odd(even, spread_exact(rows, head_columns(HALF_TILES * core + at)))
            mine, other = mine_ref[:, :, lanes], others_ref[0, :, :, lanes]
            first, second = jnp.where(even, mine, other), jnp.where(even, other, mine)
            joined[:, :group, target] = later * first[:, :group] + second[:, :group]
            joined[:, group:, target] = first[:, group:] + earlier * second[:, group:]
        for k in ORDER:
            out_copy(piece, k, chip).start()
    gathered[chip] = joined[chip]

    within_start(bc_ref, mask_ref, score_grad_ref, score, scoreT)

    def step(tile, carry):
        within_tile(tile, x_ref, tail_ref, taps_ref, valid_ref, cot_ref, runT_ref, dtT_ref, out_ref, grad_ref,
                    score_grad_ref, score, scoreT)
        return carry

    lax.fori_loop(0, TILES, step, 0)
    score_grad_ref[...] = score_grad_ref[...] * mask_ref[0]

    for piece in pieces:
        for k in ORDER:
            out_copy(piece, k, None).wait_recv()
        by_head = jnp.max(gathered[:, :, :LANES], axis=1)
        for at in range(*PIECES[piece]):
            lanes = slice(TILE * at, TILE * (at + 1))
            source = slice(LANES + TILE * at, LANES + TILE * (at + 1))
            decay[:, lanes] = spread_exact(by_head, head_columns(HALF_TILES * core + at))
            state = jnp.zeros((group, TILE), F32)
            adjoint = jnp.zeros((group, TILE), F32)
            for here in range(chips):
                ready[here, :group, lanes] = state
                state = decay[here : here + 1, lanes] * state + gathered[here, :group, source]
                back = chips - 1 - here
                ready[back, group:, lanes] = adjoint
                adjoint = decay[back : back + 1, lanes] * adjoint + gathered[back, group:, source]
        for k in ORDER:
            back_copy(piece, k, chip).start()
        lanes = lanes_of(piece)
        chips_ref[0, chip, :, lanes] = ready[chip, :, lanes]
        onward(piece, chip).start()
    for piece in pieces:
        for k in ORDER:
            back_copy(piece, k, None).wait_recv()
            onward(piece, chip_after(k)).start()
    for piece in pieces:
        for k in ORDER:
            out_copy(piece, k, None).wait_send()
            back_copy(piece, k, None).wait_send()
        for slot in range(chips):
            copy = onward(piece, slot)
            copy.wait_send()
            copy.wait_recv()
        swap(piece, theirs_ref, 0).wait_send()
        swap(piece, mine_ref, 1).wait_send()
        swap(piece, mine_ref, 1).wait_recv()
    own_decay.wait_send()


def carry_stage(group, *operands):
    chips, rows, width = STATE // group, 2 * group, INNER // 2
    wide = jax.ShapeDtypeStruct((ROWS, INNER), F32)
    both = jax.ShapeDtypeStruct((2, chips, rows, width), F32)
    in_vmem = pl.BlockSpec(memory_space=pltpu.VMEM)
    dma = pltpu.SemaphoreType.DMA((len(PIECES), chips))
    three = pltpu.SemaphoreType.DMA((2 * len(PIECES) + 1,))
    half = pltpu.VMEM((chips, rows, width), F32)
    more = pltpu.VMEM((chips, rows, width + LANES), F32)
    square = pltpu.VMEM((ROWS, ROWS), F32)
    lhs = pltpu.VMEM((2 * STATE, 2 * ROWS), BF16)
    shapes = (
        both, both, wide, wide,
        jax.ShapeDtypeStruct((ROWS, ROWS), F32),
        jax.ShapeDtypeStruct((ROWS, 2 * STATE), F32),
        jax.ShapeDtypeStruct((8, LANES), F32),
    )
    return pl.pallas_call(
        functools.partial(carry_kernel, group),
        in_specs=[in_vmem] * len(operands),
        out_specs=[in_vmem] * len(shapes),
        out_shape=shapes,
        scratch_shapes=[
            half, half, more, more, half, pltpu.VMEM((chips, width), F32), square, square, lhs, lhs,
            dma, dma, dma, dma, dma, dma, three, three,
        ],
        compiler_params=pltpu.CompilerParams(vmem_limit_bytes=CARRY_BYTES, collective_id=2, has_side_effects=True),
        name="carry",
    )(*operands)


def conv_backward(grad, shifted, taps, valid):
    width = grad.shape[1]
    zeros = jnp.zeros((8, width), F32)
    total = jnp.concatenate([zeros, grad * taps[3:4]], axis=0)
    parts = [jnp.sum(grad * shifted[0], axis=0, keepdims=True)]
    for back in range(1, CONV):
        parts.insert(0, jnp.sum(grad * shifted[back], axis=0, keepdims=True))
        moved = jnp.concatenate([zeros, grad * valid[:, back - 1 : back] * taps[3 - back : 4 - back], zeros], axis=0)
        total = total + moved[back : back + ROWS + 8]
    parts.append(jnp.sum(grad, axis=0, keepdims=True))
    parts.append(jnp.zeros((3, width), F32))
    return total, jnp.concatenate(parts, axis=0)


def finish_kernel(group, half_ref, x_ref, tail_ref, taps_ref, xs_ref, tails_ref, tapss_ref, valid_ref, cot_ref, both_ref,
                  out_in_ref, grad_in_ref, chip_ref, local_ref, bc_ref, small_ref, own_ref, partner_ref, score_grad_ref,
                  run_ref, dt_ref, sig_ref, sigsum_ref,
                  out_ref, grad_ref, end_ref, borrowed_ref, taps_grad_ref, grads_ref, ends_ref, borroweds_ref,
                  tapss_grad_ref, heads_ref,
                  lhs_hi, lhs_lo, bc_grad, by_head, by_token):
    tile = pl.program_id(0)
    valid = valid_ref[...]

    @pl.when(tile == 0)
    def _():
        for at, source, late in ((0, STATE, False), (ROWS, 0, True)):
            pick = interleave(group, late).astype(BF16)
            first, second = halves(bc_ref[:, source : source + STATE])
            lhs_hi[at : at + ROWS, :] = mm_nt(first, pick).astype(BF16)
            lhs_lo[at : at + ROWS, :] = mm_nt(second, pick).astype(BF16)
        bc_grad[...] = jnp.zeros_like(bc_grad)
        by_head[...] = jnp.zeros_like(by_head)
        by_token[...] = jnp.zeros_like(by_token)

    total, shifted = convolve(tail_ref[...].astype(F32), x_ref[...].astype(F32), taps_ref[...], valid)
    gate = sigmoid(total)
    act = total * gate
    upstream = cot_ref[...].astype(F32)
    here = tile_at(tile, half_ref)
    weight = spread_heads(both_ref, here)
    leave, entry = weight[:ROWS], weight[ROWS:]
    by_row = spread_exact(
        jnp.concatenate([own_ref[...], partner_ref[...], small_ref[...]], axis=0), head_columns(here)
    )
    even = half_ref[2] == 0
    earlier, later = even_odd(even, by_row)
    weight_state, weight_adjoint = jnp.where(even, 1.0, earlier), jnp.where(even, later, 1.0)
    with_state, with_adjoint = jnp.where(even, 0.0, 1.0), jnp.where(even, 1.0, 0.0)
    states = jnp.concatenate(
        [
            weight_state * chip_ref[:, :group, :] + with_state * local_ref[:, :group, :],
            weight_adjoint * chip_ref[:, group:, :] + with_adjoint * local_ref[:, group:, :],
        ],
        axis=1,
    ).reshape(2 * STATE, TILE)
    states_hi, states_lo = halves(states)
    read = mm(lhs_hi[...], states_hi) + mm(lhs_hi[...], states_lo) + mm(lhs_lo[...], states_hi)
    one_hot = head_columns(here)
    gain = by_row[18:19]
    through_state = out_in_ref[...] + entry * read[:ROWS]
    out_ref[...] = (through_state + gain * act).astype(BF16)
    act_grad_late = leave * read[ROWS:]
    act_grad = grad_in_ref[...] + act_grad_late

    first, second = halves(jnp.concatenate([entry * upstream, leave * act], axis=0))
    bc_grad[...] += mm_nt(first, states_hi) + mm_nt(first, states_lo) + mm_nt(second, states_hi)

    first, second = halves(jnp.concatenate([upstream * through_state, act * act_grad], axis=0))
    by_token[...] += mm_nt(first, one_hot) + mm_nt(second, one_hot)
    crossed = states * pltpu.roll(states, group, 0)
    crossed = jnp.where(iota((2 * STATE, TILE), 0) % (2 * group) >= group, crossed, 0.0)
    sums = jnp.concatenate(
        [
            jnp.sum(act * act_grad_late, axis=0, keepdims=True),
            jnp.sum(crossed, axis=0, keepdims=True),
            jnp.sum(upstream * act, axis=0, keepdims=True),
            jnp.zeros((5, TILE), F32),
        ],
        axis=0,
    )
    first = sums.astype(BF16)
    second, third = halves(sums - first.astype(F32))
    by_head[...] += mm_nt(first, one_hot) + mm_nt(second, one_hot) + mm_nt(third, one_hot)

    act_grad = act_grad + gain * upstream
    conv_grad = act_grad * (gate + act * (1.0 - gate))
    full, taps_grad_ref[...] = conv_backward(conv_grad, shifted, taps_ref[...], valid)
    borrowed_ref[...] = full[:8]
    grad_ref[...] = full[8:].astype(BF16)
    end_ref[...] = full[ROWS - 8 :]

    @pl.when(tile == TILES - 1)
    def _():
        score_grad = score_grad_ref[...]
        keys, reads = bc_ref[:, :STATE], bc_ref[:, STATE:]
        reads_grad = exact(bc_grad[:ROWS], interleave(group, False)) + exact(score_grad, keys)
        keys_grad = exact(bc_grad[ROWS:], interleave(group, True)) + exact(score_grad.T, reads)
        total, shifted = convolve(tails_ref[...].astype(F32), xs_ref[...].astype(F32), tapss_ref[...], valid)
        gate = sigmoid(total)
        small_grad = jnp.concatenate([keys_grad, reads_grad], axis=1) * (gate + total * gate * (1.0 - gate))
        full, tapss_grad_ref[...] = conv_backward(small_grad, shifted, tapss_ref[...], valid)
        borroweds_ref[...] = full[:8]
        grads_ref[...] = full[8:].astype(BF16)
        ends_ref[...] = full[ROWS - 8 :]

        read_sum, added_sum = by_token[:ROWS], by_token[ROWS:]
        at_end = by_head[0:1, :] + own_ref[0:1, :] * by_head[1:2, :]
        run_grad = read_sum - added_sum + jnp.where(iota((ROWS, LANES), 0) == ROWS - 1, at_end, 0.0)
        alog_grad = jnp.sum(run_grad * run_ref[...], axis=0, keepdims=True)
        bias_grad = jnp.sum(added_sum / dt_ref[...] * sig_ref[...], axis=0, keepdims=True)
        rate = jnp.exp(small_ref[1:2, :])
        bias_grad = bias_grad - rate * jnp.sum(run_grad * sigsum_ref[...], axis=0, keepdims=True)
        heads_ref[...] = jnp.concatenate([bias_grad, alog_grad, by_head[2:3, :], jnp.zeros((5, LANES), F32)], axis=0)


def finish_stage(group, half, *operands):
    square = whole((ROWS, LANES))
    eight = whole((8, LANES))
    shapes = (
        jax.ShapeDtypeStruct((ROWS, INNER), BF16),
        jax.ShapeDtypeStruct((ROWS, INNER), BF16),
        jax.ShapeDtypeStruct((16, INNER), F32),
        jax.ShapeDtypeStruct((8, INNER), F32),
        jax.ShapeDtypeStruct((8, INNER), F32),
        jax.ShapeDtypeStruct((ROWS, 2 * STATE), BF16),
        jax.ShapeDtypeStruct((16, 2 * STATE), F32),
        jax.ShapeDtypeStruct((8, 2 * STATE), F32),
        jax.ShapeDtypeStruct((8, 2 * STATE), F32),
        jax.ShapeDtypeStruct((8, LANES), F32),
    )
    states = pl.BlockSpec(
        (None, STATE // group, 2 * group, TILE), lambda i, half: (i // HALF_TILES, 0, 0, lax.rem(i, HALF_TILES))
    )
    return call(
        functools.partial(finish_kernel, group), "finish", half, TILES,
        [
            tile_spec(ROWS), tile_spec(8), tile_spec(8),
            small_spec(ROWS), small_spec(8), small_spec(8),
            whole((ROWS, 8)), tile_spec(ROWS), whole((2 * ROWS, 2 * LANES)),
            tile_spec(ROWS), tile_spec(ROWS), states, states,
            whole((ROWS, 2 * STATE)), eight, eight, eight, whole((ROWS, ROWS)), square, square, square, square,
        ],
        [tile_spec(part.shape[0]) for part in shapes[:5]] + [whole(part.shape) for part in shapes[5:]],
        shapes,
        [
            pltpu.VMEM((2 * ROWS, 2 * STATE), BF16), pltpu.VMEM((2 * ROWS, 2 * STATE), BF16),
            pltpu.VMEM((2 * ROWS, 2 * STATE), F32), pltpu.VMEM((8, LANES), F32), pltpu.VMEM((2 * ROWS, LANES), F32),
        ],
        operands,
    )


def total_kernel(scale, taps_ref, small_ref, heads_ref, borrowed_ref, borroweds_ref, end_ref, ends_ref, keep_ref,
                 sums_ref, last_ref,
                 parts, slots, piece, far_slots, result, got, got_small, send, receive, far_send, far_receive, back_send,
                 back_receive, rows_send, rows_receive):
    shards, groups = lax.axis_size("seq"), lax.axis_size("dp")
    others = groups * shards // 8
    place, group = lax.axis_index("seq"), lax.axis_index("dp")
    before = (group, lax.rem(place + shards - 1, shards))
    after = (group, lax.rem(place + 1, shards))
    barrier = pltpu.get_barrier_semaphore()
    for peers, size in ((near, 8), (far, others)):
        for k in range(1, size):
            pl.semaphore_signal(barrier, inc=1, device_id=peers(k)[0], device_id_type=MESH)
    for peer in (before, after):
        pl.semaphore_signal(barrier, inc=1, device_id=peer, device_id_type=MESH)
    pl.semaphore_wait(barrier, 7 + others - 1 + 2)

    depth = parts.shape[1]
    wide = CH // LANES
    for at in range(8 * depth // 8):
        if at < INNER // LANES:
            block = taps_ref[:, LANES * at : LANES * (at + 1)]
        elif at < wide:
            block = small_ref[:, LANES * at - INNER : LANES * (at + 1) - INNER]
        elif at == wide:
            block = heads_ref[...]
        else:
            block = jnp.zeros((8, LANES), F32)
        parts[at % 8, 8 * (at // 8) : 8 * (at // 8) + 8, :] = block
    send_all(near, 8, lambda slot: parts.at[slot], slots, send, receive)
    returns = [
        pltpu.make_async_remote_copy(
            src_ref=source, dst_ref=target, send_sem=rows_send.at[at], recv_sem=rows_receive.at[at], device_id=before,
            device_id_type=MESH,
        )
        for at, (source, target) in enumerate(((borrowed_ref, got), (borroweds_ref, got_small)))
    ]

    @pl.when(place > 0)
    def _():
        for copy in returns:
            copy.start()

    _, own = near(0)
    _, far_own = far(0)
    slots[own] = parts[own]
    wait_all(near, 8, lambda slot: parts.at[slot], slots, send, receive)
    piece[...] = jnp.sum(slots[...], axis=0)
    send_all(far, others, lambda slot: piece, far_slots, far_send, far_receive)
    far_slots[far_own] = piece[...]
    wait_all(far, others, lambda slot: piece, far_slots, far_send, far_receive)
    piece[...] = jnp.sum(far_slots[...], axis=0) * scale
    send_all(near, 8, lambda slot: piece, result, back_send, back_receive)
    result[own] = piece[...]

    @pl.when(place > 0)
    def _():
        for copy in returns:
            copy.wait_send()

    @pl.when(place < shards - 1)
    def _():
        for copy in returns:
            copy.wait_recv()
        keep = keep_ref[:, 0:1]
        for lanes, source, end in ((slice(0, INNER), got, end_ref), (slice(INNER, CH), got_small, ends_ref)):
            late = iota(source.shape, 0) >= 8 - CONV + 1
            rows = jnp.concatenate([end[:8, :], end[8:, :] + jnp.where(late, source[...] * keep, 0.0)], axis=0)
            last_ref[:, lanes] = rows.astype(BF16)

    @pl.when(place == shards - 1)
    def _():
        last_ref[:, :INNER] = end_ref[...].astype(BF16)
        last_ref[:, INNER:] = ends_ref[...].astype(BF16)

    wait_all(near, 8, lambda slot: piece, result, back_send, back_receive)
    for at in range(wide + 1):
        sums_ref[:, LANES * at : LANES * (at + 1)] = result[at % 8, 8 * (at // 8) : 8 * (at // 8) + 8, :]


def layout_kernel(sums_ref, last_ref, grad_ref, grads_ref, weight_ref, bias_ref, dt_bias_ref, a_log_ref, gain_ref,
                  whole_ref):
    step = pl.program_id(0)

    @pl.when(step == 0)
    def _():
        weight_ref[...] = sums_ref[:CONV, :CH]
        bias_ref[...] = sums_ref[CONV : CONV + 1, :CH].reshape(CH)
        for at, target in enumerate((dt_bias_ref, a_log_ref, gain_ref)):
            target[...] = sums_ref[at : at + 1, CH : CH + HEADS].reshape(HEADS)

    @pl.when(step < pl.num_programs(0) - 1)
    def _():
        whole_ref[:, :INNER] = grad_ref[...]
        whole_ref[:, INNER:] = grads_ref[...]

    @pl.when(step == pl.num_programs(0) - 1)
    def _():
        whole_ref[: whole_ref.shape[0] - 16, :INNER] = grad_ref[: whole_ref.shape[0] - 16, :]
        whole_ref[: whole_ref.shape[0] - 16, INNER:] = grads_ref[: whole_ref.shape[0] - 16, :]
        whole_ref[whole_ref.shape[0] - 16 :, :] = last_ref[...]


def layout_stage(sums, last, grad, grads):
    rows = 32
    shapes = (
        jax.ShapeDtypeStruct((CONV, CH), F32),
        jax.ShapeDtypeStruct((CH,), F32),
        jax.ShapeDtypeStruct((HEADS,), F32),
        jax.ShapeDtypeStruct((HEADS,), F32),
        jax.ShapeDtypeStruct((HEADS,), F32),
        jax.ShapeDtypeStruct((ROWS, CH), BF16),
    )
    blocks = [pl.BlockSpec((rows, width), lambda i: (i, 0)) for width in (INNER, 2 * STATE, CH)]
    return pl.pallas_call(
        layout_kernel,
        grid=(ROWS // rows,),
        in_specs=[whole(sums.shape), whole(last.shape)] + blocks[:2],
        out_specs=[whole(part.shape) for part in shapes[:5]] + blocks[2:],
        out_shape=shapes,
        name="layout",
    )(sums, last, grad, grads)


def total_stage(others, scale, *operands):
    depth = 8 * pl.cdiv(CH // LANES + 1, 8)
    in_vmem = pl.BlockSpec(memory_space=pltpu.VMEM)
    shapes = (jax.ShapeDtypeStruct((8, CH + LANES), F32), jax.ShapeDtypeStruct((16, CH), BF16))
    dma = pltpu.SemaphoreType.DMA
    return pl.pallas_call(
        functools.partial(total_kernel, scale),
        in_specs=[in_vmem] * len(operands),
        out_specs=[in_vmem] * len(shapes),
        out_shape=shapes,
        scratch_shapes=[
            pltpu.VMEM((8, depth, LANES), F32), pltpu.VMEM((8, depth, LANES), F32),
            pltpu.VMEM((depth, LANES), F32), pltpu.VMEM((others, depth, LANES), F32),
            pltpu.VMEM((8, depth, LANES), F32),
            pltpu.VMEM((8, INNER), F32), pltpu.VMEM((8, 2 * STATE), F32),
            dma((8,)), dma((8,)), dma((others,)), dma((others,)), dma((8,)), dma((8,)), dma((2,)), dma((2,)),
        ],
        compiler_params=pltpu.CompilerParams(
            vmem_limit_bytes=VMEM_BYTES, collective_id=1, has_side_effects=True
        ),
        name="totals",
    )(*operands)


def on_device(conv_input, doc_start, conv_weight, conv_bias, dt_raw, dt_bias, a_log, skip_gain, cotangent):
    shards, place = lax.axis_size("seq"), lax.axis_index("seq")
    group = 2 * STATE // shards
    core = lax.rem(place, 2)
    half = jnp.stack([core, place // 2, core])
    run, runT, dt, dtT, both, sig, sigsum, mask, valid, keep, tail, own, small, taps = head_stage(
        dt_raw.T, dt_bias[None], a_log[None], skip_gain[None], doc_start[None], conv_weight, conv_bias[None], conv_input
    )
    tail = lax.ppermute(tail, "seq", [(i, i + 1) for i in range(shards - 1)])
    chips, others, out_in, grad_in, score_grad, bc, partner = carry_stage(
        group, conv_input, tail, taps, valid, cotangent, both, own, runT, dtT, mask
    )
    out, grad, end, borrowed, taps_grad, grads, ends, borroweds, tapss_grad, heads = finish_stage(
        group, half, conv_input, tail, taps, conv_input, tail, taps, valid, cotangent, both, out_in, grad_in, chips,
        others, bc, small, own, partner, score_grad, run, dt, sig, sigsum,
    )
    groups = lax.axis_size("dp")
    sums, last = total_stage(
        groups * shards // 8, float(groups * shards * ROWS) ** (-0.5), taps_grad, tapss_grad, heads, borrowed, borroweds,
        end, ends, keep,
    )
    weight_grad, bias_grad, dt_bias_grad, a_log_grad, gain_grad, whole_grad = layout_stage(sums, last, grad, grads)
    return (out, whole_grad, weight_grad, bias_grad, dt_bias_grad, a_log_grad, gain_grad)


def solution(mesh):
    sharded = P(("dp", "seq"), None)
    return jax.shard_map(
        on_device,
        mesh=mesh,
        in_specs=(sharded, P(("dp", "seq")), P(), P(), sharded, P(), P(), P(), sharded),
        out_specs=(sharded, sharded, P(), P(), P(), P(), P()),
        check_vma=False,
    )
```

```python
import functools

import jax
import jax.numpy as jnp
from jax import lax
from jax.experimental import pallas as pl
from jax.experimental.pallas import tpu as pltpu
from jax.sharding import PartitionSpec as P

HEADS = 80
HEAD_DIM = 64
STATE = 128
CONV = 4
INNER = 5120
CH = 5376
ROWS = 128
TILE = 512
TILES = INNER // TILE
TILE_HEADS = TILE // HEAD_DIM
LANES = 128

F32 = jnp.float32
BF16 = jnp.bfloat16
EXACT = lax.Precision.HIGHEST
HALF_TILES = TILES // 2
VMEM_BYTES = 20 << 20
CARRY_BYTES = 28 << 20
MESH = pl.DeviceIdType.MESH


def iota(shape, axis):
    return lax.broadcasted_iota(jnp.int32, shape, axis)


def halves(value):
    high = value.astype(BF16)
    return high, (value - high.astype(F32)).astype(BF16)


def mm(a, b):
    return lax.dot_general(a, b, (((1,), (0,)), ((), ())), preferred_element_type=F32)


def mm_nt(a, b):
    return lax.dot_general(a, b, (((1,), (1,)), ((), ())), preferred_element_type=F32)


def exact(a, b):
    return lax.dot_general(
        a, b, (((1,), (0,)), ((), ())), precision=EXACT, preferred_element_type=F32
    )


def spread_exact(rows, one_hot):
    first, rest = rows.astype(BF16), rows
    rest = rest - first.astype(F32)
    second, third = halves(rest)
    return mm(first, one_hot) + mm(second, one_hot) + mm(third, one_hot)


def interleave(group, late):
    row, col = iota((2 * STATE, STATE), 0), iota((2 * STATE, STATE), 1)
    place = row % (2 * group)
    first = group if late else 0
    here = (place >= first) & (place < first + group)
    return jnp.where(here & (col == group * (row // (2 * group)) + place - first), 1.0, 0.0)


def head_columns(tile):
    head, col = iota((LANES, TILE), 0), iota((LANES, TILE), 1)
    return jnp.where(head == TILE_HEADS * tile + col // HEAD_DIM, 1.0, 0.0).astype(BF16)


def spread_heads(both_ref, tile):
    one_hot = head_columns(tile)
    return mm(both_ref[...], jnp.concatenate([one_hot, one_hot], axis=0))


def convolve(tail, rows, taps, valid):
    extended = jnp.concatenate([tail, rows], axis=0)
    total = taps[4:5] + taps[3:4] * rows
    shifted = [rows]
    for back in range(1, CONV):
        moved = extended[8 - back : 8 - back + ROWS] * valid[:, back - 1 : back]
        shifted.append(moved)
        total = total + taps[3 - back : 4 - back] * moved
    return total, shifted


def sigmoid(v):
    return 1.0 / (1.0 + jnp.exp(-v))


def near(k):
    place = lax.axis_index("seq")
    slot = lax.rem(lax.rem(place, 8) + k, 8)
    return (lax.axis_index("dp"), place - lax.rem(place, 8) + slot), slot


def far(k):
    place, group = lax.axis_index("seq"), lax.axis_index("dp")
    runs = lax.axis_size("seq") // 8
    slot = lax.rem(group * runs + place // 8 + k, lax.axis_size("dp") * runs)
    return (slot // runs, lax.rem(slot, runs) * 8 + lax.rem(place, 8)), slot


def send_all(peers, size, source, target, send, receive):
    _, own = peers(0)
    for k in range(1, size):
        peer, slot = peers(k)
        pltpu.make_async_remote_copy(
            src_ref=source(slot), dst_ref=target.at[own], send_sem=send.at[slot], recv_sem=receive.at[own],
            device_id=peer, device_id_type=MESH,
        ).start()


def wait_all(peers, size, source, target, send, receive):
    for k in range(1, size):
        peer, slot = peers(k)
        copy = pltpu.make_async_remote_copy(
            src_ref=source(slot), dst_ref=target.at[slot], send_sem=send.at[slot], recv_sem=receive.at[slot],
            device_id=peer, device_id_type=MESH,
        )
        copy.wait_send()
        copy.wait_recv()


def head_kernel(raw_in_ref, dt_bias_ref, a_log_ref, gain_ref, row_ref, weight_ref, bias_ref, end_ref, run_ref, runT_ref,
                dt_ref, dtT_ref, both_ref, sig_ref, sigsum_ref, mask_ref, valid_ref, keep_ref, tail_ref, own_ref,
                small_ref, taps_ref, raw):
    taps_ref[:CONV, :] = weight_ref[...]
    taps_ref[CONV:, :] = jnp.broadcast_to(bias_ref[...], (8 - CONV, CH))
    small_ref[...] = jnp.zeros_like(small_ref)
    for at, source in enumerate((dt_bias_ref, a_log_ref, gain_ref)):
        small_ref[at : at + 1, :HEADS] = source[...]
    reset_row = row_ref[...].astype(F32)
    token, other = iota((ROWS, ROWS), 0), iota((ROWS, ROWS), 1)
    reset_col = jnp.sum(jnp.where(token == other, reset_row, 0.0), axis=1, keepdims=True)
    low, high = token >= other, token <= other
    segment_col = jnp.sum(jnp.where(low, reset_row, 0.0), axis=1, keepdims=True)
    segment_row = jnp.sum(jnp.where(high, reset_col, 0.0), axis=0, keepdims=True)
    mask_ref[0] = jnp.where(low & (segment_col == segment_row), 1.0, 0.0)
    mask_ref[1] = jnp.where(high & (segment_col == segment_row), 1.0, 0.0)

    kept = jnp.broadcast_to(1.0 - reset_col, (ROWS, LANES))
    one_back = jnp.where(token < 1, 1.0, pltpu.roll(kept, 1, 0))
    two_back = jnp.where(token < 2, 1.0, pltpu.roll(kept, 2, 0))
    valid = jnp.where(other == 0, kept, jnp.where(other == 1, kept * one_back, kept * one_back * two_back))
    valid_ref[...] = valid[:, :8]
    one_on, two_on = pltpu.roll(kept, ROWS - 1, 0), pltpu.roll(kept, ROWS - 2, 0)
    keep = jnp.where(
        token == ROWS - 1, 1.0, jnp.where(token == ROWS - 2, one_on, jnp.where(token == ROWS - 3, one_on * two_on, 0.0))
    )[ROWS - 8 :]
    keep_ref[...] = keep
    tail_ref[...] = (end_ref[8:, :].astype(F32) * keep[:, 0:1]).astype(BF16)

    raw[...] = jnp.zeros_like(raw)
    raw[:HEADS, :] = raw_in_ref[...]
    biased = raw[...].T + small_ref[0:1, :]
    dt = jnp.maximum(biased, 0.0) + jnp.log1p(jnp.exp(-jnp.abs(biased)))
    decay = -jnp.exp(small_ref[1:2, :]) * dt
    lower = jnp.where(low, 1.0, 0.0)
    running = exact(lower, decay)
    last = running[ROWS - 1 : ROWS]
    count = segment_col[ROWS - 1 : ROWS]
    untouched = jnp.where(segment_col == 0.0, 1.0, 0.0)
    entry = jnp.exp(running) * untouched
    own_ref[...] = jnp.broadcast_to(entry[ROWS - 1 : ROWS], own_ref.shape)
    sig = sigmoid(biased)
    sig_ref[...] = sig
    sigsum_ref[...] = exact(lower, sig)
    run_ref[...] = running
    runT_ref[...] = running.T
    dt_ref[...] = dt
    dtT_ref[...] = dt.T
    leave = jnp.exp(last - running) * jnp.where(segment_col == count, 1.0, 0.0) * dt
    for at, part in ((0, leave), (ROWS, entry)):
        first, second = halves(part)
        both_ref[at : at + ROWS, :LANES] = first
        both_ref[at : at + ROWS, LANES:] = second


def head_stage(raw, dt_bias, a_log, gain, row, weight, bias, conv_input):
    square = jax.ShapeDtypeStruct((ROWS, LANES), F32)
    eight = jax.ShapeDtypeStruct((8, LANES), F32)
    shapes = (
        square, square, square, square,
        jax.ShapeDtypeStruct((2 * ROWS, 2 * LANES), BF16),
        square, square,
        jax.ShapeDtypeStruct((2, ROWS, ROWS), F32),
        jax.ShapeDtypeStruct((ROWS, 8), F32),
        eight,
        jax.ShapeDtypeStruct((8, CH), BF16),
        eight, eight,
        jax.ShapeDtypeStruct((8, CH), F32),
    )
    given = (raw, dt_bias, a_log, gain, row, weight, bias)
    return pl.pallas_call(
        head_kernel,
        grid=(1,),
        in_specs=[whole(part.shape) for part in given] + [pl.BlockSpec((16, CH), lambda *at: (ROWS // 16 - 1, 0))],
        out_specs=[whole(part.shape) for part in shapes],
        out_shape=shapes,
        scratch_shapes=[pltpu.VMEM((ROWS, LANES), F32)],
        compiler_params=pltpu.CompilerParams(vmem_limit_bytes=VMEM_BYTES),
        name="heads",
    )(*given, conv_input)


def whole(shape):
    return pl.BlockSpec(shape, lambda *at: (0,) * len(shape))


def call(kernel, name, half, grid, in_specs, out_specs, out_shape, scratch_shapes, operands, aliases={}):
    return pl.pallas_call(
        kernel,
        grid_spec=pltpu.PrefetchScalarGridSpec(
            num_scalar_prefetch=1, grid=(grid,), in_specs=in_specs, out_specs=out_specs, scratch_shapes=scratch_shapes
        ),
        out_shape=out_shape,
        input_output_aliases=aliases,
        compiler_params=pltpu.CompilerParams(vmem_limit_bytes=VMEM_BYTES),
        name=name,
    )(half, *operands)


def tile_at(i, half):
    return lax.rem(i + HALF_TILES * half[0], TILES)


def tile_spec(rows):
    return pl.BlockSpec((rows, TILE), lambda i, half: (0, tile_at(i, half)))


def small_spec(rows):
    return pl.BlockSpec((rows, 2 * STATE), lambda *at: (0, INNER // (2 * STATE)))


def pair_spec(shape, first):
    if first:
        return pl.BlockSpec(shape[:2] + (TILE,), lambda i, half: (0, 0, jnp.minimum(i, HALF_TILES - 1)))
    return pl.BlockSpec(shape[:2] + (TILE,), lambda i, half: (0, 0, jnp.maximum(i - HALF_TILES, 0)))


def local_start(group, xs, tails, tapss, valid, bc_ref, lhs_hi, lhs_lo):
    total, _ = convolve(tails.astype(F32), xs.astype(F32), tapss, valid)
    small = total * sigmoid(total)
    bc_ref[...] = small
    for at, late in ((0, False), (STATE, True)):
        pick = interleave(group, late).astype(BF16)
        first, second = halves(small[:, at : at + STATE])
        lhs_hi[:, at : at + ROWS] = mm_nt(pick, first).astype(BF16)
        lhs_lo[:, at : at + ROWS] = mm_nt(pick, second).astype(BF16)


def local_tile(tile, x_ref, tail_ref, taps_ref, valid_ref, cot_ref, both_ref, lhs_hi, lhs_lo):
    columns = pl.ds(pl.multiple_of(TILE * tile, TILE), TILE)
    total, _ = convolve(
        tail_ref[:, columns].astype(F32), x_ref[:, columns].astype(F32), taps_ref[:, columns], valid_ref[...]
    )
    act = total * sigmoid(total)
    weight = spread_heads(both_ref, tile)
    first, second = halves(weight * jnp.concatenate([act, cot_ref[:, columns].astype(F32)], axis=0))
    return mm(lhs_hi[...], first) + mm(lhs_hi[...], second) + mm(lhs_lo[...], first)


def within_start(bc_ref, mask_ref, score_grad_ref, score, scoreT):
    keys, reads = bc_ref[:, :STATE], bc_ref[:, STATE:]
    keys_hi, keys_lo = halves(keys)
    reads_hi, reads_lo = halves(reads)
    score[...] = mask_ref[0] * (mm_nt(reads_hi, keys_hi) + mm_nt(reads_hi, keys_lo) + mm_nt(reads_lo, keys_hi))
    scoreT[...] = mask_ref[1] * (mm_nt(keys_hi, reads_hi) + mm_nt(keys_hi, reads_lo) + mm_nt(keys_lo, reads_hi))
    score_grad_ref[...] = jnp.zeros_like(score_grad_ref)


def within_tile(tile, x_ref, tail_ref, taps_ref, valid_ref, cot_ref, runT_ref, dtT_ref, out_ref, grad_ref,
                score_grad_ref, score, scoreT):
    at = pl.multiple_of(TILE * tile, TILE)
    columns = pl.ds(at, TILE)
    total, _ = convolve(
        tail_ref[:, columns].astype(F32), x_ref[:, columns].astype(F32), taps_ref[:, columns], valid_ref[...]
    )
    act = total * sigmoid(total)
    rows = pl.ds(pl.multiple_of(TILE_HEADS * tile, TILE_HEADS), TILE_HEADS)
    run_rows, dt_rows = runT_ref[rows, :], dtT_ref[rows, :]
    run, dt = run_rows.T, dt_rows.T
    left = iota((ROWS, LANES), 1) < HEAD_DIM
    left = jnp.where(left, 1.0, 0.0).astype(BF16)
    right = 1.0 - left
    score_grad = score_grad_ref[...]
    for pair in range(TILE_HEADS // 2):
        lanes = slice(LANES * pair, LANES * (pair + 1))
        here = pl.ds(at + LANES * pair, LANES)
        spread, weights, weightsT = [], [], []
        for head in (2 * pair, 2 * pair + 1):
            difference = run[:, head : head + 1] - run_rows[head : head + 1, :]
            step = jnp.exp(jnp.minimum(difference, 0.0)) * dt_rows[head : head + 1, :]
            spread.append(step)
            weights.append(step * score[...])
            weightsT.append(jnp.exp(jnp.minimum(-difference, 0.0)) * dt[:, head : head + 1] * scoreT[...])
        x_hi, x_lo = halves(act[:, lanes])
        upstream = cot_ref[:, here]
        x_hi2 = jnp.concatenate([x_hi * left, x_hi * right], axis=0)
        x_lo2 = jnp.concatenate([x_lo * left, x_lo * right], axis=0)
        upstream2 = jnp.concatenate([upstream * left, upstream * right], axis=0)
        w_hi, w_lo = halves(jnp.concatenate(weights, axis=1))
        wide = mm(w_hi, jnp.concatenate([x_hi2, x_lo2], axis=1))
        out_ref[:, here] = wide[:, :LANES] + wide[:, LANES:] + mm(w_lo, x_hi2)
        wt_hi, wt_lo = halves(jnp.concatenate(weightsT, axis=1))
        grad_ref[:, here] = mm(wt_hi, upstream2) + mm(wt_lo, upstream2)
        inner = mm_nt(upstream2, jnp.concatenate([x_hi, x_lo], axis=0))
        inner = inner[:, :ROWS] + inner[:, ROWS:]
        score_grad = score_grad + inner[:ROWS] * spread[0] + inner[ROWS:] * spread[1]
    score_grad_ref[...] = score_grad


def even_odd(even, both):
    own, partner = both[0:1], both[8:9]
    return jnp.where(even, own, partner)[None], jnp.where(even, partner, own)[None]


ORDER = (10, 1, 4, 3, 12, 11, 9, 14, 6, 2, 8, 5, 15, 7, 13)


def chip_after(k):
    chip = lax.axis_index("seq") // 2
    return lax.rem(chip // 4 + k // 4, 4) * 4 + lax.rem(lax.rem(chip, 4) + k % 4, 4)


def same_core(chip):
    return (lax.axis_index("dp"), 2 * chip + lax.rem(lax.axis_index("seq"), 2))


def chip_copy(source, target, k, slot, send, receive):
    other = chip_after(k)
    slot = other if slot is None else slot
    return pltpu.make_async_remote_copy(
        src_ref=source(other), dst_ref=target(slot), send_sem=send.at[other], recv_sem=receive.at[slot],
        device_id=same_core(other), device_id_type=MESH,
    )


PIECES = ((0, 1), (1, 3), (3, 5))


def pair_copy(source, target, send, receive):
    place = lax.axis_index("seq")
    return pltpu.make_async_remote_copy(
        src_ref=source, dst_ref=target, send_sem=send, recv_sem=receive,
        device_id=(lax.axis_index("dp"), place + 1 - 2 * lax.rem(place, 2)), device_id_type=MESH,
    )


def carry_kernel(group, x_ref, tail_ref, taps_ref, valid_ref, cot_ref, both_ref, own_ref, runT_ref, dtT_ref, mask_ref,
                 chips_ref, others_ref, out_ref, grad_ref, score_grad_ref, bc_ref, partner_ref,
                 mine_ref, theirs_ref, joined, gathered, ready, decay, score, scoreT, lhs_hi, lhs_lo, send, receive,
                 back_send, back_receive, on_send, on_receive, pair_send, pair_receive):
    chips = mine_ref.shape[0]
    place = lax.axis_index("seq")
    chip, core = place // 2, lax.rem(place, 2)
    even = core == 0
    barrier = pltpu.get_barrier_semaphore()
    pl.semaphore_signal(
        barrier, inc=1, device_id=(lax.axis_index("dp"), place + 1 - 2 * core), device_id_type=MESH
    )
    for k in ORDER:
        pl.semaphore_signal(barrier, inc=1, device_id=same_core(chip_after(k)), device_id_type=MESH)
    local_start(
        group, x_ref[:, INNER:], tail_ref[:, INNER:], taps_ref[:, INNER:], valid_ref[...], bc_ref, lhs_hi, lhs_lo
    )

    def local_piece(half, piece, target):
        def tile_step(at, carry):
            result = local_tile(
                HALF_TILES * half + at, x_ref, tail_ref, taps_ref, valid_ref, cot_ref, both_ref, lhs_hi, lhs_lo
            )
            target[:, :, pl.ds(pl.multiple_of(TILE * at, TILE), TILE)] = result.reshape(chips, 2 * group, TILE)
            return carry

        lax.fori_loop(*PIECES[piece], tile_step, 0)

    def lanes_of(piece):
        first, last = PIECES[piece]
        return slice(TILE * first, TILE * last)

    def sent_lanes(piece):
        first, last = PIECES[piece]
        return slice(0 if piece == 0 else LANES + TILE * first, LANES + TILE * last)

    def swap(piece, source, at):
        lanes, slot = lanes_of(piece), 2 * piece + at
        return pair_copy(
            source.at[:, :, lanes], others_ref.at[at, :, :, lanes], pair_send.at[slot], pair_receive.at[slot]
        )

    def out_copy(piece, k, slot):
        lanes = sent_lanes(piece)
        return chip_copy(
            lambda at: joined.at[at, :, lanes], lambda at: gathered.at[at, :, lanes], k, slot, send.at[piece],
            receive.at[piece],
        )

    def back_copy(piece, k, slot):
        lanes = lanes_of(piece)
        return chip_copy(
            lambda at: ready.at[at, :, lanes], lambda at: chips_ref.at[0, at, :, lanes], k, slot, back_send.at[piece],
            back_receive.at[piece],
        )

    def onward(piece, slot):
        lanes = lanes_of(piece)
        return pair_copy(
            chips_ref.at[0, slot, :, lanes], chips_ref.at[1, slot, :, lanes], on_send.at[piece, slot],
            on_receive.at[piece, slot],
        )

    pieces = range(len(PIECES))
    own_decay = pair_copy(own_ref, partner_ref, pair_send.at[2 * len(PIECES)], pair_receive.at[2 * len(PIECES)])
    for piece in pieces:
        local_piece(1 - core, piece, theirs_ref)
        if piece == 0:
            pl.semaphore_wait(barrier, len(ORDER) + 1)
            own_decay.start()
        swap(piece, theirs_ref, 0).start()
        local_piece(core, piece, mine_ref)
        swap(piece, mine_ref, 1).start()
        if piece == 0:
            own_decay.wait_recv()
            joined[:, :, :LANES] = jnp.broadcast_to(
                (own_ref[0:1, :] * partner_ref[0:1, :])[None], joined.shape[:2] + (LANES,)
            )
        swap(piece, theirs_ref, 0).wait_recv()
        rows = jnp.concatenate([own_ref[...], partner_ref[...]], axis=0)
        for at in range(*PIECES[piece]):
            lanes = slice(TILE * at, TILE * (at + 1))
            target = slice(LANES + TILE * at, LANES + TILE * (at + 1))
            earlier, later = even_odd(even, spread_exact(rows, head_columns(HALF_TILES * core + at)))
            mine, other = mine_ref[:, :, lanes], others_ref[0, :, :, lanes]
            first, second = jnp.where(even, mine, other), jnp.where(even, other, mine)
            joined[:, :group, target] = later * first[:, :group] + second[:, :group]
            joined[:, group:, target] = first[:, group:] + earlier * second[:, group:]
        for k in ORDER:
            out_copy(piece, k, chip).start()
    gathered[chip] = joined[chip]

    within_start(bc_ref, mask_ref, score_grad_ref, score, scoreT)

    def step(tile, carry):
        within_tile(tile, x_ref, tail_ref, taps_ref, valid_ref, cot_ref, runT_ref, dtT_ref, out_ref, grad_ref,
                    score_grad_ref, score, scoreT)
        return carry

    lax.fori_loop(0, TILES, step, 0)
    score_grad_ref[...] = score_grad_ref[...] * mask_ref[0]

    for piece in pieces:
        for k in ORDER:
            out_copy(piece, k, None).wait_recv()
        by_head = jnp.max(gathered[:, :, :LANES], axis=1)
        for at in range(*PIECES[piece]):
            lanes = slice(TILE * at, TILE * (at + 1))
            source = slice(LANES + TILE * at, LANES + TILE * (at + 1))
            decay[:, lanes] = spread_exact(by_head, head_columns(HALF_TILES * core + at))
            state = jnp.zeros((group, TILE), F32)
            adjoint = jnp.zeros((group, TILE), F32)
            for here in range(chips):
                ready[here, :group, lanes] = state
                state = decay[here : here + 1, lanes] * state + gathered[here, :group, source]
                back = chips - 1 - here
                ready[back, group:, lanes] = adjoint
                adjoint = decay[back : back + 1, lanes] * adjoint + gathered[back, group:, source]
        for k in ORDER:
            back_copy(piece, k, chip).start()
        lanes = lanes_of(piece)
        chips_ref[0, chip, :, lanes] = ready[chip, :, lanes]
        onward(piece, chip).start()
    for piece in pieces:
        for k in ORDER:
            back_copy(piece, k, None).wait_recv()
            onward(piece, chip_after(k)).start()
    for piece in pieces:
        for k in ORDER:
            out_copy(piece, k, None).wait_send()
            back_copy(piece, k, None).wait_send()
        for slot in range(chips):
            copy = onward(piece, slot)
            copy.wait_send()
            copy.wait_recv()
        swap(piece, theirs_ref, 0).wait_send()
        swap(piece, mine_ref, 1).wait_send()
        swap(piece, mine_ref, 1).wait_recv()
    own_decay.wait_send()


def carry_stage(group, *operands):
    chips, rows, width = STATE // group, 2 * group, INNER // 2
    wide = jax.ShapeDtypeStruct((ROWS, INNER), F32)
    both = jax.ShapeDtypeStruct((2, chips, rows, width), F32)
    in_vmem = pl.BlockSpec(memory_space=pltpu.VMEM)
    dma = pltpu.SemaphoreType.DMA((len(PIECES), chips))
    three = pltpu.SemaphoreType.DMA((2 * len(PIECES) + 1,))
    half = pltpu.VMEM((chips, rows, width), F32)
    more = pltpu.VMEM((chips, rows, width + LANES), F32)
    square = pltpu.VMEM((ROWS, ROWS), F32)
    lhs = pltpu.VMEM((2 * STATE, 2 * ROWS), BF16)
    shapes = (
        both, both, wide, wide,
        jax.ShapeDtypeStruct((ROWS, ROWS), F32),
        jax.ShapeDtypeStruct((ROWS, 2 * STATE), F32),
        jax.ShapeDtypeStruct((8, LANES), F32),
    )
    return pl.pallas_call(
        functools.partial(carry_kernel, group),
        in_specs=[in_vmem] * len(operands),
        out_specs=[in_vmem] * len(shapes),
        out_shape=shapes,
        scratch_shapes=[
            half, half, more, more, half, pltpu.VMEM((chips, width), F32), square, square, lhs, lhs,
            dma, dma, dma, dma, dma, dma, three, three,
        ],
        compiler_params=pltpu.CompilerParams(vmem_limit_bytes=CARRY_BYTES, collective_id=2, has_side_effects=True),
        name="carry",
    )(*operands)


def conv_backward(grad, shifted, taps, valid):
    width = grad.shape[1]
    zeros = jnp.zeros((8, width), F32)
    total = jnp.concatenate([zeros, grad * taps[3:4]], axis=0)
    parts = [jnp.sum(grad * shifted[0], axis=0, keepdims=True)]
    for back in range(1, CONV):
        parts.insert(0, jnp.sum(grad * shifted[back], axis=0, keepdims=True))
        moved = jnp.concatenate([zeros, grad * valid[:, back - 1 : back] * taps[3 - back : 4 - back], zeros], axis=0)
        total = total + moved[back : back + ROWS + 8]
    parts.append(jnp.sum(grad, axis=0, keepdims=True))
    parts.append(jnp.zeros((3, width), F32))
    return total, jnp.concatenate(parts, axis=0)


def finish_kernel(group, half_ref, x_ref, tail_ref, taps_ref, xs_ref, tails_ref, tapss_ref, valid_ref, cot_ref, both_ref,
                  out_in_ref, grad_in_ref, chip_ref, local_ref, bc_ref, small_ref, own_ref, partner_ref, score_grad_ref,
                  run_ref, dt_ref, sig_ref, sigsum_ref,
                  out_ref, grad_ref, end_ref, borrowed_ref, taps_grad_ref, grads_ref, ends_ref, borroweds_ref,
                  tapss_grad_ref, heads_ref,
                  lhs_hi, lhs_lo, bc_grad, by_head, by_token):
    tile = pl.program_id(0)
    valid = valid_ref[...]

    @pl.when(tile == 0)
    def _():
        for at, source, late in ((0, STATE, False), (ROWS, 0, True)):
            pick = interleave(group, late).astype(BF16)
            first, second = halves(bc_ref[:, source : source + STATE])
            lhs_hi[at : at + ROWS, :] = mm_nt(first, pick).astype(BF16)
            lhs_lo[at : at + ROWS, :] = mm_nt(second, pick).astype(BF16)
        bc_grad[...] = jnp.zeros_like(bc_grad)
        by_head[...] = jnp.zeros_like(by_head)
        by_token[...] = jnp.zeros_like(by_token)

    total, shifted = convolve(tail_ref[...].astype(F32), x_ref[...].astype(F32), taps_ref[...], valid)
    gate = sigmoid(total)
    act = total * gate
    upstream = cot_ref[...].astype(F32)
    here = tile_at(tile, half_ref)
    weight = spread_heads(both_ref, here)
    leave, entry = weight[:ROWS], weight[ROWS:]
    by_row = spread_exact(
        jnp.concatenate([own_ref[...], partner_ref[...], small_ref[...]], axis=0), head_columns(here)
    )
    even = half_ref[2] == 0
    earlier, later = even_odd(even, by_row)
    weight_state, weight_adjoint = jnp.where(even, 1.0, earlier), jnp.where(even, later, 1.0)
    with_state, with_adjoint = jnp.where(even, 0.0, 1.0), jnp.where(even, 1.0, 0.0)
    states = jnp.concatenate(
        [
            weight_state * chip_ref[:, :group, :] + with_state * local_ref[:, :group, :],
            weight_adjoint * chip_ref[:, group:, :] + with_adjoint * local_ref[:, group:, :],
        ],
        axis=1,
    ).reshape(2 * STATE, TILE)
    states_hi, states_lo = halves(states)
    read = mm(lhs_hi[...], states_hi) + mm(lhs_hi[...], states_lo) + mm(lhs_lo[...], states_hi)
    one_hot = head_columns(here)
    gain = by_row[18:19]
    through_state = out_in_ref[...] + entry * read[:ROWS]
    out_ref[...] = (through_state + gain * act).astype(BF16)
    act_grad_late = leave * read[ROWS:]
    act_grad = grad_in_ref[...] + act_grad_late

    first, second = halves(jnp.concatenate([entry * upstream, leave * act], axis=0))
    bc_grad[...] += mm_nt(first, states_hi) + mm_nt(first, states_lo) + mm_nt(second, states_hi)

    first, second = halves(jnp.concatenate([upstream * through_state, act * act_grad], axis=0))
    by_token[...] += mm_nt(first, one_hot) + mm_nt(second, one_hot)
    crossed = states * pltpu.roll(states, group, 0)
    crossed = jnp.where(iota((2 * STATE, TILE), 0) % (2 * group) >= group, crossed, 0.0)
    sums = jnp.concatenate(
        [
            jnp.sum(act * act_grad_late, axis=0, keepdims=True),
            jnp.sum(crossed, axis=0, keepdims=True),
            jnp.sum(upstream * act, axis=0, keepdims=True),
            jnp.zeros((5, TILE), F32),
        ],
        axis=0,
    )
    first = sums.astype(BF16)
    second, third = halves(sums - first.astype(F32))
    by_head[...] += mm_nt(first, one_hot) + mm_nt(second, one_hot) + mm_nt(third, one_hot)

    act_grad = act_grad + gain * upstream
    conv_grad = act_grad * (gate + act * (1.0 - gate))
    full, taps_grad_ref[...] = conv_backward(conv_grad, shifted, taps_ref[...], valid)
    borrowed_ref[...] = full[:8]
    grad_ref[...] = full[8:].astype(BF16)
    end_ref[...] = full[ROWS - 8 :]

    @pl.when(tile == TILES - 1)
    def _():
        score_grad = score_grad_ref[...]
        keys, reads = bc_ref[:, :STATE], bc_ref[:, STATE:]
        reads_grad = exact(bc_grad[:ROWS], interleave(group, False)) + exact(score_grad, keys)
        keys_grad = exact(bc_grad[ROWS:], interleave(group, True)) + exact(score_grad.T, reads)
        total, shifted = convolve(tails_ref[...].astype(F32), xs_ref[...].astype(F32), tapss_ref[...], valid)
        gate = sigmoid(total)
        small_grad = jnp.concatenate([keys_grad, reads_grad], axis=1) * (gate + total * gate * (1.0 - gate))
        full, tapss_grad_ref[...] = conv_backward(small_grad, shifted, tapss_ref[...], valid)
        borroweds_ref[...] = full[:8]
        grads_ref[...] = full[8:].astype(BF16)
        ends_ref[...] = full[ROWS - 8 :]

        read_sum, added_sum = by_token[:ROWS], by_token[ROWS:]
        at_end = by_head[0:1, :] + own_ref[0:1, :] * by_head[1:2, :]
        run_grad = read_sum - added_sum + jnp.where(iota((ROWS, LANES), 0) == ROWS - 1, at_end, 0.0)
        alog_grad = jnp.sum(run_grad * run_ref[...], axis=0, keepdims=True)
        bias_grad = jnp.sum(added_sum / dt_ref[...] * sig_ref[...], axis=0, keepdims=True)
        rate = jnp.exp(small_ref[1:2, :])
        bias_grad = bias_grad - rate * jnp.sum(run_grad * sigsum_ref[...], axis=0, keepdims=True)
        heads_ref[...] = jnp.concatenate([bias_grad, alog_grad, by_head[2:3, :], jnp.zeros((5, LANES), F32)], axis=0)


def finish_stage(group, half, *operands):
    square = whole((ROWS, LANES))
    eight = whole((8, LANES))
    shapes = (
        jax.ShapeDtypeStruct((ROWS, INNER), BF16),
        jax.ShapeDtypeStruct((ROWS, INNER), BF16),
        jax.ShapeDtypeStruct((16, INNER), F32),
        jax.ShapeDtypeStruct((8, INNER), F32),
        jax.ShapeDtypeStruct((8, INNER), F32),
        jax.ShapeDtypeStruct((ROWS, 2 * STATE), BF16),
        jax.ShapeDtypeStruct((16, 2 * STATE), F32),
        jax.ShapeDtypeStruct((8, 2 * STATE), F32),
        jax.ShapeDtypeStruct((8, 2 * STATE), F32),
        jax.ShapeDtypeStruct((8, LANES), F32),
    )
    states = pl.BlockSpec(
        (None, STATE // group, 2 * group, TILE), lambda i, half: (i // HALF_TILES, 0, 0, lax.rem(i, HALF_TILES))
    )
    return call(
        functools.partial(finish_kernel, group), "finish", half, TILES,
        [
            tile_spec(ROWS), tile_spec(8), tile_spec(8),
            small_spec(ROWS), small_spec(8), small_spec(8),
            whole((ROWS, 8)), tile_spec(ROWS), whole((2 * ROWS, 2 * LANES)),
            tile_spec(ROWS), tile_spec(ROWS), states, states,
            whole((ROWS, 2 * STATE)), eight, eight, eight, whole((ROWS, ROWS)), square, square, square, square,
        ],
        [tile_spec(part.shape[0]) for part in shapes[:5]] + [whole(part.shape) for part in shapes[5:]],
        shapes,
        [
            pltpu.VMEM((2 * ROWS, 2 * STATE), BF16), pltpu.VMEM((2 * ROWS, 2 * STATE), BF16),
            pltpu.VMEM((2 * ROWS, 2 * STATE), F32), pltpu.VMEM((8, LANES), F32), pltpu.VMEM((2 * ROWS, LANES), F32),
        ],
        operands,
    )


def total_kernel(scale, taps_ref, small_ref, heads_ref, borrowed_ref, borroweds_ref, end_ref, ends_ref, keep_ref,
                 sums_ref, last_ref,
                 parts, slots, piece, far_slots, result, got, got_small, send, receive, far_send, far_receive, back_send,
                 back_receive, rows_send, rows_receive):
    shards, groups = lax.axis_size("seq"), lax.axis_size("dp")
    others = groups * shards // 8
    place, group = lax.axis_index("seq"), lax.axis_index("dp")
    before = (group, lax.rem(place + shards - 1, shards))
    after = (group, lax.rem(place + 1, shards))
    barrier = pltpu.get_barrier_semaphore()
    for peers, size in ((near, 8), (far, others)):
        for k in range(1, size):
            pl.semaphore_signal(barrier, inc=1, device_id=peers(k)[0], device_id_type=MESH)
    for peer in (before, after):
        pl.semaphore_signal(barrier, inc=1, device_id=peer, device_id_type=MESH)
    pl.semaphore_wait(barrier, 7 + others - 1 + 2)

    depth = parts.shape[1]
    wide = CH // LANES
    for at in range(8 * depth // 8):
        if at < INNER // LANES:
            block = taps_ref[:, LANES * at : LANES * (at + 1)]
        elif at < wide:
            block = small_ref[:, LANES * at - INNER : LANES * (at + 1) - INNER]
        elif at == wide:
            block = heads_ref[...]
        else:
            block = jnp.zeros((8, LANES), F32)
        parts[at % 8, 8 * (at // 8) : 8 * (at // 8) + 8, :] = block
    send_all(near, 8, lambda slot: parts.at[slot], slots, send, receive)
    returns = [
        pltpu.make_async_remote_copy(
            src_ref=source, dst_ref=target, send_sem=rows_send.at[at], recv_sem=rows_receive.at[at], device_id=before,
            device_id_type=MESH,
        )
        for at, (source, target) in enumerate(((borrowed_ref, got), (borroweds_ref, got_small)))
    ]

    @pl.when(place > 0)
    def _():
        for copy in returns:
            copy.start()

    _, own = near(0)
    _, far_own = far(0)
    slots[own] = parts[own]
    wait_all(near, 8, lambda slot: parts.at[slot], slots, send, receive)
    piece[...] = jnp.sum(slots[...], axis=0)
    send_all(far, others, lambda slot: piece, far_slots, far_send, far_receive)
    far_slots[far_own] = piece[...]
    wait_all(far, others, lambda slot: piece, far_slots, far_send, far_receive)
    piece[...] = jnp.sum(far_slots[...], axis=0) * scale
    send_all(near, 8, lambda slot: piece, result, back_send, back_receive)
    result[own] = piece[...]

    @pl.when(place > 0)
    def _():
        for copy in returns:
            copy.wait_send()

    @pl.when(place < shards - 1)
    def _():
        for copy in returns:
            copy.wait_recv()
        keep = keep_ref[:, 0:1]
        for lanes, source, end in ((slice(0, INNER), got, end_ref), (slice(INNER, CH), got_small, ends_ref)):
            late = iota(source.shape, 0) >= 8 - CONV + 1
            rows = jnp.concatenate([end[:8, :], end[8:, :] + jnp.where(late, source[...] * keep, 0.0)], axis=0)
            last_ref[:, lanes] = rows.astype(BF16)

    @pl.when(place == shards - 1)
    def _():
        last_ref[:, :INNER] = end_ref[...].astype(BF16)
        last_ref[:, INNER:] = ends_ref[...].astype(BF16)

    wait_all(near, 8, lambda slot: piece, result, back_send, back_receive)
    for at in range(wide + 1):
        sums_ref[:, LANES * at : LANES * (at + 1)] = result[at % 8, 8 * (at // 8) : 8 * (at // 8) + 8, :]


def layout_kernel(sums_ref, last_ref, grad_ref, grads_ref, weight_ref, bias_ref, dt_bias_ref, a_log_ref, gain_ref,
                  whole_ref):
    step = pl.program_id(0)

    @pl.when(step == 0)
    def _():
        weight_ref[...] = sums_ref[:CONV, :CH]
        bias_ref[...] = sums_ref[CONV : CONV + 1, :CH].reshape(CH)
        for at, target in enumerate((dt_bias_ref, a_log_ref, gain_ref)):
            target[...] = sums_ref[at : at + 1, CH : CH + HEADS].reshape(HEADS)

    @pl.when(step < pl.num_programs(0) - 1)
    def _():
        whole_ref[:, :INNER] = grad_ref[...]
        whole_ref[:, INNER:] = grads_ref[...]

    @pl.when(step == pl.num_programs(0) - 1)
    def _():
        whole_ref[: whole_ref.shape[0] - 16, :INNER] = grad_ref[: whole_ref.shape[0] - 16, :]
        whole_ref[: whole_ref.shape[0] - 16, INNER:] = grads_ref[: whole_ref.shape[0] - 16, :]
        whole_ref[whole_ref.shape[0] - 16 :, :] = last_ref[...]


def layout_stage(sums, last, grad, grads):
    rows = 32
    shapes = (
        jax.ShapeDtypeStruct((CONV, CH), F32),
        jax.ShapeDtypeStruct((CH,), F32),
        jax.ShapeDtypeStruct((HEADS,), F32),
        jax.ShapeDtypeStruct((HEADS,), F32),
        jax.ShapeDtypeStruct((HEADS,), F32),
        jax.ShapeDtypeStruct((ROWS, CH), BF16),
    )
    blocks = [pl.BlockSpec((rows, width), lambda i: (i, 0)) for width in (INNER, 2 * STATE, CH)]
    return pl.pallas_call(
        layout_kernel,
        grid=(ROWS // rows,),
        in_specs=[whole(sums.shape), whole(last.shape)] + blocks[:2],
        out_specs=[whole(part.shape) for part in shapes[:5]] + blocks[2:],
        out_shape=shapes,
        name="layout",
    )(sums, last, grad, grads)


def total_stage(others, scale, *operands):
    depth = 8 * pl.cdiv(CH // LANES + 1, 8)
    in_vmem = pl.BlockSpec(memory_space=pltpu.VMEM)
    shapes = (jax.ShapeDtypeStruct((8, CH + LANES), F32), jax.ShapeDtypeStruct((16, CH), BF16))
    dma = pltpu.SemaphoreType.DMA
    return pl.pallas_call(
        functools.partial(total_kernel, scale),
        in_specs=[in_vmem] * len(operands),
        out_specs=[in_vmem] * len(shapes),
        out_shape=shapes,
        scratch_shapes=[
            pltpu.VMEM((8, depth, LANES), F32), pltpu.VMEM((8, depth, LANES), F32),
            pltpu.VMEM((depth, LANES), F32), pltpu.VMEM((others, depth, LANES), F32),
            pltpu.VMEM((8, depth, LANES), F32),
            pltpu.VMEM((8, INNER), F32), pltpu.VMEM((8, 2 * STATE), F32),
            dma((8,)), dma((8,)), dma((others,)), dma((others,)), dma((8,)), dma((8,)), dma((2,)), dma((2,)),
        ],
        compiler_params=pltpu.CompilerParams(
            vmem_limit_bytes=VMEM_BYTES, collective_id=1, has_side_effects=True
        ),
        name="totals",
    )(*operands)


def on_device(conv_input, doc_start, conv_weight, conv_bias, dt_raw, dt_bias, a_log, skip_gain, cotangent):
    shards, place = lax.axis_size("seq"), lax.axis_index("seq")
    group = 2 * STATE // shards
    core = lax.rem(place, 2)
    half = jnp.stack([core, place // 2, core])
    run, runT, dt, dtT, both, sig, sigsum, mask, valid, keep, tail, own, small, taps = head_stage(
        dt_raw.T, dt_bias[None], a_log[None], skip_gain[None], doc_start[None], conv_weight, conv_bias[None], conv_input
    )
    tail = lax.ppermute(tail, "seq", [(i, i + 1) for i in range(shards - 1)])
    chips, others, out_in, grad_in, score_grad, bc, partner = carry_stage(
        group, conv_input, tail, taps, valid, cotangent, both, own, runT, dtT, mask
    )
    out, grad, end, borrowed, taps_grad, grads, ends, borroweds, tapss_grad, heads = finish_stage(
        group, half, conv_input, tail, taps, conv_input, tail, taps, valid, cotangent, both, out_in, grad_in, chips,
        others, bc, small, own, partner, score_grad, run, dt, sig, sigsum,
    )
    groups = lax.axis_size("dp")
    sums, last = total_stage(
        groups * shards // 8, float(groups * shards * ROWS) ** (-0.5), taps_grad, tapss_grad, heads, borrowed, borroweds,
        end, ends, keep,
    )
    weight_grad, bias_grad, dt_bias_grad, a_log_grad, gain_grad, whole_grad = layout_stage(sums, last, grad, grads)
    return (out, whole_grad, weight_grad, bias_grad, dt_bias_grad, a_log_grad, gain_grad)


def solution(mesh):
    sharded = P(("dp", "seq"), None)
    return jax.shard_map(
        on_device,
        mesh=mesh,
        in_specs=(sharded, P(("dp", "seq")), P(), P(), sharded, P(), P(), P(), sharded),
        out_specs=(sharded, sharded, P(), P(), P(), P(), P()),
        check_vma=False,
    )
```

```python
import functools

import jax
import jax.numpy as jnp
from jax import lax
from jax.experimental import pallas as pl
from jax.experimental.pallas import tpu as pltpu
from jax.sharding import PartitionSpec as P

HEADS = 80
HEAD_DIM = 64
STATE = 128
CONV = 4
INNER = 5120
CH = 5376
ROWS = 128
TILE = 512
TILES = INNER // TILE
TILE_HEADS = TILE // HEAD_DIM
LANES = 128

F32 = jnp.float32
BF16 = jnp.bfloat16
EXACT = lax.Precision.HIGHEST
HALF_TILES = TILES // 2
VMEM_BYTES = 20 << 20
CARRY_BYTES = 28 << 20
MESH = pl.DeviceIdType.MESH


def iota(shape, axis):
    return lax.broadcasted_iota(jnp.int32, shape, axis)


def halves(value):
    high = value.astype(BF16)
    return high, (value - high.astype(F32)).astype(BF16)


def mm(a, b):
    return lax.dot_general(a, b, (((1,), (0,)), ((), ())), preferred_element_type=F32)


def mm_nt(a, b):
    return lax.dot_general(a, b, (((1,), (1,)), ((), ())), preferred_element_type=F32)


def exact(a, b):
    return lax.dot_general(
        a, b, (((1,), (0,)), ((), ())), precision=EXACT, preferred_element_type=F32
    )


def spread_exact(rows, one_hot):
    first, rest = rows.astype(BF16), rows
    rest = rest - first.astype(F32)
    second, third = halves(rest)
    return mm(first, one_hot) + mm(second, one_hot) + mm(third, one_hot)


def interleave(group, late):
    row, col = iota((2 * STATE, STATE), 0), iota((2 * STATE, STATE), 1)
    place = row % (2 * group)
    first = group if late else 0
    here = (place >= first) & (place < first + group)
    return jnp.where(here & (col == group * (row // (2 * group)) + place - first), 1.0, 0.0)


def head_columns(tile):
    head, col = iota((LANES, TILE), 0), iota((LANES, TILE), 1)
    return jnp.where(head == TILE_HEADS * tile + col // HEAD_DIM, 1.0, 0.0).astype(BF16)


def spread_heads(both_ref, tile):
    one_hot = head_columns(tile)
    return mm(both_ref[...], jnp.concatenate([one_hot, one_hot], axis=0))


def convolve(tail, rows, taps, valid):
    extended = jnp.concatenate([tail, rows], axis=0)
    total = taps[4:5] + taps[3:4] * rows
    shifted = [rows]
    for back in range(1, CONV):
        moved = extended[8 - back : 8 - back + ROWS] * valid[:, back - 1 : back]
        shifted.append(moved)
        total = total + taps[3 - back : 4 - back] * moved
    return total, shifted


def sigmoid(v):
    return 1.0 / (1.0 + jnp.exp(-v))


def near(k):
    place = lax.axis_index("seq")
    slot = lax.rem(lax.rem(place, 8) + k, 8)
    return (lax.axis_index("dp"), place - lax.rem(place, 8) + slot), slot


def far(k):
    place, group = lax.axis_index("seq"), lax.axis_index("dp")
    runs = lax.axis_size("seq") // 8
    slot = lax.rem(group * runs + place // 8 + k, lax.axis_size("dp") * runs)
    return (slot // runs, lax.rem(slot, runs) * 8 + lax.rem(place, 8)), slot


def send_all(peers, size, source, target, send, receive):
    _, own = peers(0)
    for k in range(1, size):
        peer, slot = peers(k)
        pltpu.make_async_remote_copy(
            src_ref=source(slot), dst_ref=target.at[own], send_sem=send.at[slot], recv_sem=receive.at[own],
            device_id=peer, device_id_type=MESH,
        ).start()


def wait_all(peers, size, source, target, send, receive):
    for k in range(1, size):
        peer, slot = peers(k)
        copy = pltpu.make_async_remote_copy(
            src_ref=source(slot), dst_ref=target.at[slot], send_sem=send.at[slot], recv_sem=receive.at[slot],
            device_id=peer, device_id_type=MESH,
        )
        copy.wait_send()
        copy.wait_recv()


def head_kernel(raw_in_ref, heads_in_ref, row_ref, weight_ref, bias_ref, end_ref, run_ref, runT_ref,
                dt_ref, dtT_ref, both_ref, sig_ref, sigsum_ref, mask_ref, valid_ref, keep_ref, tail_ref, own_ref,
                small_ref, taps_ref, raw):
    taps_ref[:CONV, :] = weight_ref[...]
    taps_ref[CONV:, :] = jnp.broadcast_to(bias_ref[...], (8 - CONV, CH))
    small_ref[...] = jnp.zeros_like(small_ref)
    small_ref[:3, :HEADS] = heads_in_ref[...]
    reset_row = row_ref[...].astype(F32)
    token, other = iota((ROWS, ROWS), 0), iota((ROWS, ROWS), 1)
    reset_col = jnp.sum(jnp.where(token == other, reset_row, 0.0), axis=1, keepdims=True)
    low, high = token >= other, token <= other
    segment_col = jnp.sum(jnp.where(low, reset_row, 0.0), axis=1, keepdims=True)
    segment_row = jnp.sum(jnp.where(high, reset_col, 0.0), axis=0, keepdims=True)
    mask_ref[0] = jnp.where(low & (segment_col == segment_row), 1.0, 0.0)
    mask_ref[1] = jnp.where(high & (segment_col == segment_row), 1.0, 0.0)

    kept = jnp.broadcast_to(1.0 - reset_col, (ROWS, LANES))
    one_back = jnp.where(token < 1, 1.0, pltpu.roll(kept, 1, 0))
    two_back = jnp.where(token < 2, 1.0, pltpu.roll(kept, 2, 0))
    valid = jnp.where(other == 0, kept, jnp.where(other == 1, kept * one_back, kept * one_back * two_back))
    valid_ref[...] = valid[:, :8]
    one_on, two_on = pltpu.roll(kept, ROWS - 1, 0), pltpu.roll(kept, ROWS - 2, 0)
    keep = jnp.where(
        token == ROWS - 1, 1.0, jnp.where(token == ROWS - 2, one_on, jnp.where(token == ROWS - 3, one_on * two_on, 0.0))
    )[ROWS - 8 :]
    keep_ref[...] = keep
    tail_ref[...] = (end_ref[8:, :].astype(F32) * keep[:, 0:1]).astype(BF16)

    raw[...] = jnp.zeros_like(raw)
    raw[:HEADS, :] = raw_in_ref[...]
    biased = raw[...].T + small_ref[0:1, :]
    dt = jnp.maximum(biased, 0.0) + jnp.log1p(jnp.exp(-jnp.abs(biased)))
    decay = -jnp.exp(small_ref[1:2, :]) * dt
    lower = jnp.where(low, 1.0, 0.0)
    running = exact(lower, decay)
    last = running[ROWS - 1 : ROWS]
    count = segment_col[ROWS - 1 : ROWS]
    untouched = jnp.where(segment_col == 0.0, 1.0, 0.0)
    entry = jnp.exp(running) * untouched
    own_ref[...] = jnp.broadcast_to(entry[ROWS - 1 : ROWS], own_ref.shape)
    sig = sigmoid(biased)
    sig_ref[...] = sig
    sigsum_ref[...] = exact(lower, sig)
    run_ref[...] = running
    runT_ref[...] = running.T
    dt_ref[...] = dt
    dtT_ref[...] = dt.T
    leave = jnp.exp(last - running) * jnp.where(segment_col == count, 1.0, 0.0) * dt
    for at, part in ((0, leave), (ROWS, entry)):
        first, second = halves(part)
        both_ref[at : at + ROWS, :LANES] = first
        both_ref[at : at + ROWS, LANES:] = second


def head_stage(raw, heads_in, row, weight, bias, conv_input):
    square = jax.ShapeDtypeStruct((ROWS, LANES), F32)
    eight = jax.ShapeDtypeStruct((8, LANES), F32)
    shapes = (
        square, square, square, square,
        jax.ShapeDtypeStruct((2 * ROWS, 2 * LANES), BF16),
        square, square,
        jax.ShapeDtypeStruct((2, ROWS, ROWS), F32),
        jax.ShapeDtypeStruct((ROWS, 8), F32),
        eight,
        jax.ShapeDtypeStruct((8, CH), BF16),
        eight, eight,
        jax.ShapeDtypeStruct((8, CH), F32),
    )
    given = (raw, heads_in, row, weight, bias)
    return pl.pallas_call(
        head_kernel,
        grid=(1,),
        in_specs=[whole(part.shape) for part in given] + [pl.BlockSpec((16, CH), lambda *at: (ROWS // 16 - 1, 0))],
        out_specs=[whole(part.shape) for part in shapes],
        out_shape=shapes,
        scratch_shapes=[pltpu.VMEM((ROWS, LANES), F32)],
        compiler_params=pltpu.CompilerParams(vmem_limit_bytes=VMEM_BYTES),
        name="heads",
    )(*given, conv_input)


def whole(shape):
    return pl.BlockSpec(shape, lambda *at: (0,) * len(shape))


def call(kernel, name, half, grid, in_specs, out_specs, out_shape, scratch_shapes, operands, aliases={}):
    return pl.pallas_call(
        kernel,
        grid_spec=pltpu.PrefetchScalarGridSpec(
            num_scalar_prefetch=1, grid=(grid,), in_specs=in_specs, out_specs=out_specs, scratch_shapes=scratch_shapes
        ),
        out_shape=out_shape,
        input_output_aliases=aliases,
        compiler_params=pltpu.CompilerParams(vmem_limit_bytes=VMEM_BYTES),
        name=name,
    )(half, *operands)


def tile_at(i, half):
    return lax.rem(i + HALF_TILES * half[0], TILES)


def tile_spec(rows):
    return pl.BlockSpec((rows, TILE), lambda i, half: (0, tile_at(i, half)))


def small_spec(rows):
    return pl.BlockSpec((rows, 2 * STATE), lambda *at: (0, INNER // (2 * STATE)))


def pair_spec(shape, first):
    if first:
        return pl.BlockSpec(shape[:2] + (TILE,), lambda i, half: (0, 0, jnp.minimum(i, HALF_TILES - 1)))
    return pl.BlockSpec(shape[:2] + (TILE,), lambda i, half: (0, 0, jnp.maximum(i - HALF_TILES, 0)))


def local_start(group, xs, tails, tapss, valid, bc_ref, lhs_hi, lhs_lo):
    total, _ = convolve(tails.astype(F32), xs.astype(F32), tapss, valid)
    small = total * sigmoid(total)
    bc_ref[...] = small
    for at, late in ((0, False), (STATE, True)):
        pick = interleave(group, late).astype(BF16)
        first, second = halves(small[:, at : at + STATE])
        lhs_hi[:, at : at + ROWS] = mm_nt(pick, first).astype(BF16)
        lhs_lo[:, at : at + ROWS] = mm_nt(pick, second).astype(BF16)


def local_tile(tile, x_ref, tail_ref, taps_ref, valid_ref, cot_ref, both_ref, lhs_hi, lhs_lo):
    columns = pl.ds(pl.multiple_of(TILE * tile, TILE), TILE)
    total, _ = convolve(
        tail_ref[:, columns].astype(F32), x_ref[:, columns].astype(F32), taps_ref[:, columns], valid_ref[...]
    )
    act = total * sigmoid(total)
    weight = spread_heads(both_ref, tile)
    first, second = halves(weight * jnp.concatenate([act, cot_ref[:, columns].astype(F32)], axis=0))
    return mm(lhs_hi[...], first) + mm(lhs_hi[...], second) + mm(lhs_lo[...], first)


def within_start(bc_ref, mask_ref, score_grad_ref, score, scoreT):
    keys, reads = bc_ref[:, :STATE], bc_ref[:, STATE:]
    keys_hi, keys_lo = halves(keys)
    reads_hi, reads_lo = halves(reads)
    score[...] = mask_ref[0] * (mm_nt(reads_hi, keys_hi) + mm_nt(reads_hi, keys_lo) + mm_nt(reads_lo, keys_hi))
    scoreT[...] = mask_ref[1] * (mm_nt(keys_hi, reads_hi) + mm_nt(keys_hi, reads_lo) + mm_nt(keys_lo, reads_hi))
    score_grad_ref[...] = jnp.zeros_like(score_grad_ref)


def within_tile(tile, x_ref, tail_ref, taps_ref, valid_ref, cot_ref, runT_ref, dtT_ref, out_ref, grad_ref,
                score_grad_ref, score, scoreT):
    at = pl.multiple_of(TILE * tile, TILE)
    columns = pl.ds(at, TILE)
    total, _ = convolve(
        tail_ref[:, columns].astype(F32), x_ref[:, columns].astype(F32), taps_ref[:, columns], valid_ref[...]
    )
    act = total * sigmoid(total)
    rows = pl.ds(pl.multiple_of(TILE_HEADS * tile, TILE_HEADS), TILE_HEADS)
    run_rows, dt_rows = runT_ref[rows, :], dtT_ref[rows, :]
    run, dt = run_rows.T, dt_rows.T
    left = iota((ROWS, LANES), 1) < HEAD_DIM
    left = jnp.where(left, 1.0, 0.0).astype(BF16)
    right = 1.0 - left
    score_grad = score_grad_ref[...]
    for pair in range(TILE_HEADS // 2):
        lanes = slice(LANES * pair, LANES * (pair + 1))
        here = pl.ds(at + LANES * pair, LANES)
        spread, weights, weightsT = [], [], []
        for head in (2 * pair, 2 * pair + 1):
            difference = run[:, head : head + 1] - run_rows[head : head + 1, :]
            step = jnp.exp(jnp.minimum(difference, 0.0)) * dt_rows[head : head + 1, :]
            spread.append(step)
            weights.append(step * score[...])
            weightsT.append(jnp.exp(jnp.minimum(-difference, 0.0)) * dt[:, head : head + 1] * scoreT[...])
        x_hi, x_lo = halves(act[:, lanes])
        upstream = cot_ref[:, here]
        x_hi2 = jnp.concatenate([x_hi * left, x_hi * right], axis=0)
        x_lo2 = jnp.concatenate([x_lo * left, x_lo * right], axis=0)
        upstream2 = jnp.concatenate([upstream * left, upstream * right], axis=0)
        w_hi, w_lo = halves(jnp.concatenate(weights, axis=1))
        wide = mm(w_hi, jnp.concatenate([x_hi2, x_lo2], axis=1))
        out_ref[:, here] = wide[:, :LANES] + wide[:, LANES:] + mm(w_lo, x_hi2)
        wt_hi, wt_lo = halves(jnp.concatenate(weightsT, axis=1))
        grad_ref[:, here] = mm(wt_hi, upstream2) + mm(wt_lo, upstream2)
        inner = mm_nt(upstream2, jnp.concatenate([x_hi, x_lo], axis=0))
        inner = inner[:, :ROWS] + inner[:, ROWS:]
        score_grad = score_grad + inner[:ROWS] * spread[0] + inner[ROWS:] * spread[1]
    score_grad_ref[...] = score_grad


def even_odd(even, both):
    own, partner = both[0:1], both[8:9]
    return jnp.where(even, own, partner)[None], jnp.where(even, partner, own)[None]


ORDER = (10, 1, 4, 3, 12, 11, 9, 14, 6, 2, 8, 5, 15, 7, 13)


def chip_after(k):
    chip = lax.axis_index("seq") // 2
    return lax.rem(chip // 4 + k // 4, 4) * 4 + lax.rem(lax.rem(chip, 4) + k % 4, 4)


def same_core(chip):
    return (lax.axis_index("dp"), 2 * chip + lax.rem(lax.axis_index("seq"), 2))


def chip_copy(source, target, k, slot, send, receive):
    other = chip_after(k)
    slot = other if slot is None else slot
    return pltpu.make_async_remote_copy(
        src_ref=source(other), dst_ref=target(slot), send_sem=send.at[other], recv_sem=receive.at[slot],
        device_id=same_core(other), device_id_type=MESH,
    )


PIECES = ((0, 1), (1, 3), (3, 5))


def pair_copy(source, target, send, receive):
    place = lax.axis_index("seq")
    return pltpu.make_async_remote_copy(
        src_ref=source, dst_ref=target, send_sem=send, recv_sem=receive,
        device_id=(lax.axis_index("dp"), place + 1 - 2 * lax.rem(place, 2)), device_id_type=MESH,
    )


def carry_kernel(group, x_ref, tail_ref, taps_ref, valid_ref, cot_ref, both_ref, own_ref, runT_ref, dtT_ref, mask_ref,
                 chips_ref, others_ref, out_ref, grad_ref, score_grad_ref, bc_ref, partner_ref,
                 mine_ref, theirs_ref, joined, gathered, ready, decay, score, scoreT, lhs_hi, lhs_lo, send, receive,
                 back_send, back_receive, on_send, on_receive, pair_send, pair_receive):
    chips = mine_ref.shape[0]
    place = lax.axis_index("seq")
    chip, core = place // 2, lax.rem(place, 2)
    even = core == 0
    barrier = pltpu.get_barrier_semaphore()
    pl.semaphore_signal(
        barrier, inc=1, device_id=(lax.axis_index("dp"), place + 1 - 2 * core), device_id_type=MESH
    )
    for k in ORDER:
        pl.semaphore_signal(barrier, inc=1, device_id=same_core(chip_after(k)), device_id_type=MESH)
    local_start(
        group, x_ref[:, INNER:], tail_ref[:, INNER:], taps_ref[:, INNER:], valid_ref[...], bc_ref, lhs_hi, lhs_lo
    )

    def local_piece(half, piece, target):
        def tile_step(at, carry):
            result = local_tile(
                HALF_TILES * half + at, x_ref, tail_ref, taps_ref, valid_ref, cot_ref, both_ref, lhs_hi, lhs_lo
            )
            target[:, :, pl.ds(pl.multiple_of(TILE * at, TILE), TILE)] = result.reshape(chips, 2 * group, TILE)
            return carry

        lax.fori_loop(*PIECES[piece], tile_step, 0)

    def lanes_of(piece):
        first, last = PIECES[piece]
        return slice(TILE * first, TILE * last)

    def sent_lanes(piece):
        first, last = PIECES[piece]
        return slice(0 if piece == 0 else LANES + TILE * first, LANES + TILE * last)

    def swap(piece, source, at):
        lanes, slot = lanes_of(piece), 2 * piece + at
        return pair_copy(
            source.at[:, :, lanes], others_ref.at[at, :, :, lanes], pair_send.at[slot], pair_receive.at[slot]
        )

    def out_copy(piece, k, slot):
        lanes = sent_lanes(piece)
        return chip_copy(
            lambda at: joined.at[at, :, lanes], lambda at: gathered.at[at, :, lanes], k, slot, send.at[piece],
            receive.at[piece],
        )

    def back_copy(piece, k, slot):
        lanes = lanes_of(piece)
        return chip_copy(
            lambda at: ready.at[at, :, lanes], lambda at: chips_ref.at[0, at, :, lanes], k, slot, back_send.at[piece],
            back_receive.at[piece],
        )

    def onward(piece, slot):
        lanes = lanes_of(piece)
        return pair_copy(
            chips_ref.at[0, slot, :, lanes], chips_ref.at[1, slot, :, lanes], on_send.at[piece, slot],
            on_receive.at[piece, slot],
        )

    pieces = range(len(PIECES))
    own_decay = pair_copy(own_ref, partner_ref, pair_send.at[2 * len(PIECES)], pair_receive.at[2 * len(PIECES)])
    for piece in pieces:
        local_piece(1 - core, piece, theirs_ref)
        if piece == 0:
            pl.semaphore_wait(barrier, len(ORDER) + 1)
            own_decay.start()
        swap(piece, theirs_ref, 0).start()
        local_piece(core, piece, mine_ref)
        swap(piece, mine_ref, 1).start()
        if piece == 0:
            own_decay.wait_recv()
            joined[:, :, :LANES] = jnp.broadcast_to(
                (own_ref[0:1, :] * partner_ref[0:1, :])[None], joined.shape[:2] + (LANES,)
            )
        swap(piece, theirs_ref, 0).wait_recv()
        rows = jnp.concatenate([own_ref[...], partner_ref[...]], axis=0)
        for at in range(*PIECES[piece]):
            lanes = slice(TILE * at, TILE * (at + 1))
            target = slice(LANES + TILE * at, LANES + TILE * (at + 1))
            earlier, later = even_odd(even, spread_exact(rows, head_columns(HALF_TILES * core + at)))
            mine, other = mine_ref[:, :, lanes], others_ref[0, :, :, lanes]
            first, second = jnp.where(even, mine, other), jnp.where(even, other, mine)
            joined[:, :group, target] = later * first[:, :group] + second[:, :group]
            joined[:, group:, target] = first[:, group:] + earlier * second[:, group:]
        for k in ORDER:
            out_copy(piece, k, chip).start()
    gathered[chip] = joined[chip]

    within_start(bc_ref, mask_ref, score_grad_ref, score, scoreT)

    def step(tile, carry):
        within_tile(tile, x_ref, tail_ref, taps_ref, valid_ref, cot_ref, runT_ref, dtT_ref, out_ref, grad_ref,
                    score_grad_ref, score, scoreT)
        return carry

    lax.fori_loop(0, TILES, step, 0)
    score_grad_ref[...] = score_grad_ref[...] * mask_ref[0]

    for piece in pieces:
        for k in ORDER:
            out_copy(piece, k, None).wait_recv()
        by_head = jnp.max(gathered[:, :, :LANES], axis=1)
        for at in range(*PIECES[piece]):
            lanes = slice(TILE * at, TILE * (at + 1))
            source = slice(LANES + TILE * at, LANES + TILE * (at + 1))
            decay[:, lanes] = spread_exact(by_head, head_columns(HALF_TILES * core + at))
            state = jnp.zeros((group, TILE), F32)
            adjoint = jnp.zeros((group, TILE), F32)
            for here in range(chips):
                ready[here, :group, lanes] = state
                state = decay[here : here + 1, lanes] * state + gathered[here, :group, source]
                back = chips - 1 - here
                ready[back, group:, lanes] = adjoint
                adjoint = decay[back : back + 1, lanes] * adjoint + gathered[back, group:, source]
        for k in ORDER:
            back_copy(piece, k, chip).start()
        lanes = lanes_of(piece)
        chips_ref[0, chip, :, lanes] = ready[chip, :, lanes]
        onward(piece, chip).start()
    for piece in pieces:
        for k in ORDER:
            back_copy(piece, k, None).wait_recv()
            onward(piece, chip_after(k)).start()
    for piece in pieces:
        for k in ORDER:
            out_copy(piece, k, None).wait_send()
            back_copy(piece, k, None).wait_send()
        for slot in range(chips):
            copy = onward(piece, slot)
            copy.wait_send()
            copy.wait_recv()
        swap(piece, theirs_ref, 0).wait_send()
        swap(piece, mine_ref, 1).wait_send()
        swap(piece, mine_ref, 1).wait_recv()
    own_decay.wait_send()


def carry_stage(group, *operands):
    chips, rows, width = STATE // group, 2 * group, INNER // 2
    wide = jax.ShapeDtypeStruct((ROWS, INNER), F32)
    both = jax.ShapeDtypeStruct((2, chips, rows, width), F32)
    in_vmem = pl.BlockSpec(memory_space=pltpu.VMEM)
    dma = pltpu.SemaphoreType.DMA((len(PIECES), chips))
    three = pltpu.SemaphoreType.DMA((2 * len(PIECES) + 1,))
    half = pltpu.VMEM((chips, rows, width), F32)
    more = pltpu.VMEM((chips, rows, width + LANES), F32)
    square = pltpu.VMEM((ROWS, ROWS), F32)
    lhs = pltpu.VMEM((2 * STATE, 2 * ROWS), BF16)
    shapes = (
        both, both, wide, wide,
        jax.ShapeDtypeStruct((ROWS, ROWS), F32),
        jax.ShapeDtypeStruct((ROWS, 2 * STATE), F32),
        jax.ShapeDtypeStruct((8, LANES), F32),
    )
    return pl.pallas_call(
        functools.partial(carry_kernel, group),
        in_specs=[in_vmem] * len(operands),
        out_specs=[in_vmem] * len(shapes),
        out_shape=shapes,
        scratch_shapes=[
            half, half, more, more, half, pltpu.VMEM((chips, width), F32), square, square, lhs, lhs,
            dma, dma, dma, dma, dma, dma, three, three,
        ],
        compiler_params=pltpu.CompilerParams(vmem_limit_bytes=CARRY_BYTES, collective_id=2, has_side_effects=True),
        name="carry",
    )(*operands)


def conv_backward(grad, shifted, taps, valid):
    width = grad.shape[1]
    zeros = jnp.zeros((8, width), F32)
    total = jnp.concatenate([zeros, grad * taps[3:4]], axis=0)
    parts = [jnp.sum(grad * shifted[0], axis=0, keepdims=True)]
    for back in range(1, CONV):
        parts.insert(0, jnp.sum(grad * shifted[back], axis=0, keepdims=True))
        moved = jnp.concatenate([zeros, grad * valid[:, back - 1 : back] * taps[3 - back : 4 - back], zeros], axis=0)
        total = total + moved[back : back + ROWS + 8]
    parts.append(jnp.sum(grad, axis=0, keepdims=True))
    parts.append(jnp.zeros((3, width), F32))
    return total, jnp.concatenate(parts, axis=0)


def finish_kernel(group, half_ref, x_ref, tail_ref, taps_ref, xs_ref, tails_ref, tapss_ref, valid_ref, cot_ref, both_ref,
                  out_in_ref, grad_in_ref, chip_ref, local_ref, bc_ref, small_ref, own_ref, partner_ref, score_grad_ref,
                  run_ref, dt_ref, sig_ref, sigsum_ref,
                  out_ref, grad_ref, end_ref, borrowed_ref, taps_grad_ref, grads_ref, ends_ref, borroweds_ref,
                  tapss_grad_ref, heads_ref,
                  lhs_hi, lhs_lo, bc_grad, by_head, by_token):
    tile = pl.program_id(0)
    valid = valid_ref[...]

    @pl.when(tile == 0)
    def _():
        for at, source, late in ((0, STATE, False), (ROWS, 0, True)):
            pick = interleave(group, late).astype(BF16)
            first, second = halves(bc_ref[:, source : source + STATE])
            lhs_hi[at : at + ROWS, :] = mm_nt(first, pick).astype(BF16)
            lhs_lo[at : at + ROWS, :] = mm_nt(second, pick).astype(BF16)
        bc_grad[...] = jnp.zeros_like(bc_grad)
        by_head[...] = jnp.zeros_like(by_head)
        by_token[...] = jnp.zeros_like(by_token)

    total, shifted = convolve(tail_ref[...].astype(F32), x_ref[...].astype(F32), taps_ref[...], valid)
    gate = sigmoid(total)
    act = total * gate
    upstream = cot_ref[...].astype(F32)
    here = tile_at(tile, half_ref)
    weight = spread_heads(both_ref, here)
    leave, entry = weight[:ROWS], weight[ROWS:]
    by_row = spread_exact(
        jnp.concatenate([own_ref[...], partner_ref[...], small_ref[...]], axis=0), head_columns(here)
    )
    even = half_ref[2] == 0
    earlier, later = even_odd(even, by_row)
    weight_state, weight_adjoint = jnp.where(even, 1.0, earlier), jnp.where(even, later, 1.0)
    with_state, with_adjoint = jnp.where(even, 0.0, 1.0), jnp.where(even, 1.0, 0.0)
    states = jnp.concatenate(
        [
            weight_state * chip_ref[:, :group, :] + with_state * local_ref[:, :group, :],
            weight_adjoint * chip_ref[:, group:, :] + with_adjoint * local_ref[:, group:, :],
        ],
        axis=1,
    ).reshape(2 * STATE, TILE)
    states_hi, states_lo = halves(states)
    read = mm(lhs_hi[...], states_hi) + mm(lhs_hi[...], states_lo) + mm(lhs_lo[...], states_hi)
    one_hot = head_columns(here)
    gain = by_row[18:19]
    through_state = out_in_ref[...] + entry * read[:ROWS]
    out_ref[...] = (through_state + gain * act).astype(BF16)
    act_grad_late = leave * read[ROWS:]
    act_grad = grad_in_ref[...] + act_grad_late

    first, second = halves(jnp.concatenate([entry * upstream, leave * act], axis=0))
    bc_grad[...] += mm_nt(first, states_hi) + mm_nt(first, states_lo) + mm_nt(second, states_hi)

    first, second = halves(jnp.concatenate([upstream * through_state, act * act_grad], axis=0))
    by_token[...] += mm_nt(first, one_hot) + mm_nt(second, one_hot)
    crossed = states * pltpu.roll(states, group, 0)
    crossed = jnp.where(iota((2 * STATE, TILE), 0) % (2 * group) >= group, crossed, 0.0)
    sums = jnp.concatenate(
        [
            jnp.sum(act * act_grad_late, axis=0, keepdims=True),
            jnp.sum(crossed, axis=0, keepdims=True),
            jnp.sum(upstream * act, axis=0, keepdims=True),
            jnp.zeros((5, TILE), F32),
        ],
        axis=0,
    )
    first = sums.astype(BF16)
    second, third = halves(sums - first.astype(F32))
    by_head[...] += mm_nt(first, one_hot) + mm_nt(second, one_hot) + mm_nt(third, one_hot)

    act_grad = act_grad + gain * upstream
    conv_grad = act_grad * (gate + act * (1.0 - gate))
    full, taps_grad_ref[...] = conv_backward(conv_grad, shifted, taps_ref[...], valid)
    borrowed_ref[...] = full[:8]
    grad_ref[...] = full[8:].astype(BF16)
    end_ref[...] = full[ROWS - 8 :]

    @pl.when(tile == TILES - 1)
    def _():
        score_grad = score_grad_ref[...]
        keys, reads = bc_ref[:, :STATE], bc_ref[:, STATE:]
        reads_grad = exact(bc_grad[:ROWS], interleave(group, False)) + exact(score_grad, keys)
        keys_grad = exact(bc_grad[ROWS:], interleave(group, True)) + exact(score_grad.T, reads)
        total, shifted = convolve(tails_ref[...].astype(F32), xs_ref[...].astype(F32), tapss_ref[...], valid)
        gate = sigmoid(total)
        small_grad = jnp.concatenate([keys_grad, reads_grad], axis=1) * (gate + total * gate * (1.0 - gate))
        full, tapss_grad_ref[...] = conv_backward(small_grad, shifted, tapss_ref[...], valid)
        borroweds_ref[...] = full[:8]
        grads_ref[...] = full[8:].astype(BF16)
        ends_ref[...] = full[ROWS - 8 :]

        read_sum, added_sum = by_token[:ROWS], by_token[ROWS:]
        at_end = by_head[0:1, :] + own_ref[0:1, :] * by_head[1:2, :]
        run_grad = read_sum - added_sum + jnp.where(iota((ROWS, LANES), 0) == ROWS - 1, at_end, 0.0)
        alog_grad = jnp.sum(run_grad * run_ref[...], axis=0, keepdims=True)
        bias_grad = jnp.sum(added_sum / dt_ref[...] * sig_ref[...], axis=0, keepdims=True)
        rate = jnp.exp(small_ref[1:2, :])
        bias_grad = bias_grad - rate * jnp.sum(run_grad * sigsum_ref[...], axis=0, keepdims=True)
        heads_ref[...] = jnp.concatenate([bias_grad, alog_grad, by_head[2:3, :], jnp.zeros((5, LANES), F32)], axis=0)


def finish_stage(group, half, *operands):
    square = whole((ROWS, LANES))
    eight = whole((8, LANES))
    shapes = (
        jax.ShapeDtypeStruct((ROWS, INNER), BF16),
        jax.ShapeDtypeStruct((ROWS, INNER), BF16),
        jax.ShapeDtypeStruct((16, INNER), F32),
        jax.ShapeDtypeStruct((8, INNER), F32),
        jax.ShapeDtypeStruct((8, INNER), F32),
        jax.ShapeDtypeStruct((ROWS, 2 * STATE), BF16),
        jax.ShapeDtypeStruct((16, 2 * STATE), F32),
        jax.ShapeDtypeStruct((8, 2 * STATE), F32),
        jax.ShapeDtypeStruct((8, 2 * STATE), F32),
        jax.ShapeDtypeStruct((8, LANES), F32),
    )
    states = pl.BlockSpec(
        (None, STATE // group, 2 * group, TILE), lambda i, half: (i // HALF_TILES, 0, 0, lax.rem(i, HALF_TILES))
    )
    return call(
        functools.partial(finish_kernel, group), "finish", half, TILES,
        [
            tile_spec(ROWS), tile_spec(8), tile_spec(8),
            small_spec(ROWS), small_spec(8), small_spec(8),
            whole((ROWS, 8)), tile_spec(ROWS), whole((2 * ROWS, 2 * LANES)),
            tile_spec(ROWS), tile_spec(ROWS), states, states,
            whole((ROWS, 2 * STATE)), eight, eight, eight, whole((ROWS, ROWS)), square, square, square, square,
        ],
        [tile_spec(part.shape[0]) for part in shapes[:5]] + [whole(part.shape) for part in shapes[5:]],
        shapes,
        [
            pltpu.VMEM((2 * ROWS, 2 * STATE), BF16), pltpu.VMEM((2 * ROWS, 2 * STATE), BF16),
            pltpu.VMEM((2 * ROWS, 2 * STATE), F32), pltpu.VMEM((8, LANES), F32), pltpu.VMEM((2 * ROWS, LANES), F32),
        ],
        operands,
    )


def total_kernel(scale, taps_ref, small_ref, heads_ref, borrowed_ref, borroweds_ref, end_ref, ends_ref, keep_ref,
                 sums_ref, last_ref,
                 parts, slots, piece, far_slots, result, got, got_small, send, receive, far_send, far_receive, back_send,
                 back_receive, rows_send, rows_receive):
    shards, groups = lax.axis_size("seq"), lax.axis_size("dp")
    others = groups * shards // 8
    place, group = lax.axis_index("seq"), lax.axis_index("dp")
    before = (group, lax.rem(place + shards - 1, shards))
    after = (group, lax.rem(place + 1, shards))
    barrier = pltpu.get_barrier_semaphore()
    for peers, size in ((near, 8), (far, others)):
        for k in range(1, size):
            pl.semaphore_signal(barrier, inc=1, device_id=peers(k)[0], device_id_type=MESH)
    for peer in (before, after):
        pl.semaphore_signal(barrier, inc=1, device_id=peer, device_id_type=MESH)
    pl.semaphore_wait(barrier, 7 + others - 1 + 2)

    depth = parts.shape[1]
    wide = CH // LANES
    for at in range(8 * depth // 8):
        if at < INNER // LANES:
            block = taps_ref[:, LANES * at : LANES * (at + 1)]
        elif at < wide:
            block = small_ref[:, LANES * at - INNER : LANES * (at + 1) - INNER]
        elif at == wide:
            block = heads_ref[...]
        else:
            block = jnp.zeros((8, LANES), F32)
        parts[at % 8, 8 * (at // 8) : 8 * (at // 8) + 8, :] = block
    send_all(near, 8, lambda slot: parts.at[slot], slots, send, receive)
    returns = [
        pltpu.make_async_remote_copy(
            src_ref=source, dst_ref=target, send_sem=rows_send.at[at], recv_sem=rows_receive.at[at], device_id=before,
            device_id_type=MESH,
        )
        for at, (source, target) in enumerate(((borrowed_ref, got), (borroweds_ref, got_small)))
    ]

    @pl.when(place > 0)
    def _():
        for copy in returns:
            copy.start()

    _, own = near(0)
    _, far_own = far(0)
    slots[own] = parts[own]
    wait_all(near, 8, lambda slot: parts.at[slot], slots, send, receive)
    piece[...] = jnp.sum(slots[...], axis=0)
    send_all(far, others, lambda slot: piece, far_slots, far_send, far_receive)
    far_slots[far_own] = piece[...]
    wait_all(far, others, lambda slot: piece, far_slots, far_send, far_receive)
    piece[...] = jnp.sum(far_slots[...], axis=0) * scale
    send_all(near, 8, lambda slot: piece, result, back_send, back_receive)
    result[own] = piece[...]

    @pl.when(place > 0)
    def _():
        for copy in returns:
            copy.wait_send()

    @pl.when(place < shards - 1)
    def _():
        for copy in returns:
            copy.wait_recv()
        keep = keep_ref[:, 0:1]
        for lanes, source, end in ((slice(0, INNER), got, end_ref), (slice(INNER, CH), got_small, ends_ref)):
            late = iota(source.shape, 0) >= 8 - CONV + 1
            rows = jnp.concatenate([end[:8, :], end[8:, :] + jnp.where(late, source[...] * keep, 0.0)], axis=0)
            last_ref[:, lanes] = rows.astype(BF16)

    @pl.when(place == shards - 1)
    def _():
        last_ref[:, :INNER] = end_ref[...].astype(BF16)
        last_ref[:, INNER:] = ends_ref[...].astype(BF16)

    wait_all(near, 8, lambda slot: piece, result, back_send, back_receive)
    for at in range(wide + 1):
        sums_ref[:, LANES * at : LANES * (at + 1)] = result[at % 8, 8 * (at // 8) : 8 * (at // 8) + 8, :]


def layout_kernel(sums_ref, last_ref, grad_ref, grads_ref, weight_ref, bias_ref, dt_bias_ref, a_log_ref, gain_ref,
                  whole_ref):
    step = pl.program_id(0)

    @pl.when(step == 0)
    def _():
        weight_ref[...] = sums_ref[:CONV, :CH]
        bias_ref[...] = sums_ref[CONV : CONV + 1, :CH].reshape(CH)
        for at, target in enumerate((dt_bias_ref, a_log_ref, gain_ref)):
            target[...] = sums_ref[at : at + 1, CH : CH + HEADS].reshape(HEADS)

    @pl.when(step < pl.num_programs(0) - 1)
    def _():
        whole_ref[:, :INNER] = grad_ref[...]
        whole_ref[:, INNER:] = grads_ref[...]

    @pl.when(step == pl.num_programs(0) - 1)
    def _():
        whole_ref[: whole_ref.shape[0] - 16, :INNER] = grad_ref[: whole_ref.shape[0] - 16, :]
        whole_ref[: whole_ref.shape[0] - 16, INNER:] = grads_ref[: whole_ref.shape[0] - 16, :]
        whole_ref[whole_ref.shape[0] - 16 :, :] = last_ref[...]


def layout_stage(sums, last, grad, grads):
    rows = 32
    shapes = (
        jax.ShapeDtypeStruct((CONV, CH), F32),
        jax.ShapeDtypeStruct((CH,), F32),
        jax.ShapeDtypeStruct((HEADS,), F32),
        jax.ShapeDtypeStruct((HEADS,), F32),
        jax.ShapeDtypeStruct((HEADS,), F32),
        jax.ShapeDtypeStruct((ROWS, CH), BF16),
    )
    blocks = [pl.BlockSpec((rows, width), lambda i: (i, 0)) for width in (INNER, 2 * STATE, CH)]
    return pl.pallas_call(
        layout_kernel,
        grid=(ROWS // rows,),
        in_specs=[whole(sums.shape), whole(last.shape)] + blocks[:2],
        out_specs=[whole(part.shape) for part in shapes[:5]] + blocks[2:],
        out_shape=shapes,
        name="layout",
    )(sums, last, grad, grads)


def total_stage(others, scale, *operands):
    depth = 8 * pl.cdiv(CH // LANES + 1, 8)
    in_vmem = pl.BlockSpec(memory_space=pltpu.VMEM)
    shapes = (jax.ShapeDtypeStruct((8, CH + LANES), F32), jax.ShapeDtypeStruct((16, CH), BF16))
    dma = pltpu.SemaphoreType.DMA
    return pl.pallas_call(
        functools.partial(total_kernel, scale),
        in_specs=[in_vmem] * len(operands),
        out_specs=[in_vmem] * len(shapes),
        out_shape=shapes,
        scratch_shapes=[
            pltpu.VMEM((8, depth, LANES), F32), pltpu.VMEM((8, depth, LANES), F32),
            pltpu.VMEM((depth, LANES), F32), pltpu.VMEM((others, depth, LANES), F32),
            pltpu.VMEM((8, depth, LANES), F32),
            pltpu.VMEM((8, INNER), F32), pltpu.VMEM((8, 2 * STATE), F32),
            dma((8,)), dma((8,)), dma((others,)), dma((others,)), dma((8,)), dma((8,)), dma((2,)), dma((2,)),
        ],
        compiler_params=pltpu.CompilerParams(
            vmem_limit_bytes=VMEM_BYTES, collective_id=1, has_side_effects=True
        ),
        name="totals",
    )(*operands)


def on_device(conv_input, doc_start, conv_weight, conv_bias, dt_raw, dt_bias, a_log, skip_gain, cotangent):
    shards, place = lax.axis_size("seq"), lax.axis_index("seq")
    group = 2 * STATE // shards
    core = lax.rem(place, 2)
    half = jnp.stack([core, place // 2, core])
    run, runT, dt, dtT, both, sig, sigsum, mask, valid, keep, tail, own, small, taps = head_stage(
        dt_raw.T, jnp.stack([dt_bias, a_log, skip_gain]), doc_start[None], conv_weight, conv_bias[None], conv_input
    )
    tail = lax.ppermute(tail, "seq", [(i, i + 1) for i in range(shards - 1)])
    chips, others, out_in, grad_in, score_grad, bc, partner = carry_stage(
        group, conv_input, tail, taps, valid, cotangent, both, own, runT, dtT, mask
    )
    out, grad, end, borrowed, taps_grad, grads, ends, borroweds, tapss_grad, heads = finish_stage(
        group, half, conv_input, tail, taps, conv_input, tail, taps, valid, cotangent, both, out_in, grad_in, chips,
        others, bc, small, own, partner, score_grad, run, dt, sig, sigsum,
    )
    groups = lax.axis_size("dp")
    sums, last = total_stage(
        groups * shards // 8, float(groups * shards * ROWS) ** (-0.5), taps_grad, tapss_grad, heads, borrowed, borroweds,
        end, ends, keep,
    )
    weight_grad, bias_grad, dt_bias_grad, a_log_grad, gain_grad, whole_grad = layout_stage(sums, last, grad, grads)
    return (out, whole_grad, weight_grad, bias_grad, dt_bias_grad, a_log_grad, gain_grad)


def solution(mesh):
    sharded = P(("dp", "seq"), None)
    return jax.shard_map(
        on_device,
        mesh=mesh,
        in_specs=(sharded, P(("dp", "seq")), P(), P(), sharded, P(), P(), P(), sharded),
        out_specs=(sharded, sharded, P(), P(), P(), P(), P()),
        check_vma=False,
    )
```
